32 devices in a mesh: fsdp: 8 (over z, x), tp: 4 (over y, core).
Axes of the slice: x: 2, y: 2, z: 4, core: 2. Of those that a mesh axis runs over, the one named last changes fastest.
Arguments:
- tokens: bfloat16 [8192, 1024], P(('fsdp', 'tp')), may hold values from -6 to 6
- lengths: int32 [4], replicated, may hold values from 1 to 4096, 8192 in all
- attn_gain: bfloat16 [1024], P('fsdp'), may hold values from 0.5 to 1.5
- w_query: bfloat16 [1024, 1024], P('fsdp', 'tp'), may hold values from -0.1875 to 0.1875
- w_key: bfloat16 [1024, 1024], P('fsdp', 'tp'), may hold values from -0.1875 to 0.1875
- w_value: bfloat16 [1024, 2048], P('fsdp', 'tp'), may hold values from -0.1875 to 0.1875
- w_gate_out: bfloat16 [1024, 2048], P('fsdp', 'tp'), may hold values from -0.1875 to 0.1875
- w_beta: bfloat16 [1024, 8], P('fsdp', 'tp'), may hold values from -0.1875 to 0.1875
- w_decay: bfloat16 [1024, 8], P('fsdp', 'tp'), may hold values from -0.1875 to 0.1875
- conv_query: bfloat16 [4, 8, 128], P(None, 'tp', 'fsdp'), may hold values from -2.5 to 2.5
- conv_key: bfloat16 [4, 8, 128], P(None, 'tp', 'fsdp'), may hold values from -2.5 to 2.5
- conv_value: bfloat16 [4, 8, 256], P(None, 'tp', 'fsdp'), may hold values from -2.5 to 2.5
- decay_log: float32 [8], P('tp'), may hold values from -6 to -1
- decay_bias: float32 [8], P('tp'), may hold values from -1.5 to 0.5
- out_gain: bfloat16 [256], P('fsdp'), may hold values from 0.5 to 1.5
- w_out: bfloat16 [2048, 1024], P('tp', 'fsdp'), may hold values from -0.25 to 0.25
- ffn_gain: bfloat16 [1024], P('fsdp'), may hold values from 0.5 to 1.5
- w_ffn_gate: bfloat16 [1024, 2816], P('fsdp', 'tp'), may hold values from -0.1875 to 0.1875
- w_ffn_up: bfloat16 [1024, 2816], P('fsdp', 'tp'), may hold values from -0.1875 to 0.1875
- w_ffn_down: bfloat16 [2816, 1024], P('tp', 'fsdp'), may hold values from -0.21875 to 0.21875
- cotangent: bfloat16 [8192, 1024], P(('fsdp', 'tp')), may hold values from -6 to 6
Outputs:
- output: float32 [8192, 1024], P(('fsdp', 'tp'))
- d_tokens: float32 [8192, 1024], P(('fsdp', 'tp'))
- grad_attn_gain: float32 [1024], P('fsdp')
- grad_w_query: float32 [1024, 1024], P('fsdp', 'tp')
- grad_w_key: float32 [1024, 1024], P('fsdp', 'tp')
- grad_w_value: float32 [1024, 2048], P('fsdp', 'tp')
- grad_w_gate_out: float32 [1024, 2048], P('fsdp', 'tp')
- grad_w_beta: float32 [1024, 8], P('fsdp', 'tp')
- grad_w_decay: float32 [1024, 8], P('fsdp', 'tp')
- grad_conv_query: float32 [4, 8, 128], P(None, 'tp', 'fsdp')
- grad_conv_key: float32 [4, 8, 128], P(None, 'tp', 'fsdp')
- grad_conv_value: float32 [4, 8, 256], P(None, 'tp', 'fsdp')
- grad_decay_log: float32 [8], P('tp')
- grad_decay_bias: float32 [8], P('tp')
- grad_out_gain: float32 [256], P('fsdp')
- grad_w_out: float32 [2048, 1024], P('tp', 'fsdp')
- grad_ffn_gain: float32 [1024], P('fsdp')
- grad_w_ffn_gate: float32 [1024, 2816], P('fsdp', 'tp')
- grad_w_ffn_up: float32 [1024, 2816], P('fsdp', 'tp')
- grad_w_ffn_down: float32 [2816, 1024], P('tp', 'fsdp')
The draws below stay inside these ranges and needn't reach their ends.
Inputs may be any that keep to these rules, and one draw needn't show every extreme that they name: The 4 lengths sum to 8192; the largest is exactly 4096.
All inputs are finite; a program needn't handle non-finite values.
Results may differ from the reference program's by a relative error of at most 0.03.
Values may be sent and summed in bfloat16 or wider, within the bound.
A program may use at most 256 MiB of HBM per device.

```python
import math
import jax
import jax.numpy as jnp
import numpy as np
from jax import lax

D = 1024
H = 8
K = 128
V = 256
FF = 2816
CONV = 4
GROUP = 64
MAXLEN = 4096
TOKENS = 8192
NSEQ = 4


def shard_levels(rng, shape, cuts, low, high):
    gain = 1.0
    for position, parts in cuts:
        heights = jax.random.uniform(jax.random.fold_in(jax.random.fold_in(rng, 6), position), (parts,), jnp.float32, low / len(cuts), high / len(cuts))
        gain = gain * jnp.repeat(jnp.exp(heights), shape[position] // parts).reshape((-1,) + (1,) * (len(shape) - 1 - position))
    return gain


def split_up(count, total, bound, slope):
    portions = [(1 << 20) // math.isqrt(rank ** slope) + 1 for rank in range(2, count + 1)]
    surplus, counts = total - bound - (count - 1), [1] * (count - 1)
    while surplus > 0:
        movable = [i for i in range(count - 1) if counts[i] < bound]
        pool, left = sum([portions[i] for i in movable]), surplus
        for i in movable:
            addition = min(bound - counts[i], max(1, left * portions[i] // pool), surplus)
            counts[i] = counts[i] + addition
            surplus = surplus - addition
    return np.array([bound] + counts)


def ragged_sizes(stream_key, amount, total, limit, slope):
    if amount == 2:
        one = jax.random.randint(stream_key, (), max(1, total - limit), min(limit, total - 1) + 1)
        return jnp.stack([one, total - one])
    tallies = jnp.asarray(split_up(amount, total, limit, slope), jnp.int32)
    pairs = (amount - 1) // 2
    donor, receiver = tallies[1:1 + 2 * pairs:2], tallies[2:2 + 2 * pairs:2]
    margin = jnp.minimum(donor - 1, limit - receiver)
    moved = jax.random.randint(jax.random.fold_in(stream_key, 1), (pairs,), 0, 1 << 20) % (margin + 1)
    tallies = tallies.at[1:1 + 2 * pairs:2].set(donor - moved).at[2:2 + 2 * pairs:2].set(receiver + moved)
    return tallies[jax.random.permutation(jax.random.fold_in(stream_key, 2), amount)]


def scatter_about(rng, shape, scale, limit, cuts=(), kind=jnp.bfloat16):
    gain = shard_levels(rng, shape, cuts, -0.22, 0.18) if cuts else 1.0
    array = jax.random.normal(rng, shape, jnp.float32) * scale * gain
    return jnp.minimum(jnp.maximum(array, -limit), limit).astype(kind)


def setup_inputs(seed: int = 0) -> dict:
    arg_keys = jax.random.split(jax.random.key(seed), 22)
    tokens = scatter_about(arg_keys[0], (TOKENS, D), 1.0, 6.0, ((0, 32),))
    lengths = ragged_sizes(arg_keys[1], NSEQ, TOKENS, MAXLEN, 2).astype(jnp.int32)
    attn_gain = jnp.clip(1.0 + 0.1 * jax.random.normal(arg_keys[2], (D,), jnp.float32), 0.5, 1.5).astype(jnp.bfloat16)
    w_query = scatter_about(arg_keys[3], (D, H * K), D ** -0.5, 0.1875, ((0, 8), (1, 4)))
    w_key = scatter_about(arg_keys[4], (D, H * K), D ** -0.5, 0.1875, ((0, 8), (1, 4)))
    w_value = scatter_about(arg_keys[5], (D, H * V), D ** -0.5, 0.1875, ((0, 8), (1, 4)))
    w_gate_out = scatter_about(arg_keys[6], (D, H * V), D ** -0.5, 0.1875, ((0, 8), (1, 4)))
    w_beta = scatter_about(arg_keys[7], (D, H), D ** -0.5, 0.1875, ((0, 8), (1, 4)))
    w_decay = scatter_about(arg_keys[8], (D, H), D ** -0.5, 0.1875, ((0, 8), (1, 4)))
    conv_query = scatter_about(arg_keys[9], (CONV, H, K), 0.5, 2.5, ((1, 4), (2, 8)))
    conv_key = scatter_about(arg_keys[10], (CONV, H, K), 0.5, 2.5, ((1, 4), (2, 8)))
    conv_value = scatter_about(arg_keys[11], (CONV, H, V), 0.5, 2.5, ((1, 4), (2, 8)))
    decay_log = jnp.clip(-6.0 + 5.0 * jax.random.uniform(arg_keys[12], (H,), jnp.float32) ** shard_levels(arg_keys[12], (H,), ((0, 4),), -0.2, 0.2), -6.0, -1.0)
    decay_bias = jnp.clip(-1.5 + 2.0 * jax.random.uniform(arg_keys[13], (H,), jnp.float32) ** shard_levels(arg_keys[13], (H,), ((0, 4),), -0.2, 0.2), -1.5, 0.5)
    out_gain = jnp.clip(1.0 + 0.1 * jax.random.normal(arg_keys[14], (V,), jnp.float32), 0.5, 1.5).astype(jnp.bfloat16)
    w_out = scatter_about(arg_keys[15], (H * V, D), (H * V // 4) ** -0.5, 0.25, ((0, 4), (1, 8)))
    ffn_gain = jnp.clip(1.0 + 0.1 * jax.random.normal(arg_keys[16], (D,), jnp.float32), 0.5, 1.5).astype(jnp.bfloat16)
    w_ffn_gate = scatter_about(arg_keys[17], (D, FF), D ** -0.5, 0.1875, ((0, 8), (1, 4)))
    w_ffn_up = scatter_about(arg_keys[18], (D, FF), D ** -0.5, 0.1875, ((0, 8), (1, 4)))
    w_ffn_down = scatter_about(arg_keys[19], (FF, D), (FF // 4) ** -0.5, 0.21875, ((0, 4), (1, 8)))
    cotangent = scatter_about(arg_keys[20], (TOKENS, D), 1.0, 6.0, ((0, 32),))
    return {"tokens": tokens, "lengths": lengths, "attn_gain": attn_gain, "w_query": w_query, "w_key": w_key, "w_value": w_value, "w_gate_out": w_gate_out, "w_beta": w_beta, "w_decay": w_decay, "conv_query": conv_query, "conv_key": conv_key, "conv_value": conv_value, "decay_log": decay_log, "decay_bias": decay_bias, "out_gain": out_gain, "w_out": w_out, "ffn_gain": ffn_gain, "w_ffn_gate": w_ffn_gate, "w_ffn_up": w_ffn_up, "w_ffn_down": w_ffn_down, "cotangent": cotangent}


highest = lax.Precision.HIGHEST

def mat_dot(left, right):
    return jnp.dot(left.astype(jnp.float32), right.astype(jnp.float32), preferred_element_type=jnp.float32)

def rms_scale(values, scale_gain):
    return values * lax.rsqrt(lax.optimization_barrier(jnp.mean(values * values, axis=-1, keepdims=True)) + 1e-06) * scale_gain

def unit_rows(values):
    return values * lax.rsqrt(lax.optimization_barrier(jnp.sum(values * values, axis=-1, keepdims=True)) + 1e-06)

def seq_begin(lengths, positions):
    offsets = (jnp.cumsum(lengths) - lengths).astype(jnp.int32)
    chosen = jnp.where(offsets[None, :] <= positions[:, None], offsets[None, :], 0)
    return lax.optimization_barrier(jnp.max(chosen, axis=1)).astype(jnp.int32)

def split_heads(flat, width):
    return flat.reshape(flat.shape[0], -1, width).transpose(1, 0, 2)

def merge_heads(stacked):
    return stacked.transpose(1, 0, 2).reshape(stacked.shape[1], -1)

def short_conv(inputs, rim_rows, kernel, begins, positions):
    row_count = inputs.shape[0]
    padded = jnp.concatenate([rim_rows, inputs], axis=0)
    result = kernel[0] * inputs
    for lag_step in range(1, CONV):
        in_range = (positions - lag_step >= begins).astype(inputs.dtype)[:, None]
        start_row = CONV - 1 - lag_step
        result = result + kernel[lag_step] * padded[start_row:start_row + row_count] * in_range
    return jax.nn.silu(result)

def head_inputs(query_raw, key_raw, value_raw, query_rim, key_rim, value_rim, query_kernel, key_kernel, value_kernel, beta_raw, decay_raw, decay_scale, decay_shift, begins, positions):
    query_vec = unit_rows(short_conv(query_raw, query_rim, query_kernel, begins, positions)) * query_raw.shape[1] ** (-0.5)
    key_vec = unit_rows(short_conv(key_raw, key_rim, key_kernel, begins, positions))
    value_vec = short_conv(value_raw, value_rim, value_kernel, begins, positions)
    beta_gate = jax.nn.sigmoid(beta_raw)
    decay_rate = -jnp.exp(decay_scale) * jax.nn.softplus(decay_raw + decay_shift)
    return (query_vec, key_vec, value_vec, beta_gate, decay_rate)

def block_terms(query_vec, key_vec, value_vec, beta_gate, decay_rate, begins, positions):
    blocks = query_vec.shape[0] // GROUP
    query_block = query_vec.reshape(blocks, GROUP, -1)
    key_block = key_vec.reshape(blocks, GROUP, -1)
    value_block = value_vec.reshape(blocks, GROUP, -1)
    beta_block = beta_gate.reshape(blocks, GROUP)
    decay_block = decay_rate.reshape(blocks, GROUP)
    begin_block = begins.reshape(blocks, GROUP)
    place_block = positions.reshape(blocks, GROUP)
    cumul = jnp.cumsum(decay_block, axis=1)
    same_seq = (begin_block[:, :, None] <= place_block[:, None, :]) & (place_block[:, None, :] <= place_block[:, :, None])
    same_float = same_seq.astype(query_vec.dtype)
    factor = jnp.exp(jnp.where(same_seq, cumul[:, :, None] - cumul[:, None, :], 0.0)) * same_float
    alive_mask = (begin_block < place_block[:, :1]).astype(query_vec.dtype)
    carry_scale = jnp.exp(cumul) * alive_mask
    strict = (place_block[:, None, :] < place_block[:, :, None]).astype(query_vec.dtype)
    key_gram = jnp.einsum('ntd,nsd->nts', key_block, key_block, precision=highest)
    lower_mat = jnp.eye(GROUP, dtype=query_vec.dtype)[None] + beta_block[:, :, None] * key_gram * factor * strict
    value_part = lax.linalg.triangular_solve(lower_mat, beta_block[:, :, None] * value_block, left_side=True, lower=True, unit_diagonal=True)
    key_part = lax.linalg.triangular_solve(lower_mat, (beta_block * carry_scale)[:, :, None] * key_block, left_side=True, lower=True, unit_diagonal=True)
    scores = jnp.einsum('ntd,nsd->nts', query_block, key_block, precision=highest) * factor
    key_last = key_block * factor[:, -1, :, None]
    return (query_block, carry_scale, scores, value_part, key_part, key_last)

def mixer_head(query_raw, key_raw, value_raw, query_kernel, key_kernel, value_kernel, beta_raw, decay_raw, decay_scale, decay_shift, gate_raw, out_scale, begins, positions):
    query_rim = jnp.zeros((CONV - 1, query_raw.shape[1]), query_raw.dtype)
    key_rim = jnp.zeros((CONV - 1, key_raw.shape[1]), key_raw.dtype)
    value_rim = jnp.zeros((CONV - 1, value_raw.shape[1]), value_raw.dtype)
    inputs = head_inputs(query_raw, key_raw, value_raw, query_rim, key_rim, value_rim, query_kernel, key_kernel, value_kernel, beta_raw, decay_raw, decay_scale, decay_shift, begins, positions)
    block_parts = block_terms(*inputs, begins, positions)

    def advance(state_now, pieces):
        query_block, scale_block, score_block, value_block, key_block, last_block = pieces
        update = value_block - jnp.dot(key_block, state_now, precision=highest)
        result = scale_block[:, None] * jnp.dot(query_block, state_now, precision=highest) + jnp.dot(score_block, update, precision=highest)
        state_now = scale_block[-1] * state_now + jnp.dot(last_block.T, update, precision=highest)
        return (state_now, result)
    start_state = jnp.zeros((key_raw.shape[1], value_raw.shape[1]), query_raw.dtype)
    _, results = lax.scan(advance, start_state, block_parts)
    outputs = results.reshape(-1, value_raw.shape[1])
    return rms_scale(outputs, out_scale) * jax.nn.silu(gate_raw)

def reference(tokens, lengths, attn_gain, w_query, w_key, w_value, w_gate_out, w_beta, w_decay, conv_query, conv_key, conv_value, decay_log, decay_bias, out_gain, w_out, ffn_gain, w_ffn_gate, w_ffn_up, w_ffn_down, cotangent):
    row_count = tokens.shape[0]
    positions = jnp.arange(row_count, dtype=jnp.int32)
    begins = seq_begin(lengths, positions)
    rows_float = tokens.astype(jnp.float32)
    normed_attn, pull_attn = jax.vjp(rms_scale, rows_float, attn_gain.astype(jnp.float32))
    normed_attn = normed_attn.astype(jnp.bfloat16)
    proj_query = mat_dot(normed_attn, w_query).astype(jnp.bfloat16)
    proj_key = mat_dot(normed_attn, w_key).astype(jnp.bfloat16)
    proj_value = mat_dot(normed_attn, w_value).astype(jnp.bfloat16)
    gate_raw = mat_dot(normed_attn, w_gate_out)
    beta_raw = mat_dot(normed_attn, w_beta)
    decay_raw = mat_dot(normed_attn, w_decay)
    out_scale = out_gain.astype(jnp.float32)
    head_items = (split_heads(proj_query.astype(jnp.float32), K), split_heads(proj_key.astype(jnp.float32), K), split_heads(proj_value.astype(jnp.float32), V), jnp.transpose(conv_query.astype(jnp.float32), (1, 0, 2)), jnp.transpose(conv_key.astype(jnp.float32), (1, 0, 2)), jnp.transpose(conv_value.astype(jnp.float32), (1, 0, 2)), beta_raw.T, decay_raw.T, decay_log, decay_bias, split_heads(gate_raw, V))

    def head_forward(items):
        return mixer_head(*items, out_scale, begins, positions)
    mixer_out = lax.map(head_forward, head_items)
    normed_mixer = merge_heads(mixer_out).astype(jnp.bfloat16)
    hidden = rows_float + mat_dot(normed_mixer, w_out)
    normed_ffn, pull_ffn = jax.vjp(rms_scale, hidden, ffn_gain.astype(jnp.float32))
    normed_ffn = normed_ffn.astype(jnp.bfloat16)
    gate_pre = mat_dot(normed_ffn, w_ffn_gate)
    up_pre = mat_dot(normed_ffn, w_ffn_up)
    gate_sigmoid = jax.nn.sigmoid(gate_pre)
    activated = (gate_pre * gate_sigmoid * up_pre).astype(jnp.bfloat16)
    output = hidden + mat_dot(activated, w_ffn_down)
    d_active = mat_dot(cotangent, w_ffn_down.T)
    grad_w_ffn_down = mat_dot(activated.T, cotangent)
    d_gate = (d_active * up_pre * gate_sigmoid * (1.0 + gate_pre * (1.0 - gate_sigmoid))).astype(jnp.bfloat16)
    d_upper = (d_active * gate_pre * gate_sigmoid).astype(jnp.bfloat16)
    grad_w_ffn_gate = mat_dot(normed_ffn.T, d_gate)
    grad_w_ffn_up = mat_dot(normed_ffn.T, d_upper)
    d_normed_ffn = mat_dot(d_gate, w_ffn_gate.T) + mat_dot(d_upper, w_ffn_up.T)
    d_hidden_norm, grad_ffn_gain = pull_ffn(d_normed_ffn)
    d_hidden = cotangent.astype(jnp.float32) + d_hidden_norm
    d_hidden_half = d_hidden.astype(jnp.bfloat16)
    d_mixer = mat_dot(d_hidden_half, w_out.T)
    grad_w_out = mat_dot(normed_mixer.T, d_hidden_half)

    def head_backward(items):
        primal = items[:11]

        def local_head(*head_args):
            return mixer_head(*head_args, begins, positions)
        _, pull_head = jax.vjp(local_head, *primal, out_scale)
        return pull_head(items[11])
    head_grads = lax.map(head_backward, head_items + (split_heads(d_mixer, V),))
    d_query_half = merge_heads(head_grads[0]).astype(jnp.bfloat16)
    d_key_half = merge_heads(head_grads[1]).astype(jnp.bfloat16)
    d_value_half = merge_heads(head_grads[2]).astype(jnp.bfloat16)
    d_gate_half = merge_heads(head_grads[10]).astype(jnp.bfloat16)
    d_beta_half = head_grads[6].T.astype(jnp.bfloat16)
    d_decay_half = head_grads[7].T.astype(jnp.bfloat16)
    grad_conv_query = jnp.transpose(head_grads[3], (1, 0, 2))
    grad_conv_key = jnp.transpose(head_grads[4], (1, 0, 2))
    grad_conv_value = jnp.transpose(head_grads[5], (1, 0, 2))
    grad_decay_log = head_grads[8]
    grad_decay_bias = head_grads[9]
    grad_out_gain = lax.optimization_barrier(jnp.sum(head_grads[11], axis=0))
    grad_w_query = mat_dot(normed_attn.T, d_query_half)
    grad_w_key = mat_dot(normed_attn.T, d_key_half)
    grad_w_value = mat_dot(normed_attn.T, d_value_half)
    grad_w_gate_out = mat_dot(normed_attn.T, d_gate_half)
    grad_w_beta = mat_dot(normed_attn.T, d_beta_half)
    grad_w_decay = mat_dot(normed_attn.T, d_decay_half)
    d_normed_attn = mat_dot(d_query_half, w_query.T) + mat_dot(d_key_half, w_key.T) + mat_dot(d_value_half, w_value.T) + mat_dot(d_gate_half, w_gate_out.T) + mat_dot(d_beta_half, w_beta.T) + mat_dot(d_decay_half, w_decay.T)
    d_rows_norm, grad_attn_gain = pull_attn(d_normed_attn)
    d_tokens = d_hidden + d_rows_norm
    return (output, d_tokens, grad_attn_gain, grad_w_query, grad_w_key, grad_w_value, grad_w_gate_out, grad_w_beta, grad_w_decay, grad_conv_query, grad_conv_key, grad_conv_value, grad_decay_log, grad_decay_bias, grad_out_gain, grad_w_out, grad_ffn_gain, grad_w_ffn_gate, grad_w_ffn_up, grad_w_ffn_down)
```

```python
import functools

import jax
import jax.numpy as jnp
from jax import lax
from jax.experimental import pallas as pl
from jax.experimental.pallas import tpu as pltpu
from jax.sharding import PartitionSpec as P

K = 128
V = 256
CONV = 4
GROUP = 128
MAXLEN = 4096


highest = lax.Precision.HIGHEST
high = lax.Precision.HIGH


def shifted(array, axis, by):
    count = lax.axis_size(axis)
    pairs = [(i, i + by) for i in range(count) if 0 <= i + by < count]
    return lax.ppermute(array, axis, pairs)


def mat_dot(left, right):
    return jnp.dot(left, right, preferred_element_type=jnp.float32)


def rms_scale(values, scale_gain):
    return (
        values * lax.rsqrt(jnp.mean(values * values, axis=-1, keepdims=True) + 1e-06) * scale_gain
    )


def unit_rows(values):
    return values * lax.rsqrt(jnp.sum(values * values, axis=-1, keepdims=True) + 1e-06)


def seq_begin(lengths, positions):
    number = lengths.shape[0]
    earlier = jnp.arange(number)[None, :] < jnp.arange(number)[:, None]
    offsets = jnp.sum(jnp.where(earlier, lengths[None, :], 0), axis=1)
    chosen = jnp.where(offsets[None, :] <= positions[:, None], offsets[None, :], 0)
    return jnp.max(chosen, axis=1)


def split_heads(flat, width):
    return flat.reshape(flat.shape[0], -1, width).transpose(1, 0, 2)


def merge_heads(stacked):
    return stacked.transpose(1, 0, 2).reshape(stacked.shape[1], -1)


def short_conv(inputs, rim_rows, kernel, begins, positions):
    row_count = inputs.shape[0]
    padded = jnp.concatenate([rim_rows, inputs], axis=0)
    result = kernel[0] * inputs
    for lag_step in range(1, CONV):
        in_range = (positions - lag_step >= begins).astype(inputs.dtype)[:, None]
        start_row = CONV - 1 - lag_step
        result = result + kernel[lag_step] * padded[start_row : start_row + row_count] * in_range
    return jax.nn.silu(result)


def head_inputs(
    query_raw,
    key_raw,
    value_raw,
    query_rim,
    key_rim,
    value_rim,
    query_kernel,
    key_kernel,
    value_kernel,
    beta_raw,
    decay_raw,
    decay_scale,
    decay_shift,
    begins,
    positions,
):
    query_vec = unit_rows(
        short_conv(query_raw, query_rim, query_kernel, begins, positions)
    ) * query_raw.shape[1] ** (-0.5)
    key_vec = unit_rows(short_conv(key_raw, key_rim, key_kernel, begins, positions))
    value_vec = short_conv(value_raw, value_rim, value_kernel, begins, positions)
    beta_gate = jax.nn.sigmoid(beta_raw)
    decay_rate = -jnp.exp(decay_scale) * jax.nn.softplus(decay_raw + decay_shift)
    return (query_vec, key_vec, value_vec, beta_gate, decay_rate)


def level_mask(size, step):
    row = lax.broadcasted_iota(jnp.int32, (size, size), 0) // step
    col = lax.broadcasted_iota(jnp.int32, (size, size), 1) // step
    return ((row // 2 == col // 2) & (row > col)).astype(jnp.float32)


@jax.custom_vjp
def unit_lower_inverse(strict_lower):
    size = strict_lower.shape[-1]
    inverse = jnp.eye(size, dtype=strict_lower.dtype) - strict_lower * level_mask(size, 1)
    step = 2
    while step < size:
        corner = strict_lower * level_mask(size, step)
        inverse = inverse - jnp.matmul(
            jnp.matmul(inverse, corner, precision=high), inverse, precision=high
        )
        step = step * 2
    return inverse


def unit_lower_inverse_fwd(strict_lower):
    inverse = unit_lower_inverse(strict_lower)
    return inverse, inverse


def unit_lower_inverse_bwd(inverse, grad):
    flipped = jnp.swapaxes(inverse, -1, -2)
    return (-jnp.matmul(jnp.matmul(flipped, grad, precision=high), flipped, precision=high),)


unit_lower_inverse.defvjp(unit_lower_inverse_fwd, unit_lower_inverse_bwd)


def block_terms(query_vec, key_vec, value_vec, beta_gate, decay_rate, begins, positions):
    blocks = query_vec.shape[0] // GROUP
    query_block = query_vec.reshape(blocks, GROUP, -1)
    key_block = key_vec.reshape(blocks, GROUP, -1)
    value_block = value_vec.reshape(blocks, GROUP, -1)
    beta_block = beta_gate.reshape(blocks, GROUP)
    decay_block = decay_rate.reshape(blocks, GROUP)
    begin_block = begins.reshape(blocks, GROUP)
    place_block = positions.reshape(blocks, GROUP)
    upper = jnp.triu(jnp.ones((GROUP, GROUP), decay_block.dtype))
    cumul = jnp.dot(decay_block, upper, precision=highest)
    same_seq = (begin_block[:, :, None] <= place_block[:, None, :]) & (
        place_block[:, None, :] <= place_block[:, :, None]
    )
    same_float = same_seq.astype(query_vec.dtype)
    factor = jnp.exp(jnp.where(same_seq, cumul[:, :, None] - cumul[:, None, :], 0.0)) * same_float
    alive_mask = (begin_block < place_block[:, :1]).astype(query_vec.dtype)
    carry_scale = jnp.exp(cumul) * alive_mask
    strict = (place_block[:, None, :] < place_block[:, :, None]).astype(query_vec.dtype)
    key_gram = jnp.einsum("ntd,nsd->nts", key_block, key_block, precision=high)
    inverse = unit_lower_inverse(beta_block[:, :, None] * key_gram * factor * strict)
    value_part = jnp.matmul(inverse, beta_block[:, :, None] * value_block)
    key_part = jnp.matmul(inverse, (beta_block * carry_scale)[:, :, None] * key_block)
    scores = jnp.einsum("ntd,nsd->nts", query_block, key_block) * factor
    key_last = key_block * factor[:, -1, :, None]
    return (query_block, carry_scale, scores, value_part, key_part, key_last)


def state_maps(block_parts):
    _, carry_scale, _, value_part, key_part, key_last = block_parts
    maps = jnp.einsum("hncj,hnck->hnjk", key_last, key_part)
    offsets = jnp.einsum("hncj,hncv->hnjv", key_last, value_part)
    return carry_scale[:, :, -1][:, :, None, None], maps, offsets


def state_run(scales, maps, offsets):
    heads, blocks = maps.shape[:2]
    matrix = jnp.broadcast_to(jnp.eye(K, dtype=jnp.float32), (heads, K, K))
    pair = jnp.concatenate([matrix, jnp.zeros_like(offsets[:, 0])], axis=-1)
    drive = jnp.concatenate([jnp.zeros_like(maps), offsets], axis=-1)
    starts = []
    for block in range(blocks):
        starts.append(pair)
        pair = (
            scales[:, block] * pair
            + drive[:, block]
            - jnp.einsum("hij,hjv->hiv", maps[:, block], pair, precision=high)
        )
    return jnp.stack(starts, axis=1), pair


def adjoint_run(scales, maps, local_grads, last):
    blocks = maps.shape[1]
    after = [None] * blocks
    grad = last
    for block in reversed(range(blocks)):
        after[block] = grad
        grad = (
            scales[:, block] * grad
            + local_grads[:, block]
            - jnp.einsum("hji,hjv->hiv", maps[:, block], grad, precision=high)
        )
    return jnp.stack(after, axis=1), grad


def entering(pairs, axis, row_count):
    count, mine = (lax.axis_size(axis), lax.axis_index(axis))
    hops = min(count - 1, -(-MAXLEN // row_count))
    state = jnp.zeros_like(pairs[0][..., K:])
    for hop in range(hops, 0, -1):
        piece = lax.dynamic_index_in_dim(pairs, jnp.maximum(mine - hop, 0), 0, False)
        new = (
            jnp.einsum("hij,hjv->hiv", piece[..., :K], state, precision=high) + piece[..., K:]
        )
        state = jnp.where(mine >= hop, new, state)
    return state


def carried_in(pairs, grads, axis, row_count):
    count, mine = (lax.axis_size(axis), lax.axis_index(axis))
    hops = min(count - 1, -(-MAXLEN // row_count))
    grad = jnp.zeros(grads.shape[1:], jnp.float32)
    for hop in range(hops, 0, -1):
        source = jnp.minimum(mine + hop, count - 1)
        piece = lax.dynamic_index_in_dim(pairs, source, 0, False)
        own = lax.dynamic_index_in_dim(grads, source, 0, False).astype(jnp.float32)
        new = jnp.einsum("hji,hjv->hiv", piece[..., :K], grad, precision=high) + own
        grad = jnp.where(mine + hop < count, new, grad)
    return grad


def step_states(block_parts, start_states):
    _, carry_scale, _, value_part, key_part, key_last = block_parts
    update = value_part - jnp.einsum("hncj,hnjv->hncv", key_part, start_states)
    return carry_scale[:, :, -1][:, :, None, None] * start_states + jnp.einsum(
        "hncj,hncv->hnjv", key_last, update
    )


def front_all(
    mixed_raw,
    rim_raw,
    query_kernel,
    key_kernel,
    value_kernel,
    beta_raw,
    decay_raw,
    decay_scale,
    decay_shift,
    begins,
    positions,
    head_count,
):
    query_width = head_count * K

    def front_one_head(
        query_raw,
        key_raw,
        value_raw,
        query_rim,
        key_rim,
        value_rim,
        query_taps,
        key_taps,
        value_taps,
        beta_head,
        decay_head,
        scale_head,
        shift_head,
    ):
        inputs = head_inputs(
            query_raw,
            key_raw,
            value_raw,
            query_rim,
            key_rim,
            value_rim,
            query_taps,
            key_taps,
            value_taps,
            beta_head,
            decay_head,
            scale_head,
            shift_head,
            begins,
            positions,
        )
        return block_terms(*inputs, begins, positions)

    return jax.vmap(front_one_head)(
        split_heads(mixed_raw[:, :query_width], K),
        split_heads(mixed_raw[:, query_width : 2 * query_width], K),
        split_heads(mixed_raw[:, 2 * query_width :], V),
        split_heads(rim_raw[:, :query_width], K),
        split_heads(rim_raw[:, query_width : 2 * query_width], K),
        split_heads(rim_raw[:, 2 * query_width :], V),
        jnp.transpose(query_kernel, (1, 0, 2)),
        jnp.transpose(key_kernel, (1, 0, 2)),
        jnp.transpose(value_kernel, (1, 0, 2)),
        beta_raw.T,
        decay_raw.T,
        decay_scale,
        decay_shift,
    )


def back_all(block_parts, start_states, gate_heads, out_scale):
    query_block, carry_scale, scores, value_part, key_part, _ = block_parts
    update = value_part - jnp.einsum("hncj,hnjv->hncv", key_part, start_states)
    outputs = carry_scale[..., None] * jnp.einsum("hncj,hnjv->hncv", query_block, start_states)
    outputs = outputs + jnp.einsum("hnts,hnsv->hntv", scores, update)
    outputs = outputs.reshape(outputs.shape[0], -1, outputs.shape[-1])
    return rms_scale(outputs, out_scale) * jax.nn.silu(gate_heads)


MESH = pl.DeviceIdType.MESH
INNER = 2


def on_axis(axis, index):
    return {axis: index}


def halves(axis):
    me = lax.axis_index(axis)
    return me, lax.div(me, INNER), lax.rem(me, INNER)


def entry_barrier(axes, everyone=False):
    barrier = pltpu.get_barrier_semaphore()
    total = 0
    for axis, count in axes:
        me, outer, inner = halves(axis)
        outers = count // INNER
        peers = [outer * INNER + (1 - inner)]
        for d in range(1, outers):
            peers.append(lax.rem(outer + d, outers) * INNER + inner)
        if everyone:
            peers = [lax.rem(me + d, count) for d in range(1, count)]
        for peer in peers:
            pl.semaphore_signal(
                barrier, inc=1, device_id=on_axis(axis, peer), device_id_type=MESH
            )
        total += len(peers)
    pl.semaphore_wait(barrier, total)


class Gather:
    def __init__(self, axis, count, buf, send, recv, own=None):
        self.axis, self.count, self.buf, self.send, self.recv = axis, count, buf, send, recv
        self.outers = count // INNER
        self.me, self.outer, self.inner = halves(axis)
        self.own = buf.at[self.me] if own is None else own
        self.copies = []

    def block(self, d, across):
        outer = lax.rem(self.outer + self.outers - d, self.outers)
        return outer * INNER + ((1 - self.inner) if across else self.inner)

    def push(self, src, index, target):
        copy = pltpu.make_async_remote_copy(
            src_ref=src,
            dst_ref=self.buf.at[index],
            send_sem=self.send.at[len(self.copies)],
            recv_sem=self.recv.at[index],
            device_id=on_axis(self.axis, target),
            device_id_type=MESH,
        )
        copy.start()
        self.copies.append(copy)

    def start(self):
        for d in range(1, self.outers):
            self.push(
                self.own, self.me, lax.rem(self.outer + d, self.outers) * INNER + self.inner
            )
        self.push(self.own, self.me, self.outer * INNER + 1 - self.inner)

    def arrive(self, index):
        pltpu.make_async_remote_copy(
            src_ref=self.buf.at[index],
            dst_ref=self.buf.at[index],
            send_sem=self.send.at[0],
            recv_sem=self.recv.at[index],
            device_id=on_axis(self.axis, self.outer * INNER + 1 - self.inner),
            device_id_type=MESH,
        ).wait_recv()

    def forward(self, d):
        index = self.block(d, False)
        self.arrive(index)
        self.push(self.buf.at[index], index, self.outer * INNER + 1 - self.inner)
        return index

    def finish(self):
        for copy in self.copies:
            copy.wait_send()


class Scatter:
    def __init__(self, axis, count, out, stage, send2, stage2, sems, full=None):
        self.axis, self.count, self.full = axis, count, full
        self.outers = count // INNER
        self.me, self.outer, self.inner = halves(axis)
        self.out, self.stage, self.send2, self.stage2 = out, stage, send2, stage2
        self.send_a, self.recv_a, self.send_b, self.recv_b = sems
        self.copies = []

    def target(self, d, across):
        outer = lax.rem(self.outer + d, self.outers)
        return outer * INNER + ((1 - self.inner) if across else self.inner)

    def first(self, d):
        return pltpu.make_async_remote_copy(
            src_ref=self.out.at[d] if self.full is None else self.full.at[self.target(d, True)],
            dst_ref=self.stage.at[d],
            send_sem=self.send_a.at[d],
            recv_sem=self.recv_a.at[d],
            device_id=on_axis(self.axis, self.outer * INNER + 1 - self.inner),
            device_id_type=MESH,
        )

    def second(self, d):
        return pltpu.make_async_remote_copy(
            src_ref=self.send2.at[d - 1],
            dst_ref=self.stage2.at[d - 1],
            send_sem=self.send_b.at[d - 1],
            recv_sem=self.recv_b.at[d - 1],
            device_id=on_axis(self.axis, self.target(d, False)),
            device_id_type=MESH,
        )

    def send_across(self, d):
        copy = self.first(d)
        copy.start()
        self.copies.append(copy)

    def take_across(self, d):
        self.first(d).wait_recv()

    def send_outer(self, d):
        copy = self.second(d)
        copy.start()
        self.copies.append(copy)

    def take_outer(self, d):
        self.second(d).wait_recv()

    def finish(self):
        for copy in self.copies:
            copy.wait_send()


def scatter_scratch(count, rows, cols, dtype=jnp.bfloat16, full=False):
    outers = count // INNER
    own = [] if full else [pltpu.VMEM((outers, rows, cols), dtype)]
    return own + [
        pltpu.VMEM((outers, rows, cols), dtype),
        pltpu.VMEM((max(outers - 1, 1), rows, cols), dtype),
        pltpu.VMEM((max(outers - 1, 1), rows, cols), dtype),
        pltpu.SemaphoreType.DMA((outers,)),
        pltpu.SemaphoreType.DMA((outers,)),
        pltpu.SemaphoreType.DMA((max(outers - 1, 1),)),
        pltpu.SemaphoreType.DMA((max(outers - 1, 1),)),
    ]


def comm_params(ident, vmem_mb):
    return pltpu.CompilerParams(
        collective_id=ident, has_side_effects=True, vmem_limit_bytes=vmem_mb * 2**20
    )


def gather_kernel(axes, *refs):
    number = len(axes)
    ins, outs = refs[:number], refs[number : 2 * number]
    sems = refs[2 * number :]
    entry_barrier(sorted(set(axes)))
    gathers, locals_ = [], []
    for k, (axis, count) in enumerate(axes):
        gather = Gather(axis, count, outs[k], sems[3 * k], sems[3 * k + 1], own=ins[k])
        gather.start()
        copy = pltpu.make_async_copy(ins[k], outs[k].at[gather.me], sems[3 * k + 2])
        copy.start()
        gathers.append(gather)
        locals_.append(copy)
    for d in range(1, max(g.outers for g in gathers)):
        for gather in gathers:
            if d < gather.outers:
                gather.forward(d)
    for gather in gathers:
        for d in range(gather.outers):
            gather.arrive(gather.block(d, True))
    for gather, copy in zip(gathers, locals_):
        gather.finish()
        copy.wait()


def gather_all(arrays, axes, ident):
    axes = [(axis, lax.axis_size(axis)) for axis in axes]
    scratch = []
    for _, count in axes:
        scratch += [
            pltpu.SemaphoreType.DMA((count - 1,)),
            pltpu.SemaphoreType.DMA((count,)),
            pltpu.SemaphoreType.DMA,
        ]
    return pl.pallas_call(
        functools.partial(gather_kernel, axes),
        out_shape=[
            jax.ShapeDtypeStruct((count,) + array.shape, array.dtype)
            for array, (_, count) in zip(arrays, axes)
        ],
        in_specs=[pl.BlockSpec(memory_space=pl.ANY)] * len(arrays),
        out_specs=[pl.BlockSpec(memory_space=pl.ANY)] * len(arrays),
        scratch_shapes=scratch,
        compiler_params=comm_params(ident, 16),
        name="gather",
    )(*arrays)


def dot_nn(left, right):
    return lax.dot_general(
        left, right, (((1,), (0,)), ((), ())), preferred_element_type=jnp.float32
    )


def dot_nt(left, right):
    return lax.dot_general(
        left, right, (((1,), (1,)), ((), ())), preferred_element_type=jnp.float32
    )


def dot_tn(left, right):
    return lax.dot_general(
        left, right, (((0,), (0,)), ((), ())), preferred_element_type=jnp.float32
    )


def ffn_kernel(
    count,
    nm_ref,
    tok_ref,
    cot_ref,
    out_w_ref,
    gain_ref,
    cot_any,
    gate_any,
    up_any,
    down_any,
    output_ref,
    d_hidden_ref,
    d_mixer_ref,
    g_gate_ref,
    g_up_ref,
    g_down_ref,
    g_out_ref,
    g_gain_ref,
    cot_rows,
    gate_w,
    up_w,
    down_w,
    n2,
    dh,
    act_s,
    dgate_s,
    dup_s,
    hidden_s,
    dact_s,
    load_sem,
    n2_send,
    n2_recv,
    dh_send,
    dh_recv,
    *scatters,
):
    bf16, f32 = jnp.bfloat16, jnp.float32
    loads = [
        pltpu.make_async_copy(src, dst, load_sem.at[k])
        for k, (src, dst) in enumerate(
            ((cot_any, cot_rows), (down_any, down_w), (gate_any, gate_w), (up_any, up_w))
        )
    ]
    for load in loads:
        load.start()
    entry_barrier([("tp", count)])
    outers = count // INNER
    sets = [scatters[8 * k : 8 * k + 8] for k in range(3)]
    mix_s, dn_s, ffn_s = [
        Scatter("tp", count, s[0], s[1], s[2], s[3], s[4:]) for s in sets
    ]
    order = list(range(1, outers)) + [0]

    for d in order:
        mix_s.out[d] = dot_nt(nm_ref[mix_s.target(d, True)], out_w_ref[...]).astype(bf16)
        mix_s.send_across(d)
    for d in order:
        part = dot_nt(nm_ref[mix_s.target(d, False)], out_w_ref[...])
        mix_s.take_across(d)
        if d:
            mix_s.send2[d - 1] = (part + mix_s.stage[d].astype(f32)).astype(bf16)
            mix_s.send_outer(d)
        else:
            hidden_s[...] = part + mix_s.stage[0].astype(f32) + tok_ref[...].astype(f32)
    loads[0].wait()
    loads[1].wait()
    for b in range(count):
        dact_s[b] = dot_nn(cot_rows[b], down_w[...])
    total = hidden_s[...]
    for d in range(1, outers):
        mix_s.take_outer(d)
        total = total + mix_s.stage2[d - 1].astype(f32)
    hidden_s[...] = total
    root = lax.rsqrt(jnp.mean(total * total, axis=-1, keepdims=True) + 1e-06)
    me = mix_s.me
    n2[me] = (total * root * gain_ref[...]).astype(bf16)
    gather = Gather("tp", count, n2, n2_send, n2_recv)
    gather.start()
    loads[2].wait()
    loads[3].wait()

    def block_ffn(b):
        rows = n2[b]
        gate_pre = dot_nn(rows, gate_w[...])
        up_pre = dot_nn(rows, up_w[...])
        sig = jax.nn.sigmoid(gate_pre)
        silu = gate_pre * sig
        d_active = dact_s[b]
        d_gate = (d_active * up_pre * (sig + silu * (1.0 - sig))).astype(bf16)
        d_up = (d_active * silu).astype(bf16)
        dgate_s[b] = d_gate
        dup_s[b] = d_up
        act_s[b] = (silu * up_pre).astype(bf16)
        return dot_nt(d_gate, gate_w[...]) + dot_nt(d_up, up_w[...])

    own_part = block_ffn(me)
    hold = {0: own_part}
    across = gather.block(0, True)
    gather.arrive(across)
    dn_s.out[0] = block_ffn(across).astype(bf16)
    dn_s.send_across(0)
    for d in range(1, outers):
        gather.forward(d)
    for d in range(1, outers):
        index = gather.block(d, True)
        gather.arrive(index)
        back = outers - d
        dn_s.out[back] = block_ffn(index).astype(bf16)
        dn_s.send_across(back)
    for d in range(1, outers):
        index = gather.block(d, False)
        back = outers - d
        part = block_ffn(index)
        dn_s.take_across(back)
        dn_s.send2[back - 1] = (part + dn_s.stage[back].astype(f32)).astype(bf16)
        dn_s.send_outer(back)
    for d in order:
        b = ffn_s.target(d, True)
        ffn_s.out[d] = dot_nt(act_s[b], down_w[...]).astype(bf16)
        ffn_s.send_across(d)
    g_cols = 256

    def down_grad(k, carry):
        cols = pl.ds(pl.multiple_of(k * g_cols, g_cols), g_cols)
        total = dot_tn(cot_rows[0, :, cols], act_s[0])
        for b in range(1, count):
            total = total + dot_tn(cot_rows[b, :, cols], act_s[b])
        g_down_ref[cols, :] = total.astype(bf16)
        return carry

    width = n2.shape[2]
    lax.fori_loop(0, width // g_cols, down_grad, 0)
    dn_s.take_across(0)
    d_norm = own_part + dn_s.stage[0].astype(f32)
    for d in range(1, outers):
        dn_s.take_outer(d)
        d_norm = d_norm + dn_s.stage2[d - 1].astype(f32)
    hidden = hidden_s[...]
    root = lax.rsqrt(jnp.mean(hidden * hidden, axis=-1, keepdims=True) + 1e-06)
    scaled = hidden * root
    g_gain_ref[...] = jnp.sum(d_norm * scaled, axis=0, keepdims=True)
    pulled = d_norm * gain_ref[...]
    d_hidden = cot_ref[...].astype(f32) + root * (
        pulled - scaled * jnp.mean(pulled * scaled, axis=-1, keepdims=True)
    )
    d_hidden_ref[...] = d_hidden
    dh[me] = d_hidden.astype(bf16)
    gather2 = Gather("tp", count, dh, dh_send, dh_recv)
    gather2.start()
    for d in order:
        part = dot_nt(act_s[ffn_s.target(d, False)], down_w[...])
        ffn_s.take_across(d)
        if d:
            ffn_s.send2[d - 1] = (part + ffn_s.stage[d].astype(f32)).astype(bf16)
            ffn_s.send_outer(d)
        else:
            output_ref[...] = hidden_s[...] + part + ffn_s.stage[0].astype(f32)

    def gate_grad(k, carry):
        cols = pl.ds(pl.multiple_of(k * g_cols, g_cols), g_cols)
        gate_total = dot_tn(n2[0, :, cols], dgate_s[0])
        up_total = dot_tn(n2[0, :, cols], dup_s[0])
        for b in range(1, count):
            gate_total = gate_total + dot_tn(n2[b, :, cols], dgate_s[b])
            up_total = up_total + dot_tn(n2[b, :, cols], dup_s[b])
        g_gate_ref[cols, :] = gate_total.astype(bf16)
        g_up_ref[cols, :] = up_total.astype(bf16)
        return carry

    lax.fori_loop(0, width // g_cols, gate_grad, 0)
    for d in range(1, outers):
        gather2.forward(d)
    for d in range(outers):
        gather2.arrive(gather2.block(d, True))
    for b in range(count):
        d_mixer_ref[b] = dot_nn(dh[b], out_w_ref[...])

    def out_grad(k, carry):
        cols = pl.ds(pl.multiple_of(k * g_cols, g_cols), g_cols)
        total = dot_tn(dh[0, :, cols], nm_ref[0])
        for b in range(1, count):
            total = total + dot_tn(dh[b, :, cols], nm_ref[b])
        g_out_ref[cols, :] = total.astype(bf16)
        return carry

    lax.fori_loop(0, width // g_cols, out_grad, 0)
    for d in range(1, outers):
        ffn_s.take_outer(d)
        output_ref[...] = output_ref[...] + ffn_s.stage2[d - 1].astype(f32)
    for part in (mix_s, gather, dn_s, ffn_s, gather2):
        part.finish()


def ffn_all(nm, tokens, cotangent, out_w, gain, cot_rows, gate_w, up_w, down_w, ident):
    count = lax.axis_size("tp")
    rows, width = tokens.shape
    hidden = gate_w.shape[1]
    values = out_w.shape[1]
    f32, bf16 = jnp.float32, jnp.bfloat16
    vmem = pl.BlockSpec(memory_space=pltpu.VMEM)
    anys = pl.BlockSpec(memory_space=pl.ANY)
    dma = pltpu.SemaphoreType.DMA
    outs = [
        jax.ShapeDtypeStruct((rows, width), f32),
        jax.ShapeDtypeStruct((rows, width), f32),
        jax.ShapeDtypeStruct((count, rows, values), f32),
        jax.ShapeDtypeStruct((width, hidden), bf16),
        jax.ShapeDtypeStruct((width, hidden), bf16),
        jax.ShapeDtypeStruct((width, hidden), bf16),
        jax.ShapeDtypeStruct((width, values), bf16),
        jax.ShapeDtypeStruct((1, width), f32),
    ]
    scratch = [
        pltpu.VMEM((count, rows, width), bf16),
        pltpu.VMEM((width, hidden), bf16),
        pltpu.VMEM((width, hidden), bf16),
        pltpu.VMEM((width, hidden), bf16),
        pltpu.VMEM((count, rows, width), bf16),
        pltpu.VMEM((count, rows, width), bf16),
        pltpu.VMEM((count, rows, hidden), bf16),
        pltpu.VMEM((count, rows, hidden), bf16),
        pltpu.VMEM((count, rows, hidden), bf16),
        pltpu.VMEM((rows, width), f32),
        pltpu.VMEM((count, rows, hidden), f32),
        dma((4,)),
        dma((count - 1,)),
        dma((count,)),
        dma((count - 1,)),
        dma((count,)),
    ]
    for _ in range(3):
        scratch += scatter_scratch(count, rows, width)
    return pl.pallas_call(
        functools.partial(ffn_kernel, count),
        out_shape=outs,
        in_specs=[vmem] * 5 + [anys] * 4,
        out_specs=[vmem] * len(outs),
        scratch_shapes=scratch,
        compiler_params=comm_params(ident, 58),
        name="ffn",
    )(nm, tokens, cotangent, out_w, gain, cot_rows, gate_w, up_w, down_w)


def exchange_small(axis, count, src, buf, send, recv, spread):
    me = lax.axis_index(axis)
    copies = []
    for d in range(1, count):
        peer = lax.rem(me + d, count)
        copy = pltpu.make_async_remote_copy(
            src_ref=src.at[peer] if spread else src,
            dst_ref=buf.at[d - 1],
            send_sem=send.at[d - 1],
            recv_sem=recv.at[d - 1],
            device_id=on_axis(axis, peer),
            device_id_type=MESH,
        )
        copy.start()
        copies.append(copy)
    return copies


def last_kernel(tp_count, fsdp_count, extra_count, *refs):
    bf16, f32 = jnp.bfloat16, jnp.float32
    refs = list(refs)

    def take(number):
        out = refs[:number]
        del refs[:number]
        return out

    d_raw_ref, w_ref, n1_ref, tok_ref, gain_ref, d_hidden_ref, small_ref = take(7)
    extras = take(extra_count)
    d_tok_ref, gw_ref, small_own_ref, small_all_ref = take(4)
    extra_outs = take(extra_count)
    gw_full, small_send, small_buf, small_buf2 = take(4)
    small_sems = take(4)
    dn = take(8)
    fulls = [take(7) for _ in range(1 + extra_count)]
    entry_barrier([("fsdp", fsdp_count), ("tp", tp_count)], everyone=True)
    dn_s = Scatter("tp", tp_count, dn[0], dn[1], dn[2], dn[3], dn[4:])
    sums = [
        Scatter("fsdp", fsdp_count, None, s[0], s[1], s[2], s[3:], full=full)
        for s, full in zip(fulls, [gw_full] + extras)
    ]
    gw_s, extra_s = sums[0], sums[1:]
    tp_order = list(range(1, dn_s.outers)) + [0]
    fsdp_order = list(range(1, gw_s.outers)) + [0]
    for d in tp_order:
        dn_s.out[d] = dot_nt(d_raw_ref[dn_s.target(d, True)], w_ref[...]).astype(bf16)
        dn_s.send_across(d)
    for d in fsdp_order:
        for item in extra_s:
            item.send_across(d)
    depth = gw_full.shape[1]
    chunk = max(256, depth)
    per = chunk // depth

    def weight_grad(k, carry):
        cols = pl.ds(pl.multiple_of(k * chunk, chunk), chunk)
        total = dot_tn(n1_ref[0, :, cols], d_raw_ref[0])
        for b in range(1, tp_count):
            total = total + dot_tn(n1_ref[b, :, cols], d_raw_ref[b])
        for j in range(per):
            gw_full[k * per + j] = total[j * depth : (j + 1) * depth].astype(bf16)
        return carry

    lax.fori_loop(0, n1_ref.shape[2] // chunk, weight_grad, 0)
    for d in fsdp_order:
        gw_s.send_across(d)
    held = None
    for d in tp_order:
        part = dot_nt(d_raw_ref[dn_s.target(d, False)], w_ref[...])
        dn_s.take_across(d)
        if d:
            dn_s.send2[d - 1] = (part + dn_s.stage[d].astype(f32)).astype(bf16)
            dn_s.send_outer(d)
        else:
            held = part + dn_s.stage[0].astype(f32)
    outs = [gw_ref] + list(extra_outs)
    turns = list(zip(sums, outs))
    turns = turns[1:] + turns[:1]
    for item, out in turns:
        for d in fsdp_order:
            item.take_across(d)
            total = item.full[item.target(d, False)].astype(f32) + item.stage[d].astype(f32)
            if d:
                item.send2[d - 1] = total.astype(bf16)
                item.send_outer(d)
            else:
                out[...] = total
    for d in range(1, dn_s.outers):
        dn_s.take_outer(d)
        held = held + dn_s.stage2[d - 1].astype(f32)
    tokens = tok_ref[...].astype(f32)
    root = lax.rsqrt(jnp.mean(tokens * tokens, axis=-1, keepdims=True) + 1e-06)
    scaled = tokens * root
    gain_part = jnp.sum(held * scaled, axis=0, keepdims=True)
    pulled = held * gain_ref[...]
    d_tok_ref[...] = d_hidden_ref[...] + root * (
        pulled - scaled * jnp.mean(pulled * scaled, axis=-1, keepdims=True)
    )
    small_send[...] = small_ref[...]
    share = gain_part.shape[1] // fsdp_count
    for f in range(fsdp_count):
        small_send[f, 0:1, 0:share] = gain_part[:, f * share : (f + 1) * share]
    copies = exchange_small(
        "fsdp", fsdp_count, small_send, small_buf, small_sems[0], small_sems[1], True
    )
    me = lax.axis_index("fsdp")
    small_sum = small_send[me]
    for d, copy in enumerate(copies):
        copy.wait_recv()
        small_sum = small_sum + small_buf[d]
    small_own_ref[...] = small_sum
    copies2 = exchange_small(
        "tp", tp_count, small_own_ref, small_buf2, small_sems[2], small_sems[3], False
    )
    for item, out in turns:
        for d in range(1, item.outers):
            item.take_outer(d)
            out[...] = out[...] + item.stage2[d - 1].astype(f32)
    for d, copy in enumerate(copies2):
        copy.wait_recv()
        small_sum = small_sum + small_buf2[d]
    small_all_ref[...] = small_sum
    for copy in copies + copies2:
        copy.wait_send()
    for item in [dn_s] + sums:
        item.finish()


def last_all(d_raw, w, n1, tokens, gain, d_hidden, small, extras, ident):
    tp_count, fsdp_count = lax.axis_size("tp"), lax.axis_size("fsdp")
    rows, width = tokens.shape
    cols = w.shape[1]
    depth = width // fsdp_count
    f32, bf16 = jnp.float32, jnp.bfloat16
    vmem = pl.BlockSpec(memory_space=pltpu.VMEM)
    dma = pltpu.SemaphoreType.DMA
    outs = [
        jax.ShapeDtypeStruct((rows, width), f32),
        jax.ShapeDtypeStruct((depth, cols), f32),
        jax.ShapeDtypeStruct(small.shape[1:], f32),
        jax.ShapeDtypeStruct(small.shape[1:], f32),
    ] + [jax.ShapeDtypeStruct(extra.shape[1:], f32) for extra in extras]
    scratch = [
        pltpu.VMEM((fsdp_count, depth, cols), bf16),
        pltpu.VMEM(small.shape, f32),
        pltpu.VMEM((fsdp_count - 1,) + small.shape[1:], f32),
        pltpu.VMEM((tp_count - 1,) + small.shape[1:], f32),
        dma((fsdp_count - 1,)),
        dma((fsdp_count - 1,)),
        dma((tp_count - 1,)),
        dma((tp_count - 1,)),
    ]
    scratch += scatter_scratch(tp_count, rows, width)
    scratch += scatter_scratch(fsdp_count, depth, cols, full=True)
    for extra in extras:
        scratch += scatter_scratch(fsdp_count, extra.shape[1], extra.shape[2], full=True)
    return pl.pallas_call(
        functools.partial(last_kernel, tp_count, fsdp_count, len(extras)),
        out_shape=outs,
        in_specs=[vmem] * (7 + len(extras)),
        out_specs=[vmem] * len(outs),
        scratch_shapes=scratch,
        compiler_params=comm_params(ident, 58),
        name="last",
    )(d_raw, w, n1, tokens, gain, d_hidden, small, *extras)


def shards(
    tokens,
    lengths,
    attn_gain,
    w_query,
    w_key,
    w_value,
    w_gate_out,
    w_beta,
    w_decay,
    conv_query,
    conv_key,
    conv_value,
    decay_log,
    decay_bias,
    out_gain,
    w_out,
    ffn_gain,
    w_ffn_gate,
    w_ffn_up,
    w_ffn_down,
    cotangent,
):
    count = lax.axis_size("fsdp")
    shard_rows = tokens.shape[0]
    query_cols, value_cols = w_query.shape[1], w_value.shape[1]
    hidden_cols = w_ffn_gate.shape[1]
    head_count = query_cols // K
    mixed_cols = 2 * query_cols + value_cols
    raw_cols = mixed_cols + value_cols

    tp_count = lax.axis_size("tp")
    width = tokens.shape[1]
    small_list = (attn_gain, ffn_gain, out_gain, conv_query, conv_key, conv_value)
    small = jnp.concatenate([part.astype(jnp.float32).reshape(-1) for part in small_list])
    small_width = -(-small.shape[0] // 1024) * 1024
    small = jnp.pad(small, (0, small_width - small.shape[0])).reshape(8, -1)
    mixer_own = jnp.concatenate(
        [w_query, w_key, w_value, w_gate_out, w_beta, w_decay], axis=1
    )
    token_rows, mixer_w, small = gather_all(
        [tokens, mixer_own, small], ["tp", "fsdp", "fsdp"], 0
    )
    small = small.reshape(count, -1)
    smalls, at = ([], 0)
    for part in small_list:
        piece = small[:, at : at + part.size]
        at = at + part.size
        if part.ndim == 3:
            piece = piece.reshape((count,) + part.shape).transpose(1, 2, 0, 3)
            smalls.append(piece.reshape(part.shape[0], part.shape[1], -1))
        else:
            smalls.append(piece.reshape(-1))
    gain_one, gain_two, norm_out, query_taps, key_taps, value_taps = smalls
    mixer_w = mixer_w.reshape(width, -1)
    token_rows = token_rows.reshape(-1, width).astype(jnp.float32)
    normed_one = rms_scale(token_rows, gain_one).astype(jnp.bfloat16)
    normed_blocks = normed_one.reshape(tp_count, shard_rows, width)
    out_t = lax.all_gather(w_out.T, "fsdp", axis=0, tiled=True)
    ffn_gate_w = lax.all_gather(w_ffn_gate, "fsdp", axis=0, tiled=True)
    ffn_up_w = lax.all_gather(w_ffn_up, "fsdp", axis=0, tiled=True)
    down_t = lax.all_gather(w_ffn_down.T, "fsdp", axis=0, tiled=True)
    row_count = normed_one.shape[0]
    positions = lax.axis_index("fsdp") * row_count + jnp.arange(row_count, dtype=jnp.int32)
    begins = seq_begin(lengths, positions)
    raw = mat_dot(normed_one, mixer_w)
    mixed_raw = raw[:, :mixed_cols].astype(jnp.bfloat16)
    gate_raw = raw[:, mixed_cols:raw_cols]
    beta_raw = raw[:, raw_cols : raw_cols + head_count]
    decay_raw = raw[:, raw_cols + head_count :]
    rim_recv = shifted(mixed_raw[row_count - (CONV - 1) :], "fsdp", 1)

    def front_local(*inputs):
        return front_all(*inputs, begins, positions, head_count)

    block_parts, pull_front = jax.vjp(
        front_local,
        mixed_raw.astype(jnp.float32),
        rim_recv.astype(jnp.float32),
        query_taps,
        key_taps,
        value_taps,
        beta_raw,
        decay_raw,
        decay_log,
        decay_bias,
    )
    scales, maps, offsets = state_maps(block_parts)
    prefixes, final_pair = state_run(scales, maps, offsets)
    pairs, cot_blocks = gather_all(
        [final_pair.astype(jnp.bfloat16), cotangent], ["fsdp", "tp"], 1
    )
    pairs = pairs.astype(jnp.float32)
    state_in = entering(pairs, "fsdp", row_count)
    start_states = (
        jnp.einsum("hnij,hjv->hniv", prefixes[..., :K], state_in, precision=high)
        + prefixes[..., K:]
    )
    mixer_out, pull_back = jax.vjp(
        back_all, block_parts, start_states, split_heads(gate_raw, V), norm_out
    )
    normed_mixer = merge_heads(mixer_out).astype(jnp.bfloat16)
    (
        output,
        d_hidden,
        d_mixer,
        g_gate,
        g_up,
        g_down,
        g_out,
        gain_two_part,
    ) = ffn_all(
        normed_mixer.reshape(tp_count, shard_rows, -1),
        tokens,
        cotangent,
        out_t,
        gain_two.reshape(1, -1),
        cot_blocks,
        ffn_gate_w,
        ffn_up_w,
        down_t,
        2,
    )
    d_mixer = d_mixer.reshape(row_count, -1)
    gain_two_part = gain_two_part.reshape(-1)

    def summed(grad):
        return lax.psum_scatter(grad, "fsdp", scatter_dimension=0, tiled=True).astype(
            jnp.float32
        )

    grad_w_ffn_gate = summed(g_gate)
    grad_w_ffn_up = summed(g_up)
    d_parts, d_starts, d_gate_heads, norm_out_part = pull_back(split_heads(d_mixer, V))
    _, d_state_in = adjoint_run(scales, maps, d_starts, jnp.zeros_like(state_in))
    (d_states,) = gather_all([d_state_in.astype(jnp.bfloat16)], ["fsdp"], 3)
    d_state_out = carried_in(pairs, d_states, "fsdp", row_count)
    d_next, _ = adjoint_run(scales, maps, d_starts, d_state_out)
    _, pull_step = jax.vjp(lambda parts: step_states(parts, start_states), block_parts)
    d_parts = jax.tree.map(jnp.add, d_parts, pull_step(d_next)[0])
    (
        d_mixed,
        d_rim,
        d_query_taps,
        d_key_taps,
        d_value_taps,
        d_beta_raw,
        d_decay_raw,
        d_decay_log,
        d_decay_bias,
    ) = pull_front(d_parts)
    rim_grad = shifted(d_rim, "fsdp", -1)
    d_mixed = d_mixed.at[row_count - (CONV - 1) :].add(rim_grad)
    d_raw = jnp.concatenate(
        [
            part.astype(jnp.bfloat16)
            for part in (d_mixed, merge_heads(d_gate_heads), d_beta_raw, d_decay_raw)
        ],
        axis=1,
    )
    def spread(taps):
        taps = taps.reshape(taps.shape[0], taps.shape[1], count, -1)
        return taps.transpose(2, 0, 1, 3).reshape(count, -1)

    decay_pair = jnp.concatenate([d_decay_log, d_decay_bias])
    small_parts = [
        gain_two_part.reshape(count, -1),
        norm_out_part.reshape(count, -1),
        spread(d_query_taps),
        spread(d_key_taps),
        spread(d_value_taps),
        jnp.broadcast_to(decay_pair[None, :], (count, decay_pair.shape[0])),
    ]
    small_cat = jnp.concatenate(small_parts, axis=1)
    lanes = -(-max(small_cat.shape[1], 7 * (width // count)) // (7 * 128)) * 128
    small_cat = jnp.pad(small_cat, ((0, 0), (lanes, 7 * lanes - small_cat.shape[1])))
    d_tokens, grad_mixer_w, small_own, small_all, grad_down_t, grad_out_t = last_all(
        d_raw.reshape(tp_count, shard_rows, -1),
        mixer_w,
        normed_blocks,
        tokens,
        gain_one.reshape(1, -1),
        d_hidden,
        small_cat.reshape(count, 8, lanes),
        [g_down.reshape(count, width // count, -1), g_out.reshape(count, width // count, -1)],
        4,
    )
    grad_w_ffn_down = grad_down_t.T
    grad_w_out = grad_out_t.T
    cuts = (
        query_cols,
        2 * query_cols,
        mixed_cols,
        raw_cols,
        raw_cols + head_count,
    )
    grads_w = jnp.split(grad_mixer_w, cuts, axis=1)
    small_cuts, at = ([], lanes)
    for part in small_parts:
        small_cuts.append(at)
        at = at + part.shape[1]
    small_cuts.append(at)
    own_parts = jnp.split(small_own.reshape(-1), small_cuts)
    all_parts = jnp.split(small_all.reshape(-1), small_cuts)
    small_out = [
        small_all[0, : width // count],
        all_parts[1],
        all_parts[2],
        own_parts[3],
        own_parts[4],
        own_parts[5],
        own_parts[6],
    ]
    return (
        output,
        d_tokens,
        small_out[0],
        *grads_w,
        small_out[3].reshape(conv_query.shape),
        small_out[4].reshape(conv_key.shape),
        small_out[5].reshape(conv_value.shape),
        small_out[6][:head_count],
        small_out[6][head_count:],
        small_out[2],
        grad_w_out,
        small_out[1],
        grad_w_ffn_gate,
        grad_w_ffn_up,
        grad_w_ffn_down,
    )


def solution(mesh):
    placed = (
        P(("fsdp", "tp"), None),
        P(),
        P("fsdp"),
        P("fsdp", "tp"),
        P("fsdp", "tp"),
        P("fsdp", "tp"),
        P("fsdp", "tp"),
        P("fsdp", "tp"),
        P("fsdp", "tp"),
        P(None, "tp", "fsdp"),
        P(None, "tp", "fsdp"),
        P(None, "tp", "fsdp"),
        P("tp"),
        P("tp"),
        P("fsdp"),
        P("tp", "fsdp"),
        P("fsdp"),
        P("fsdp", "tp"),
        P("fsdp", "tp"),
        P("tp", "fsdp"),
        P(("fsdp", "tp"), None),
    )
    return jax.shard_map(
        shards,
        mesh=mesh,
        in_specs=placed,
        out_specs=(
            P(("fsdp", "tp"), None),
            P(("fsdp", "tp"), None),
            P("fsdp"),
            P("fsdp", "tp"),
            P("fsdp", "tp"),
            P("fsdp", "tp"),
            P("fsdp", "tp"),
            P("fsdp", "tp"),
            P("fsdp", "tp"),
            P(None, "tp", "fsdp"),
            P(None, "tp", "fsdp"),
            P(None, "tp", "fsdp"),
            P("tp"),
            P("tp"),
            P("fsdp"),
            P("tp", "fsdp"),
            P("fsdp"),
            P("fsdp", "tp"),
            P("fsdp", "tp"),
            P("tp", "fsdp"),
        ),
        check_vma=False,
    )
```

```python
import functools

import jax
import jax.numpy as jnp
from jax import lax
from jax.experimental import pallas as pl
from jax.experimental.pallas import tpu as pltpu
from jax.sharding import PartitionSpec as P

K = 128
V = 256
CONV = 4
GROUP = 128
MAXLEN = 4096
RIM = 16


def mat_dot(left, right):
    return jnp.dot(left, right, preferred_element_type=jnp.float32)


def rms_scale(values, scale_gain):
    return (
        values * lax.rsqrt(jnp.mean(values * values, axis=-1, keepdims=True) + 1e-06) * scale_gain
    )


def seq_begin(lengths, positions):
    number = lengths.shape[0]
    earlier = jnp.arange(number)[None, :] < jnp.arange(number)[:, None]
    offsets = jnp.sum(jnp.where(earlier, lengths[None, :], 0), axis=1)
    chosen = jnp.where(offsets[None, :] <= positions[:, None], offsets[None, :], 0)
    return jnp.max(chosen, axis=1)


MESH = pl.DeviceIdType.MESH
INNER = 2


def on_axis(axis, index):
    return {axis: index}


def halves(axis):
    me = lax.axis_index(axis)
    return me, lax.div(me, INNER), lax.rem(me, INNER)


def entry_barrier(axes, everyone=False):
    barrier = pltpu.get_barrier_semaphore()
    total = 0
    for axis, count in axes:
        me, outer, inner = halves(axis)
        outers = count // INNER
        peers = [outer * INNER + (1 - inner)]
        for d in range(1, outers):
            peers.append(lax.rem(outer + d, outers) * INNER + inner)
        if everyone:
            peers = [lax.rem(me + d, count) for d in range(1, count)]
        for peer in peers:
            pl.semaphore_signal(
                barrier, inc=1, device_id=on_axis(axis, peer), device_id_type=MESH
            )
        total += len(peers)
    pl.semaphore_wait(barrier, total)


class Gather:
    def __init__(self, axis, count, buf, send, recv, own=None):
        self.axis, self.count, self.buf, self.send, self.recv = axis, count, buf, send, recv
        self.outers = count // INNER
        self.me, self.outer, self.inner = halves(axis)
        self.own = buf.at[self.me] if own is None else own
        self.copies = []

    def block(self, d, across):
        outer = lax.rem(self.outer + self.outers - d, self.outers)
        return outer * INNER + ((1 - self.inner) if across else self.inner)

    def push(self, src, index, target):
        copy = pltpu.make_async_remote_copy(
            src_ref=src,
            dst_ref=self.buf.at[index],
            send_sem=self.send.at[len(self.copies)],
            recv_sem=self.recv.at[index],
            device_id=on_axis(self.axis, target),
            device_id_type=MESH,
        )
        copy.start()
        self.copies.append(copy)

    def start(self):
        for d in range(1, self.outers):
            self.push(
                self.own, self.me, lax.rem(self.outer + d, self.outers) * INNER + self.inner
            )
        self.push(self.own, self.me, self.outer * INNER + 1 - self.inner)

    def arrive(self, index):
        pltpu.make_async_remote_copy(
            src_ref=self.buf.at[index],
            dst_ref=self.buf.at[index],
            send_sem=self.send.at[0],
            recv_sem=self.recv.at[index],
            device_id=on_axis(self.axis, self.outer * INNER + 1 - self.inner),
            device_id_type=MESH,
        ).wait_recv()

    def forward(self, d):
        index = self.block(d, False)
        self.arrive(index)
        self.push(self.buf.at[index], index, self.outer * INNER + 1 - self.inner)
        return index

    def finish(self):
        for copy in self.copies:
            copy.wait_send()


class Scatter:
    def __init__(self, axis, count, out, stage, send2, stage2, sems, full=None):
        self.axis, self.count, self.full = axis, count, full
        self.outers = count // INNER
        self.me, self.outer, self.inner = halves(axis)
        self.out, self.stage, self.send2, self.stage2 = out, stage, send2, stage2
        self.send_a, self.recv_a, self.send_b, self.recv_b = sems
        self.copies = []

    def target(self, d, across):
        outer = lax.rem(self.outer + d, self.outers)
        return outer * INNER + ((1 - self.inner) if across else self.inner)

    def first(self, d):
        return pltpu.make_async_remote_copy(
            src_ref=self.out.at[d] if self.full is None else self.full.at[self.target(d, True)],
            dst_ref=self.stage.at[d],
            send_sem=self.send_a.at[d],
            recv_sem=self.recv_a.at[d],
            device_id=on_axis(self.axis, self.outer * INNER + 1 - self.inner),
            device_id_type=MESH,
        )

    def second(self, d):
        return pltpu.make_async_remote_copy(
            src_ref=self.send2.at[d - 1],
            dst_ref=self.stage2.at[d - 1],
            send_sem=self.send_b.at[d - 1],
            recv_sem=self.recv_b.at[d - 1],
            device_id=on_axis(self.axis, self.target(d, False)),
            device_id_type=MESH,
        )

    def send_across(self, d):
        copy = self.first(d)
        copy.start()
        self.copies.append(copy)

    def take_across(self, d):
        self.first(d).wait_recv()

    def send_outer(self, d):
        copy = self.second(d)
        copy.start()
        self.copies.append(copy)

    def take_outer(self, d):
        self.second(d).wait_recv()

    def finish(self):
        for copy in self.copies:
            copy.wait_send()


def scatter_scratch(count, rows, cols, dtype=jnp.bfloat16, full=False):
    outers = count // INNER
    own = [] if full else [pltpu.VMEM((outers, rows, cols), dtype)]
    return own + [
        pltpu.VMEM((outers, rows, cols), dtype),
        pltpu.VMEM((max(outers - 1, 1), rows, cols), dtype),
        pltpu.VMEM((max(outers - 1, 1), rows, cols), dtype),
        pltpu.SemaphoreType.DMA((outers,)),
        pltpu.SemaphoreType.DMA((outers,)),
        pltpu.SemaphoreType.DMA((max(outers - 1, 1),)),
        pltpu.SemaphoreType.DMA((max(outers - 1, 1),)),
    ]


def comm_params(ident, vmem_mb):
    return pltpu.CompilerParams(
        collective_id=ident, has_side_effects=True, vmem_limit_bytes=vmem_mb * 2**20
    )


def gather_kernel(axes, *refs):
    number = len(axes)
    ins, outs = refs[:number], refs[number : 2 * number]
    sems = refs[2 * number :]
    entry_barrier(sorted(set(axes)))
    gathers, locals_ = [], []
    for k, (axis, count) in enumerate(axes):
        gather = Gather(axis, count, outs[k], sems[3 * k], sems[3 * k + 1], own=ins[k])
        gather.start()
        copy = pltpu.make_async_copy(ins[k], outs[k].at[gather.me], sems[3 * k + 2])
        copy.start()
        gathers.append(gather)
        locals_.append(copy)
    for d in range(1, max(g.outers for g in gathers)):
        for gather in gathers:
            if d < gather.outers:
                gather.forward(d)
    for gather in gathers:
        for d in range(gather.outers):
            gather.arrive(gather.block(d, True))
    for gather, copy in zip(gathers, locals_):
        gather.finish()
        copy.wait()


def gather_all(arrays, axes, ident):
    axes = [(axis, lax.axis_size(axis)) for axis in axes]
    scratch = []
    for _, count in axes:
        scratch += [
            pltpu.SemaphoreType.DMA((count - 1,)),
            pltpu.SemaphoreType.DMA((count,)),
            pltpu.SemaphoreType.DMA,
        ]
    return pl.pallas_call(
        functools.partial(gather_kernel, axes),
        out_shape=[
            jax.ShapeDtypeStruct((count,) + array.shape, array.dtype)
            for array, (_, count) in zip(arrays, axes)
        ],
        in_specs=[pl.BlockSpec(memory_space=pl.ANY)] * len(arrays),
        out_specs=[pl.BlockSpec(memory_space=pl.ANY)] * len(arrays),
        scratch_shapes=scratch,
        compiler_params=comm_params(ident, 16),
        name="gather",
    )(*arrays)


def dot_nn(left, right):
    return lax.dot_general(
        left, right, (((1,), (0,)), ((), ())), preferred_element_type=jnp.float32
    )


def dot_nt(left, right):
    return lax.dot_general(
        left, right, (((1,), (1,)), ((), ())), preferred_element_type=jnp.float32
    )


def dot_tn(left, right):
    return lax.dot_general(
        left, right, (((0,), (0,)), ((), ())), preferred_element_type=jnp.float32
    )


def ffn_kernel(
    count,
    nm_ref,
    tok_ref,
    cot_ref,
    out_w_ref,
    gain_ref,
    cot_any,
    gate_any,
    up_any,
    down_any,
    output_ref,
    d_hidden_ref,
    d_mixer_ref,
    g_gate_ref,
    g_up_ref,
    g_down_ref,
    g_out_ref,
    g_gain_ref,
    cot_rows,
    gate_w,
    up_w,
    down_w,
    n2,
    dh,
    act_s,
    dgate_s,
    dup_s,
    hidden_s,
    dact_s,
    load_sem,
    n2_send,
    n2_recv,
    dh_send,
    dh_recv,
    *scatters,
):
    bf16, f32 = jnp.bfloat16, jnp.float32
    loads = [
        pltpu.make_async_copy(src, dst, load_sem.at[k])
        for k, (src, dst) in enumerate(
            ((cot_any, cot_rows), (down_any, down_w), (gate_any, gate_w), (up_any, up_w))
        )
    ]
    for load in loads:
        load.start()
    entry_barrier([("tp", count)])
    outers = count // INNER
    sets = [scatters[8 * k : 8 * k + 8] for k in range(3)]
    mix_s, dn_s, ffn_s = [
        Scatter("tp", count, s[0], s[1], s[2], s[3], s[4:]) for s in sets
    ]
    order = list(range(1, outers)) + [0]

    for d in order:
        mix_s.out[d] = dot_nt(nm_ref[mix_s.target(d, True)], out_w_ref[...]).astype(bf16)
        mix_s.send_across(d)
    for d in order:
        part = dot_nt(nm_ref[mix_s.target(d, False)], out_w_ref[...])
        mix_s.take_across(d)
        if d:
            mix_s.send2[d - 1] = (part + mix_s.stage[d].astype(f32)).astype(bf16)
            mix_s.send_outer(d)
        else:
            hidden_s[...] = part + mix_s.stage[0].astype(f32) + tok_ref[...].astype(f32)
    loads[0].wait()
    loads[1].wait()
    for b in range(count):
        dact_s[b] = dot_nn(cot_rows[b], down_w[...])
    total = hidden_s[...]
    for d in range(1, outers):
        mix_s.take_outer(d)
        total = total + mix_s.stage2[d - 1].astype(f32)
    hidden_s[...] = total
    root = lax.rsqrt(jnp.mean(total * total, axis=-1, keepdims=True) + 1e-06)
    me = mix_s.me
    n2[me] = (total * root * gain_ref[...]).astype(bf16)
    gather = Gather("tp", count, n2, n2_send, n2_recv)
    gather.start()
    loads[2].wait()
    loads[3].wait()

    def block_ffn(b):
        rows = n2[b]
        gate_pre = dot_nn(rows, gate_w[...])
        up_pre = dot_nn(rows, up_w[...])
        sig = jax.nn.sigmoid(gate_pre)
        silu = gate_pre * sig
        d_active = dact_s[b]
        d_gate = (d_active * up_pre * (sig + silu * (1.0 - sig))).astype(bf16)
        d_up = (d_active * silu).astype(bf16)
        dgate_s[b] = d_gate
        dup_s[b] = d_up
        act_s[b] = (silu * up_pre).astype(bf16)
        return dot_nt(d_gate, gate_w[...]) + dot_nt(d_up, up_w[...])

    own_part = block_ffn(me)
    hold = {0: own_part}
    across = gather.block(0, True)
    gather.arrive(across)
    dn_s.out[0] = block_ffn(across).astype(bf16)
    dn_s.send_across(0)
    for d in range(1, outers):
        gather.forward(d)
    for d in range(1, outers):
        index = gather.block(d, True)
        gather.arrive(index)
        back = outers - d
        dn_s.out[back] = block_ffn(index).astype(bf16)
        dn_s.send_across(back)
    for d in range(1, outers):
        index = gather.block(d, False)
        back = outers - d
        part = block_ffn(index)
        dn_s.take_across(back)
        dn_s.send2[back - 1] = (part + dn_s.stage[back].astype(f32)).astype(bf16)
        dn_s.send_outer(back)
    for d in order:
        b = ffn_s.target(d, True)
        ffn_s.out[d] = dot_nt(act_s[b], down_w[...]).astype(bf16)
        ffn_s.send_across(d)
    g_cols = 256

    def down_grad(k, carry):
        cols = pl.ds(pl.multiple_of(k * g_cols, g_cols), g_cols)
        total = dot_tn(cot_rows[0, :, cols], act_s[0])
        for b in range(1, count):
            total = total + dot_tn(cot_rows[b, :, cols], act_s[b])
        g_down_ref[cols, :] = total.astype(bf16)
        return carry

    width = n2.shape[2]
    lax.fori_loop(0, width // g_cols, down_grad, 0)
    dn_s.take_across(0)
    d_norm = own_part + dn_s.stage[0].astype(f32)
    for d in range(1, outers):
        dn_s.take_outer(d)
        d_norm = d_norm + dn_s.stage2[d - 1].astype(f32)
    hidden = hidden_s[...]
    root = lax.rsqrt(jnp.mean(hidden * hidden, axis=-1, keepdims=True) + 1e-06)
    scaled = hidden * root
    g_gain_ref[...] = jnp.sum(d_norm * scaled, axis=0, keepdims=True)
    pulled = d_norm * gain_ref[...]
    d_hidden = cot_ref[...].astype(f32) + root * (
        pulled - scaled * jnp.mean(pulled * scaled, axis=-1, keepdims=True)
    )
    d_hidden_ref[...] = d_hidden
    dh[me] = d_hidden.astype(bf16)
    gather2 = Gather("tp", count, dh, dh_send, dh_recv)
    gather2.start()
    for d in order:
        part = dot_nt(act_s[ffn_s.target(d, False)], down_w[...])
        ffn_s.take_across(d)
        if d:
            ffn_s.send2[d - 1] = (part + ffn_s.stage[d].astype(f32)).astype(bf16)
            ffn_s.send_outer(d)
        else:
            output_ref[...] = hidden_s[...] + part + ffn_s.stage[0].astype(f32)

    def gate_grad(k, carry):
        cols = pl.ds(pl.multiple_of(k * g_cols, g_cols), g_cols)
        gate_total = dot_tn(n2[0, :, cols], dgate_s[0])
        up_total = dot_tn(n2[0, :, cols], dup_s[0])
        for b in range(1, count):
            gate_total = gate_total + dot_tn(n2[b, :, cols], dgate_s[b])
            up_total = up_total + dot_tn(n2[b, :, cols], dup_s[b])
        g_gate_ref[cols, :] = gate_total.astype(bf16)
        g_up_ref[cols, :] = up_total.astype(bf16)
        return carry

    lax.fori_loop(0, width // g_cols, gate_grad, 0)
    for d in range(1, outers):
        gather2.forward(d)
    for d in range(outers):
        gather2.arrive(gather2.block(d, True))
    for b in range(count):
        d_mixer_ref[b] = dot_nn(dh[b], out_w_ref[...])

    def out_grad(k, carry):
        cols = pl.ds(pl.multiple_of(k * g_cols, g_cols), g_cols)
        total = dot_tn(dh[0, :, cols], nm_ref[0])
        for b in range(1, count):
            total = total + dot_tn(dh[b, :, cols], nm_ref[b])
        g_out_ref[cols, :] = total.astype(bf16)
        return carry

    lax.fori_loop(0, width // g_cols, out_grad, 0)
    for d in range(1, outers):
        ffn_s.take_outer(d)
        output_ref[...] = output_ref[...] + ffn_s.stage2[d - 1].astype(f32)
    for part in (mix_s, gather, dn_s, ffn_s, gather2):
        part.finish()


def ffn_all(nm, tokens, cotangent, out_w, gain, cot_rows, gate_w, up_w, down_w, ident):
    count = lax.axis_size("tp")
    rows, width = tokens.shape
    hidden = gate_w.shape[1]
    values = out_w.shape[1]
    f32, bf16 = jnp.float32, jnp.bfloat16
    vmem = pl.BlockSpec(memory_space=pltpu.VMEM)
    anys = pl.BlockSpec(memory_space=pl.ANY)
    dma = pltpu.SemaphoreType.DMA
    outs = [
        jax.ShapeDtypeStruct((rows, width), f32),
        jax.ShapeDtypeStruct((rows, width), f32),
        jax.ShapeDtypeStruct((count, rows, values), f32),
        jax.ShapeDtypeStruct((width, hidden), bf16),
        jax.ShapeDtypeStruct((width, hidden), bf16),
        jax.ShapeDtypeStruct((width, hidden), bf16),
        jax.ShapeDtypeStruct((width, values), bf16),
        jax.ShapeDtypeStruct((1, width), f32),
    ]
    scratch = [
        pltpu.VMEM((count, rows, width), bf16),
        pltpu.VMEM((width, hidden), bf16),
        pltpu.VMEM((width, hidden), bf16),
        pltpu.VMEM((width, hidden), bf16),
        pltpu.VMEM((count, rows, width), bf16),
        pltpu.VMEM((count, rows, width), bf16),
        pltpu.VMEM((count, rows, hidden), bf16),
        pltpu.VMEM((count, rows, hidden), bf16),
        pltpu.VMEM((count, rows, hidden), bf16),
        pltpu.VMEM((rows, width), f32),
        pltpu.VMEM((count, rows, hidden), f32),
        dma((4,)),
        dma((count - 1,)),
        dma((count,)),
        dma((count - 1,)),
        dma((count,)),
    ]
    for _ in range(3):
        scratch += scatter_scratch(count, rows, width)
    return pl.pallas_call(
        functools.partial(ffn_kernel, count),
        out_shape=outs,
        in_specs=[vmem] * 5 + [anys] * 4,
        out_specs=[vmem] * len(outs),
        scratch_shapes=scratch,
        compiler_params=comm_params(ident, 58),
        name="ffn",
    )(nm, tokens, cotangent, out_w, gain, cot_rows, gate_w, up_w, down_w)


def exchange_small(axis, count, src, buf, send, recv, spread):
    me = lax.axis_index(axis)
    copies = []
    for d in range(1, count):
        peer = lax.rem(me + d, count)
        copy = pltpu.make_async_remote_copy(
            src_ref=src.at[peer] if spread else src,
            dst_ref=buf.at[d - 1],
            send_sem=send.at[d - 1],
            recv_sem=recv.at[d - 1],
            device_id=on_axis(axis, peer),
            device_id_type=MESH,
        )
        copy.start()
        copies.append(copy)
    return copies


def last_kernel(tp_count, fsdp_count, extra_count, *refs):
    bf16, f32 = jnp.bfloat16, jnp.float32
    refs = list(refs)

    def take(number):
        out = refs[:number]
        del refs[:number]
        return out

    d_raw_ref, w_ref, n1_ref, tok_ref, gain_ref, d_hidden_ref, small_ref = take(7)
    extras = take(extra_count)
    d_tok_ref, gw_ref, small_own_ref, small_all_ref = take(4)
    extra_outs = take(extra_count)
    gw_full, small_send, small_buf, small_buf2 = take(4)
    small_sems = take(4)
    dn = take(8)
    fulls = [take(7) for _ in range(1 + extra_count)]
    entry_barrier([("fsdp", fsdp_count), ("tp", tp_count)], everyone=True)
    dn_s = Scatter("tp", tp_count, dn[0], dn[1], dn[2], dn[3], dn[4:])
    sums = [
        Scatter("fsdp", fsdp_count, None, s[0], s[1], s[2], s[3:], full=full)
        for s, full in zip(fulls, [gw_full] + extras)
    ]
    gw_s, extra_s = sums[0], sums[1:]
    tp_order = list(range(1, dn_s.outers)) + [0]
    fsdp_order = list(range(1, gw_s.outers)) + [0]
    for d in tp_order:
        dn_s.out[d] = dot_nt(d_raw_ref[dn_s.target(d, True)], w_ref[...]).astype(bf16)
        dn_s.send_across(d)
    for d in fsdp_order:
        for item in extra_s:
            item.send_across(d)
    depth = gw_full.shape[1]
    chunk = max(256, depth)
    per = chunk // depth

    def weight_grad(k, carry):
        cols = pl.ds(pl.multiple_of(k * chunk, chunk), chunk)
        total = dot_tn(n1_ref[0, :, cols], d_raw_ref[0])
        for b in range(1, tp_count):
            total = total + dot_tn(n1_ref[b, :, cols], d_raw_ref[b])
        for j in range(per):
            gw_full[k * per + j] = total[j * depth : (j + 1) * depth].astype(bf16)
        return carry

    lax.fori_loop(0, n1_ref.shape[2] // chunk, weight_grad, 0)
    for d in fsdp_order:
        gw_s.send_across(d)
    held = None
    for d in tp_order:
        part = dot_nt(d_raw_ref[dn_s.target(d, False)], w_ref[...])
        dn_s.take_across(d)
        if d:
            dn_s.send2[d - 1] = (part + dn_s.stage[d].astype(f32)).astype(bf16)
            dn_s.send_outer(d)
        else:
            held = part + dn_s.stage[0].astype(f32)
    outs = [gw_ref] + list(extra_outs)
    turns = list(zip(sums, outs))
    turns = turns[1:] + turns[:1]
    for item, out in turns:
        for d in fsdp_order:
            item.take_across(d)
            total = item.full[item.target(d, False)].astype(f32) + item.stage[d].astype(f32)
            if d:
                item.send2[d - 1] = total.astype(bf16)
                item.send_outer(d)
            else:
                out[...] = total
    for d in range(1, dn_s.outers):
        dn_s.take_outer(d)
        held = held + dn_s.stage2[d - 1].astype(f32)
    tokens = tok_ref[...].astype(f32)
    root = lax.rsqrt(jnp.mean(tokens * tokens, axis=-1, keepdims=True) + 1e-06)
    scaled = tokens * root
    gain_part = jnp.sum(held * scaled, axis=0, keepdims=True)
    pulled = held * gain_ref[...]
    d_tok_ref[...] = d_hidden_ref[...] + root * (
        pulled - scaled * jnp.mean(pulled * scaled, axis=-1, keepdims=True)
    )
    small_send[...] = small_ref[...]
    share = gain_part.shape[1] // fsdp_count
    for f in range(fsdp_count):
        small_send[f, 0:1, 0:share] = gain_part[:, f * share : (f + 1) * share]
    copies = exchange_small(
        "fsdp", fsdp_count, small_send, small_buf, small_sems[0], small_sems[1], True
    )
    me = lax.axis_index("fsdp")
    small_sum = small_send[me]
    for d, copy in enumerate(copies):
        copy.wait_recv()
        small_sum = small_sum + small_buf[d]
    small_own_ref[...] = small_sum
    copies2 = exchange_small(
        "tp", tp_count, small_own_ref, small_buf2, small_sems[2], small_sems[3], False
    )
    for item, out in turns:
        for d in range(1, item.outers):
            item.take_outer(d)
            out[...] = out[...] + item.stage2[d - 1].astype(f32)
    for d, copy in enumerate(copies2):
        copy.wait_recv()
        small_sum = small_sum + small_buf2[d]
    small_all_ref[...] = small_sum
    for copy in copies + copies2:
        copy.wait_send()
    for item in [dn_s] + sums:
        item.finish()


def last_all(d_raw, w, n1, tokens, gain, d_hidden, small, extras, ident):
    tp_count, fsdp_count = lax.axis_size("tp"), lax.axis_size("fsdp")
    rows, width = tokens.shape
    cols = w.shape[1]
    depth = width // fsdp_count
    f32, bf16 = jnp.float32, jnp.bfloat16
    vmem = pl.BlockSpec(memory_space=pltpu.VMEM)
    dma = pltpu.SemaphoreType.DMA
    outs = [
        jax.ShapeDtypeStruct((rows, width), f32),
        jax.ShapeDtypeStruct((depth, cols), f32),
        jax.ShapeDtypeStruct(small.shape[1:], f32),
        jax.ShapeDtypeStruct(small.shape[1:], f32),
    ] + [jax.ShapeDtypeStruct(extra.shape[1:], f32) for extra in extras]
    scratch = [
        pltpu.VMEM((fsdp_count, depth, cols), bf16),
        pltpu.VMEM(small.shape, f32),
        pltpu.VMEM((fsdp_count - 1,) + small.shape[1:], f32),
        pltpu.VMEM((tp_count - 1,) + small.shape[1:], f32),
        dma((fsdp_count - 1,)),
        dma((fsdp_count - 1,)),
        dma((tp_count - 1,)),
        dma((tp_count - 1,)),
    ]
    scratch += scatter_scratch(tp_count, rows, width)
    scratch += scatter_scratch(fsdp_count, depth, cols, full=True)
    for extra in extras:
        scratch += scatter_scratch(fsdp_count, extra.shape[1], extra.shape[2], full=True)
    return pl.pallas_call(
        functools.partial(last_kernel, tp_count, fsdp_count, len(extras)),
        out_shape=outs,
        in_specs=[vmem] * (7 + len(extras)),
        out_specs=[vmem] * len(outs),
        scratch_shapes=scratch,
        compiler_params=comm_params(ident, 58),
        name="last",
    )(d_raw, w, n1, tokens, gain, d_hidden, small, *extras)


def split_two(value):
    top = value.astype(jnp.bfloat16)
    return top, (value - top.astype(jnp.float32)).astype(jnp.bfloat16)


def dot_three(left, right, dot):
    (a, b), (c, d) = split_two(left), split_two(right)
    return dot(a, c) + (dot(a, d) + dot(b, c))


def half(value):
    return value.astype(jnp.bfloat16)


def triangles():
    row = lax.broadcasted_iota(jnp.int32, (GROUP, GROUP), 0)
    col = lax.broadcasted_iota(jnp.int32, (GROUP, GROUP), 1)
    return row, col


def pair_mask(row, col, step):
    shift = step.bit_length() - 1
    high_row, high_col = row >> shift, col >> shift
    return ((high_row >> 1) == (high_col >> 1)) & (high_row > high_col)


def unit_inverses(lowers):
    row, col = triangles()
    eye = (row == col).astype(jnp.float32)
    mask = pair_mask(row, col, 1)
    inverses = [eye - jnp.where(mask, lower, 0.0) for lower in lowers]
    step = 2
    while step < GROUP:
        mask = pair_mask(row, col, step)
        corners = [half(jnp.where(mask, lower, 0.0)) for lower in lowers]
        tops = [half(inverse) for inverse in inverses]
        inner = [half(dot_nn(top, corner)) for top, corner in zip(tops, corners)]
        inverses = [
            inverse - dot_nn(left, top) for inverse, left, top in zip(inverses, inner, tops)
        ]
        step = step * 2
    rest = [
        eye - inverse - dot_three(lower, inverse, dot_nn)
        for inverse, lower in zip(inverses, lowers)
    ]
    return [
        inverse + dot_nn(half(inverse), half(gap)) for inverse, gap in zip(inverses, rest)
    ]


def conv_rows(padded, taps, ranges):
    rim = padded.shape[0] - GROUP
    total = taps[0:1] * padded[rim:]
    for lag in range(1, CONV):
        total = total + taps[lag : lag + 1] * (
            pltpu.roll(padded, lag, 0)[rim:] * ranges[lag - 1]
        )
    return total


def unit_norm(values):
    return lax.rsqrt(jnp.sum(values * values, axis=-1, keepdims=True) + 1e-06)


def soft_plus(value):
    return jnp.maximum(value, 0.0) + jnp.log1p(jnp.exp(-jnp.abs(value)))


class Chunk:
    def __init__(self, refs, head, heads, n, first_place):
        padded_ref, taps_ref, bd_ref, begin_ref, rate_ref, shift_ref = refs
        self.head, self.n = head, n
        cols = (
            (head * K, K),
            (heads * K + head * K, K),
            (2 * heads * K + head * V, V),
        )
        self.cols = cols
        if isinstance(n, int):
            rows, padded_rows = pl.ds(n * GROUP, GROUP), pl.ds(n * GROUP, GROUP + RIM)
        else:
            start = pl.multiple_of(n * GROUP, GROUP)
            rows, padded_rows = pl.ds(start, GROUP), pl.ds(start, GROUP + RIM)
        self.rows = rows
        row, col = triangles()
        begin = begin_ref[rows, :]
        base = first_place + n * GROUP
        place = base + lax.broadcasted_iota(jnp.int32, (GROUP, 1), 0)
        self.ranges = [
            (place - lag >= begin).astype(jnp.float32) for lag in range(1, CONV)
        ]
        self.padded = [
            padded_ref[padded_rows, at : at + size].astype(jnp.float32) for at, size in cols
        ]
        self.taps = [taps_ref[:, at : at + size] for at, size in cols]
        self.pres = [
            conv_rows(padded, taps, self.ranges)
            for padded, taps in zip(self.padded, self.taps)
        ]
        self.sigs = [jax.nn.sigmoid(pre) for pre in self.pres]
        query, key, self.value = [pre * sig for pre, sig in zip(self.pres, self.sigs)]
        self.query_root, self.key_root = unit_norm(query), unit_norm(key)
        self.query = query * (self.query_root * K ** (-0.5))
        self.key = key * self.key_root
        self.beta = jax.nn.sigmoid(bd_ref[rows, head : head + 1])
        self.decay_in = bd_ref[rows, heads + head : heads + head + 1] + shift_ref[head]
        self.rate = rate_ref[head]
        decay = self.rate * soft_plus(self.decay_in)
        self.decay = decay
        lower = row >= col
        decay_row = jnp.sum(jnp.where(row == col, decay, 0.0), axis=0, keepdims=True)
        cumul = jnp.sum(jnp.where(lower, decay_row, 0.0), axis=1, keepdims=True)
        cumul_row = jnp.sum(jnp.where(row <= col, decay, 0.0), axis=0, keepdims=True)
        same = (begin <= base + col) & lower
        self.factor = jnp.where(same, jnp.exp(jnp.where(same, cumul - cumul_row, 0.0)), 0.0)
        self.carry = jnp.where(begin < base, jnp.exp(cumul), 0.0)
        self.scale = self.carry[GROUP - 1 :, :]
        last_alive = begin[GROUP - 1 :, :] <= place
        gap = cumul[GROUP - 1 :, :] - cumul
        self.last = jnp.where(last_alive, jnp.exp(jnp.where(last_alive, gap, 0.0)), 0.0)
        self.key_last = self.key * self.last
        self.weights = jnp.where(row > col, self.factor, 0.0)

    def sides(self):
        return jnp.concatenate(
            [self.beta * self.value, (self.beta * self.carry) * self.key], axis=1
        )


def mixer_kernel(heads, blocks, tp_count, fsdp_count, wide, weight_count, *refs):
    bf16, f32 = jnp.bfloat16, jnp.float32
    refs = list(refs)

    def take(number):
        out = refs[:number]
        del refs[:number]
        return out

    mixed_any, gate_ref, bd_ref, taps_ref, begin_ref, rate_ref, shift_ref, norm_ref = take(8)
    cot_any = take(1)[0]
    shards = take(weight_count)
    normed_ref, inv_ref, side_ref, query_ref, score_ref, state_ref, update_ref, out_ref = take(8)
    maps, scales, padded, pairs, cot_rows = take(5)
    wholes = take(weight_count)
    prefix, own_pair, rim_sems, load_sem, pair_send, pair_recv, cot_sems, cot_send, cot_recv = take(9)
    weight_sems = take(3 * weight_count)
    rows = blocks * GROUP
    mine = lax.axis_index("fsdp")
    load = pltpu.make_async_copy(mixed_any, padded.at[pl.ds(RIM, rows)], load_sem)
    load.start()
    entry_barrier([("fsdp", fsdp_count), ("tp", tp_count)], everyone=True)
    rim = pltpu.make_async_remote_copy(
        src_ref=mixed_any.at[pl.ds(rows - RIM, RIM)],
        dst_ref=padded.at[pl.ds(0, RIM)],
        send_sem=rim_sems.at[0],
        recv_sem=rim_sems.at[1],
        device_id=on_axis("fsdp", lax.rem(mine + 1, fsdp_count)),
        device_id_type=MESH,
    )
    rim.start()
    gathers, locals_ = [], []
    for k in range(weight_count):
        sems = weight_sems[3 * k : 3 * k + 3]
        gather = Gather("fsdp", fsdp_count, wholes[k], sems[0], sems[1], own=shards[k])
        copy = pltpu.make_async_copy(shards[k], wholes[k].at[mine], sems[2])
        gather.start()
        copy.start()
        gathers.append(gather)
        locals_.append(copy)
    cot = Gather("tp", tp_count, cot_rows, cot_send, cot_recv, own=cot_any)
    cot.start()
    cot_local = pltpu.make_async_copy(cot_any, cot_rows.at[cot.me], cot_sems)
    cot_local.start()
    load.wait()
    rim.wait()
    first_place = mine * rows
    source = (padded, taps_ref, bd_ref, begin_ref, rate_ref, shift_ref)
    row, col = triangles()
    for h in range(heads):
        own_pair[h] = jnp.concatenate(
            [(row == col).astype(f32), jnp.zeros((K, V), f32)], axis=1
        )

    def front(step, carry):
        units = [
            Chunk(source, h, heads, step * wide + j, first_place)
            for j in range(wide)
            for h in range(heads)
        ]
        lowers = [
            unit.beta * dot_three(unit.key, unit.key, dot_nt) * unit.weights for unit in units
        ]
        inverses = [half(inverse) for inverse in unit_inverses(lowers)]
        solved = [dot_nn(inv, half(unit.sides())) for inv, unit in zip(inverses, units)]
        for unit, inv, sides in zip(units, inverses, solved):
            h, n = unit.head, unit.n
            inv_ref[h, n] = inv
            side_ref[h, n] = sides
            query_ref[h, n] = half(unit.query * unit.carry)
            score_ref[h, n] = half(
                dot_nt(half(unit.query), half(unit.key)) * unit.factor
            )
            driven = dot_tn(half(unit.key_last), half(sides))
            maps[h, n] = driven[:, V:]
            scales[h, n] = jnp.broadcast_to(unit.scale, (8, 128))
            pair = own_pair[h]
            prefix[h, n] = pair
            moved = dot_three(driven[:, V:], pair, dot_nn)
            drive = jnp.concatenate([jnp.zeros((K, K), f32), driven[:, :V]], axis=1)
            own_pair[h] = unit.scale * pair + drive - moved
        return carry

    turns = blocks // wide
    early = max(1, turns // 2)
    lax.fori_loop(0, early, front, 0)
    for d in range(1, cot.outers):
        cot.forward(d)
    for d in range(1, gathers[0].outers if gathers else 1):
        for gather in gathers:
            gather.forward(d)
    lax.fori_loop(early, turns, front, 0)
    for h in range(heads):
        pairs[mine, pl.ds(h * K, K), :] = half(own_pair[h])
    ring = Gather("fsdp", fsdp_count, pairs, pair_send, pair_recv)
    ring.start()
    for d in range(1, ring.outers):
        ring.forward(d)
    for d in range(ring.outers):
        ring.arrive(ring.block(d, True))
    hops = min(fsdp_count - 1, -(-MAXLEN // rows))
    states = [jnp.zeros((K, V), f32) for _ in range(heads)]
    for hop in range(hops, 0, -1):
        spot = jnp.maximum(mine - hop, 0)
        for h in range(heads):
            piece = pairs[spot, pl.ds(h * K, K), :]
            top, low = split_two(states[h])
            new = dot_nn(piece[:, :K], top) + dot_nn(piece[:, :K], low)
            states[h] = jnp.where(mine >= hop, new + piece[:, K:].astype(f32), states[h])

    def back(n, carry):
        at = pl.ds(pl.multiple_of(n * GROUP, GROUP), GROUP)
        for h in range(heads):
            pair = prefix[h, n]
            start = half(dot_three(pair[:, :K], states[h], dot_nn) + pair[:, K:])
            state_ref[h, n] = start
            sides = side_ref[h, n]
            update = half(sides[:, :V] - dot_nn(half(sides[:, V:]), start))
            update_ref[h, n] = update
            out = dot_nn(query_ref[h, n], start) + dot_nn(score_ref[h, n], update)
            out_ref[h, n] = out
            gate = gate_ref[at, h * V : (h + 1) * V]
            root = lax.rsqrt(jnp.mean(out * out, axis=-1, keepdims=True) + 1e-06)
            normed_ref[at, h * V : (h + 1) * V] = half(
                out * root * norm_ref[...] * (gate * jax.nn.sigmoid(gate))
            )
        return carry

    lax.fori_loop(0, blocks, back, 0)
    for d in range(cot.outers):
        cot.arrive(cot.block(d, True))
    for gather in gathers:
        for d in range(gather.outers):
            gather.arrive(gather.block(d, True))
    for copy in locals_ + [cot_local]:
        copy.wait()
    for gather in gathers + [ring, cot]:
        gather.finish()


def mixer_all(mixed, gate, bd, taps, begins, rate, shift, norm, cotangent, shards, ident):
    tp_count, fsdp_count = lax.axis_size("tp"), lax.axis_size("fsdp")
    heads = bd.shape[1] // 2
    rows = mixed.shape[0]
    blocks = rows // GROUP
    wide = 2 if blocks % 2 == 0 else 1
    f32, bf16 = jnp.float32, jnp.bfloat16
    vmem = pl.BlockSpec(memory_space=pltpu.VMEM)
    smem = pl.BlockSpec(memory_space=pltpu.SMEM)
    anys = pl.BlockSpec(memory_space=pl.ANY)
    dma = pltpu.SemaphoreType.DMA
    shape = jax.ShapeDtypeStruct
    outs = [
        shape((rows, heads * V), bf16),
        shape((heads, blocks, GROUP, GROUP), bf16),
        shape((heads, blocks, GROUP, V + K), f32),
        shape((heads, blocks, GROUP, K), bf16),
        shape((heads, blocks, GROUP, GROUP), bf16),
        shape((heads, blocks, K, V), bf16),
        shape((heads, blocks, GROUP, V), bf16),
        shape((heads, blocks, GROUP, V), f32),
        shape((heads, blocks, K, K), f32),
        shape((heads, blocks, 8, 128), f32),
        shape((rows + RIM, mixed.shape[1]), bf16),
        shape((fsdp_count, heads * K, K + V), bf16),
        shape((tp_count,) + cotangent.shape, bf16),
    ] + [shape((fsdp_count,) + shard.shape, shard.dtype) for shard in shards]
    scratch = [
        pltpu.VMEM((heads, blocks, K, K + V), f32),
        pltpu.VMEM((heads, K, K + V), f32),
        dma((2,)),
        dma,
        dma((fsdp_count - 1,)),
        dma((fsdp_count,)),
        dma,
        dma((tp_count - 1,)),
        dma((tp_count,)),
    ]
    for _ in shards:
        scratch += [dma((fsdp_count - 1,)), dma((fsdp_count,)), dma]
    return pl.pallas_call(
        functools.partial(
            mixer_kernel, heads, blocks, tp_count, fsdp_count, wide, len(shards)
        ),
        out_shape=outs,
        in_specs=[anys] + [vmem] * 4 + [smem] * 2 + [vmem] + [anys] * (1 + len(shards)),
        out_specs=[vmem] * 12 + [anys] * (1 + len(shards)),
        scratch_shapes=scratch,
        compiler_params=comm_params(ident, 56),
        name="mixer",
    )(mixed, gate, bd, taps, begins, rate, shift, norm, cotangent, *shards)


def mixer_grad_kernel(heads, blocks, tp_count, fsdp_count, extra_count, *refs):
    bf16, f32 = jnp.bfloat16, jnp.float32
    refs = list(refs)

    def take(number):
        out = refs[:number]
        del refs[:number]
        return out

    padded, gate_ref, bd_ref, taps_ref, begin_ref, rate_ref, shift_ref, norm_ref = take(8)
    inv_ref, side_ref, query_ref, score_ref, state_ref, update_ref, out_ref = take(7)
    maps, scales, pairs, dm_ref = take(4)
    extras = take(extra_count)
    d_raw_ref, g_taps_ref, g_decay_ref, g_norm_ref = take(4)
    extra_outs = take(extra_count)
    d_out, base, local, d_state, halo, tail, d_all, rim_buf = take(8)
    rim_sems, ring_send, ring_recv = take(3)
    fulls = [take(7) for _ in range(extra_count)]
    rows = blocks * GROUP
    mine = lax.axis_index("fsdp")
    first_place = mine * rows
    mixed_cols = 2 * heads * K + heads * V
    entry_barrier([("fsdp", fsdp_count)], everyone=True)
    sums = [
        Scatter("fsdp", fsdp_count, None, s[0], s[1], s[2], s[3:], full=full)
        for s, full in zip(fulls, extras)
    ]
    outers = fsdp_count // INNER
    order = list(range(1, outers)) + [0]
    for item in sums:
        for d in order:
            item.send_across(d)
    g_norm_ref[...] = jnp.zeros_like(g_norm_ref)
    g_taps_ref[...] = jnp.zeros_like(g_taps_ref)
    g_decay_ref[...] = jnp.zeros_like(g_decay_ref)
    halo[...] = jnp.zeros_like(halo)
    source = (padded, taps_ref, bd_ref, begin_ref, rate_ref, shift_ref)
    row, col = triangles()

    def first(n, carry):
        at = pl.ds(pl.multiple_of(n * GROUP, GROUP), GROUP)
        for h in range(heads):
            cols = slice(h * V, (h + 1) * V)
            out = out_ref[h, n]
            root = lax.rsqrt(jnp.mean(out * out, axis=-1, keepdims=True) + 1e-06)
            normed = out * root
            gate = gate_ref[at, cols]
            sig = jax.nn.sigmoid(gate)
            silu = gate * sig
            given = dm_ref[at, cols]
            g_norm_ref[...] += jnp.sum(given * normed * silu, axis=0, keepdims=True)
            pulled = given * norm_ref[...]
            d_raw_ref[at, mixed_cols + h * V : mixed_cols + (h + 1) * V] = half(
                pulled * normed * (sig + silu * (1.0 - sig))
            )
            pulled = pulled * silu
            grad = root * (pulled - normed * jnp.mean(pulled * normed, axis=-1, keepdims=True))
            grad = half(grad)
            d_out[h, n] = grad
            through = dot_tn(score_ref[h, n], grad)
            base[h, n] = through
            key_part = half(side_ref[h, n][:, V:])
            local[h, n] = dot_tn(query_ref[h, n], grad) - dot_tn(key_part, half(through))
        return carry

    lax.fori_loop(0, blocks, first, 0)

    def pull_state(n, h, grad):
        scale = scales[h, n][0:1, 0:1]
        return scale * grad + local[h, n] - dot_three(maps[h, n], grad, dot_tn)

    for h in range(heads):
        d_state[h] = jnp.zeros((K, V), f32)

    def chain(step, carry):
        n = blocks - 1 - step
        for h in range(heads):
            d_state[h] = pull_state(n, h, d_state[h])
        return carry

    lax.fori_loop(0, blocks, chain, 0)
    for h in range(heads):
        d_all[mine, pl.ds(h * K, K), :] = half(d_state[h])
    ring = Gather("fsdp", fsdp_count, d_all, ring_send, ring_recv)
    ring.start()
    for item in sums:
        for d in order:
            item.take_across(d)
            total = item.full[item.target(d, False)].astype(f32) + item.stage[d].astype(f32)
            if d:
                item.send2[d - 1] = half(total)
                item.send_outer(d)
            else:
                extra_outs[sums.index(item)][...] = total
    for d in range(1, ring.outers):
        ring.forward(d)
    for d in range(ring.outers):
        ring.arrive(ring.block(d, True))
    hops = min(fsdp_count - 1, -(-MAXLEN // rows))
    for h in range(heads):
        grad = jnp.zeros((K, V), f32)
        for hop in range(hops, 0, -1):
            spot = jnp.minimum(mine + hop, fsdp_count - 1)
            piece = pairs[spot, pl.ds(h * K, K), :][:, :K]
            top, low = split_two(grad)
            new = dot_tn(piece, top) + dot_tn(piece, low)
            new = new + d_all[spot, pl.ds(h * K, K), :].astype(f32)
            grad = jnp.where(mine + hop < fsdp_count, new, grad)
        d_state[h] = grad

    def second(step, carry):
        n = blocks - 1 - step
        at = pl.ds(pl.multiple_of(n * GROUP, GROUP), GROUP)
        lane = lax.broadcasted_iota(jnp.int32, (1, g_decay_ref.shape[1]), 1)
        smalls = []
        for h in range(heads):
            unit = Chunk(source, h, heads, n, first_place)
            query, key, key_last = half(unit.query), half(unit.key), half(unit.key_last)
            after = d_state[h]
            d_state[h] = pull_state(n, h, after)
            after_half = half(after)
            state, grad, update = state_ref[h, n], d_out[h, n], update_ref[h, n]
            sides = side_ref[h, n]
            d_update = half(base[h, n] + dot_nn(key_last, after_half))
            d_key_part = -dot_nt(d_update, state)
            read = dot_nt(grad, state)
            d_query = unit.carry * read
            d_carry = jnp.sum(read * unit.query, axis=1, keepdims=True)
            d_scores = dot_nt(grad, update)
            d_key_last = dot_nt(update, after_half)
            d_scale = jnp.sum(
                jnp.sum(after * state.astype(f32), axis=1, keepdims=True), axis=0, keepdims=True
            )
            d_sides = dot_tn(
                inv_ref[h, n], jnp.concatenate([d_update, half(d_key_part)], axis=1)
            )
            d_lower = -dot_nt(half(d_sides), half(sides))
            gram = dot_nt(key, key) * unit.weights
            pulled = d_lower * gram
            d_beta = jnp.sum(pulled, axis=1, keepdims=True)
            moved = unit.beta * pulled + d_scores * score_ref[h, n].astype(f32)
            d_gram = half(d_lower * (unit.beta * unit.weights))
            d_qk = half(d_scores * unit.factor)
            d_query = d_query + dot_nn(d_qk, key)
            d_key = dot_tn(d_qk, query) + dot_nn(d_gram, key) + dot_tn(d_gram, key)
            d_key = d_key + d_key_last * unit.last
            d_last = jnp.sum(d_key_last * unit.key_last, axis=1, keepdims=True)
            d_value_side, d_key_side = d_sides[:, :V], d_sides[:, V:]
            d_beta = d_beta + jnp.sum(d_value_side * unit.value, axis=1, keepdims=True)
            d_value = unit.beta * d_value_side
            mixed_side = jnp.sum(d_key_side * unit.key, axis=1, keepdims=True)
            d_key = d_key + (unit.beta * unit.carry) * d_key_side
            d_beta = d_beta + unit.carry * mixed_side
            d_carry = d_carry + unit.beta * mixed_side
            at_end = lax.broadcasted_iota(jnp.int32, (GROUP, 1), 0) == GROUP - 1
            d_carry = d_carry + jnp.where(at_end, d_scale, 0.0)
            d_cumul = d_carry * unit.carry - d_last
            d_cumul = d_cumul + jnp.where(
                at_end, jnp.sum(d_last, axis=0, keepdims=True), 0.0
            )
            d_cumul = d_cumul + jnp.sum(moved, axis=1, keepdims=True)
            d_row = jnp.sum(jnp.where(row == col, d_cumul, 0.0), axis=0, keepdims=True)
            d_row = d_row - jnp.sum(moved, axis=0, keepdims=True)
            d_decay = jnp.sum(jnp.where(col >= row, d_row, 0.0), axis=1, keepdims=True)
            d_decay_in = d_decay * unit.rate * jax.nn.sigmoid(unit.decay_in)
            log_sum = jnp.sum(d_decay * unit.decay, axis=0, keepdims=True)
            bias_sum = jnp.sum(d_decay_in, axis=0, keepdims=True)
            g_decay_ref[...] += jnp.where(lane == h, log_sum, 0.0) + jnp.where(
                lane == heads + h, bias_sum, 0.0
            )
            smalls.append((d_beta * unit.beta * (1.0 - unit.beta), d_decay_in))
            unscaled = unit.query * K**0.5
            d_query = d_query * K ** (-0.5)
            d_query = unit.query_root * (
                d_query - unscaled * jnp.sum(d_query * unscaled, axis=1, keepdims=True)
            )
            d_key = unit.key_root * (
                d_key - unit.key * jnp.sum(d_key * unit.key, axis=1, keepdims=True)
            )
            for part, given in enumerate((d_query, d_key, d_value)):
                start, size = unit.cols[part]
                sig, pre = unit.sigs[part], unit.pres[part]
                d_pre = given * sig * (1.0 + pre * (1.0 - sig))
                taps, spread = unit.taps[part], unit.padded[part]
                total = taps[0:1] * d_pre
                edge = jnp.zeros((RIM, size), f32)
                grads = [jnp.sum(d_pre * spread[RIM:], axis=0, keepdims=True)]
                whole = jnp.concatenate([edge, total], axis=0)
                for lag in range(1, CONV):
                    masked = d_pre * unit.ranges[lag - 1]
                    grads.append(
                        jnp.sum(
                            masked * pltpu.roll(spread, lag, 0)[RIM:], axis=0, keepdims=True
                        )
                    )
                    ext = jnp.concatenate([edge, taps[lag : lag + 1] * masked], axis=0)
                    whole = whole + pltpu.roll(ext, GROUP + RIM - lag, 0)
                for lag in range(CONV):
                    g_taps_ref[lag : lag + 1, start : start + size] += grads[lag]
                body = whole[RIM:]
                ended = body[GROUP - RIM :] + halo[:, start : start + size]
                halo[:, start : start + size] = whole[:RIM]
                body = jnp.concatenate([body[: GROUP - RIM], ended], axis=0)
                d_raw_ref[at, start : start + size] = half(body)

                @pl.when(step == 0)
                def _():
                    tail[:, start : start + size] = ended

        spot = lax.broadcasted_iota(jnp.int32, (GROUP, 2 * heads), 1)
        joined = jnp.zeros((GROUP, 2 * heads), f32)
        for h, (d_beta, d_decay_in) in enumerate(smalls):
            joined = joined + jnp.where(spot == h, d_beta, 0.0)
            joined = joined + jnp.where(spot == heads + h, d_decay_in, 0.0)
        d_raw_ref[at, mixed_cols + heads * V :] = half(joined)
        return carry

    lax.fori_loop(0, blocks, second, 0)
    rim = pltpu.make_async_remote_copy(
        src_ref=halo,
        dst_ref=rim_buf,
        send_sem=rim_sems.at[0],
        recv_sem=rim_sems.at[1],
        device_id=on_axis("fsdp", lax.rem(mine + fsdp_count - 1, fsdp_count)),
        device_id_type=MESH,
    )
    rim.start()
    for item, out in zip(sums, extra_outs):
        for d in range(1, item.outers):
            item.take_outer(d)
            out[...] = out[...] + item.stage2[d - 1].astype(f32)
    rim.wait()
    d_raw_ref[rows - RIM : rows, 0:mixed_cols] = half(tail[...] + rim_buf[...])
    for item in sums + [ring]:
        item.finish()


def mixer_grad_all(
    padded, gate, bd, taps, begins, rate, shift, norm, saved, pairs, d_mixer, extras, ident
):
    tp_count, fsdp_count = lax.axis_size("tp"), lax.axis_size("fsdp")
    heads = bd.shape[1] // 2
    rows = gate.shape[0]
    blocks = rows // GROUP
    mixed_cols = padded.shape[1]
    f32, bf16 = jnp.float32, jnp.bfloat16
    vmem = pl.BlockSpec(memory_space=pltpu.VMEM)
    smem = pl.BlockSpec(memory_space=pltpu.SMEM)
    dma = pltpu.SemaphoreType.DMA
    shape = jax.ShapeDtypeStruct
    outs = [
        shape((rows, mixed_cols + heads * V + 2 * heads), bf16),
        shape((CONV, mixed_cols), f32),
        shape((1, 128), f32),
        shape((1, V), f32),
    ] + [shape(extra.shape[1:], f32) for extra in extras]
    scratch = [
        pltpu.VMEM((heads, blocks, GROUP, V), bf16),
        pltpu.VMEM((heads, blocks, GROUP, V), f32),
        pltpu.VMEM((heads, blocks, K, V), f32),
        pltpu.VMEM((heads, K, V), f32),
        pltpu.VMEM((RIM, mixed_cols), f32),
        pltpu.VMEM((RIM, mixed_cols), f32),
        pltpu.VMEM((fsdp_count, heads * K, V), bf16),
        pltpu.VMEM((RIM, mixed_cols), f32),
        dma((2,)),
        dma((fsdp_count - 1,)),
        dma((fsdp_count,)),
    ]
    for extra in extras:
        scratch += scatter_scratch(fsdp_count, extra.shape[1], extra.shape[2], full=True)
    return pl.pallas_call(
        functools.partial(
            mixer_grad_kernel, heads, blocks, tp_count, fsdp_count, len(extras)
        ),
        out_shape=outs,
        in_specs=[vmem] * 5 + [smem] * 2 + [vmem] * (12 + len(extras)),
        out_specs=[vmem] * len(outs),
        scratch_shapes=scratch,
        compiler_params=comm_params(ident, 60),
        name="mixer_grad",
    )(padded, gate, bd, taps, begins, rate, shift, norm, *saved, pairs, d_mixer, *extras)


def shards(
    tokens,
    lengths,
    attn_gain,
    w_query,
    w_key,
    w_value,
    w_gate_out,
    w_beta,
    w_decay,
    conv_query,
    conv_key,
    conv_value,
    decay_log,
    decay_bias,
    out_gain,
    w_out,
    ffn_gain,
    w_ffn_gate,
    w_ffn_up,
    w_ffn_down,
    cotangent,
):
    count = lax.axis_size("fsdp")
    shard_rows = tokens.shape[0]
    query_cols, value_cols = w_query.shape[1], w_value.shape[1]
    hidden_cols = w_ffn_gate.shape[1]
    head_count = query_cols // K
    mixed_cols = 2 * query_cols + value_cols
    raw_cols = mixed_cols + value_cols

    tp_count = lax.axis_size("tp")
    width = tokens.shape[1]
    small_list = (attn_gain, ffn_gain, out_gain, conv_query, conv_key, conv_value)
    small = jnp.concatenate([part.astype(jnp.float32).reshape(-1) for part in small_list])
    small_width = -(-small.shape[0] // 1024) * 1024
    small = jnp.pad(small, (0, small_width - small.shape[0])).reshape(8, -1)
    mixer_own = jnp.concatenate(
        [w_query, w_key, w_value, w_gate_out, w_beta, w_decay], axis=1
    )
    token_rows, mixer_w, small = gather_all(
        [tokens, mixer_own, small], ["tp", "fsdp", "fsdp"], 0
    )
    small = small.reshape(count, -1)
    smalls, at = ([], 0)
    for part in small_list:
        piece = small[:, at : at + part.size]
        at = at + part.size
        if part.ndim == 3:
            piece = piece.reshape((count,) + part.shape).transpose(1, 2, 0, 3)
            smalls.append(piece.reshape(part.shape[0], part.shape[1], -1))
        else:
            smalls.append(piece.reshape(-1))
    gain_one, gain_two, norm_out, query_taps, key_taps, value_taps = smalls
    mixer_w = mixer_w.reshape(width, -1)
    token_rows = token_rows.reshape(-1, width).astype(jnp.float32)
    normed_one = rms_scale(token_rows, gain_one).astype(jnp.bfloat16)
    normed_blocks = normed_one.reshape(tp_count, shard_rows, width)
    row_count = normed_one.shape[0]
    positions = lax.axis_index("fsdp") * row_count + jnp.arange(row_count, dtype=jnp.int32)
    begins = seq_begin(lengths, positions)
    raw = mat_dot(normed_one, mixer_w)
    mixed_raw = raw[:, :mixed_cols].astype(jnp.bfloat16)
    gate_raw = raw[:, mixed_cols:raw_cols]
    bd_raw = raw[:, raw_cols:]
    taps = jnp.concatenate(
        [part.reshape(CONV, -1) for part in (query_taps, key_taps, value_taps)], axis=1
    )
    common = (
        gate_raw,
        bd_raw,
        taps,
        begins.reshape(-1, 1),
        -jnp.exp(decay_log),
        decay_bias,
        norm_out.reshape(1, -1),
    )
    normed_mixer, *saved, padded, pairs, cot_blocks, out_t, ffn_gate_w, ffn_up_w, down_t = (
        mixer_all(
            mixed_raw,
            *common,
            cotangent,
            [w_out.T, w_ffn_gate, w_ffn_up, w_ffn_down.T],
            1,
        )
    )
    out_t, ffn_gate_w, ffn_up_w, down_t = [
        part.reshape(width, -1) for part in (out_t, ffn_gate_w, ffn_up_w, down_t)
    ]
    (
        output,
        d_hidden,
        d_mixer,
        g_gate,
        g_up,
        g_down,
        g_out,
        gain_two_part,
    ) = ffn_all(
        normed_mixer.reshape(tp_count, shard_rows, -1),
        tokens,
        cotangent,
        out_t,
        gain_two.reshape(1, -1),
        cot_blocks,
        ffn_gate_w,
        ffn_up_w,
        down_t,
        2,
    )
    d_mixer = d_mixer.reshape(row_count, -1)
    gain_two_part = gain_two_part.reshape(-1)

    d_raw, g_taps, g_decay, norm_out_part, *grads_ffn = mixer_grad_all(
        padded,
        *common,
        saved,
        pairs,
        d_mixer,
        [part.reshape(count, width // count, -1) for part in (g_out, g_gate, g_up, g_down)],
        3,
    )
    grad_out_t, grad_w_ffn_gate, grad_w_ffn_up, grad_down_t = grads_ffn
    d_taps = [
        part.reshape(CONV, head_count, -1)
        for part in jnp.split(g_taps, (query_cols, 2 * query_cols), axis=1)
    ]
    decay_pair = g_decay[0, : 2 * head_count]

    def spread(taps):
        taps = taps.reshape(taps.shape[0], taps.shape[1], count, -1)
        return taps.transpose(2, 0, 1, 3).reshape(count, -1)

    small_parts = [
        gain_two_part.reshape(count, -1),
        norm_out_part.reshape(count, -1),
        spread(d_taps[0]),
        spread(d_taps[1]),
        spread(d_taps[2]),
        jnp.broadcast_to(decay_pair[None, :], (count, decay_pair.shape[0])),
    ]
    small_cat = jnp.concatenate(small_parts, axis=1)
    lanes = -(-max(small_cat.shape[1], 7 * (width // count)) // (7 * 128)) * 128
    small_cat = jnp.pad(small_cat, ((0, 0), (lanes, 7 * lanes - small_cat.shape[1])))
    d_tokens, grad_mixer_w, small_own, small_all = last_all(
        d_raw.reshape(tp_count, shard_rows, -1),
        mixer_w,
        normed_blocks,
        tokens,
        gain_one.reshape(1, -1),
        d_hidden,
        small_cat.reshape(count, 8, lanes),
        [],
        4,
    )
    grad_w_ffn_down = grad_down_t.T
    grad_w_out = grad_out_t.T
    cuts = (
        query_cols,
        2 * query_cols,
        mixed_cols,
        raw_cols,
        raw_cols + head_count,
    )
    grads_w = jnp.split(grad_mixer_w, cuts, axis=1)
    small_cuts, at = ([], lanes)
    for part in small_parts:
        small_cuts.append(at)
        at = at + part.shape[1]
    small_cuts.append(at)
    own_parts = jnp.split(small_own.reshape(-1), small_cuts)
    all_parts = jnp.split(small_all.reshape(-1), small_cuts)
    small_out = [
        small_all[0, : width // count],
        all_parts[1],
        all_parts[2],
        own_parts[3],
        own_parts[4],
        own_parts[5],
        own_parts[6],
    ]
    return (
        output,
        d_tokens,
        small_out[0],
        *grads_w,
        small_out[3].reshape(conv_query.shape),
        small_out[4].reshape(conv_key.shape),
        small_out[5].reshape(conv_value.shape),
        small_out[6][:head_count],
        small_out[6][head_count:],
        small_out[2],
        grad_w_out,
        small_out[1],
        grad_w_ffn_gate,
        grad_w_ffn_up,
        grad_w_ffn_down,
    )


def solution(mesh):
    placed = (
        P(("fsdp", "tp"), None),
        P(),
        P("fsdp"),
        P("fsdp", "tp"),
        P("fsdp", "tp"),
        P("fsdp", "tp"),
        P("fsdp", "tp"),
        P("fsdp", "tp"),
        P("fsdp", "tp"),
        P(None, "tp", "fsdp"),
        P(None, "tp", "fsdp"),
        P(None, "tp", "fsdp"),
        P("tp"),
        P("tp"),
        P("fsdp"),
        P("tp", "fsdp"),
        P("fsdp"),
        P("fsdp", "tp"),
        P("fsdp", "tp"),
        P("tp", "fsdp"),
        P(("fsdp", "tp"), None),
    )
    return jax.shard_map(
        shards,
        mesh=mesh,
        in_specs=placed,
        out_specs=(
            P(("fsdp", "tp"), None),
            P(("fsdp", "tp"), None),
            P("fsdp"),
            P("fsdp", "tp"),
            P("fsdp", "tp"),
            P("fsdp", "tp"),
            P("fsdp", "tp"),
            P("fsdp", "tp"),
            P("fsdp", "tp"),
            P(None, "tp", "fsdp"),
            P(None, "tp", "fsdp"),
            P(None, "tp", "fsdp"),
            P("tp"),
            P("tp"),
            P("fsdp"),
            P("tp", "fsdp"),
            P("fsdp"),
            P("fsdp", "tp"),
            P("fsdp", "tp"),
            P("tp", "fsdp"),
        ),
        check_vma=False,
    )
```

```python
import functools

import jax
import jax.numpy as jnp
from jax import lax
from jax.experimental import pallas as pl
from jax.experimental.pallas import tpu as pltpu
from jax.sharding import PartitionSpec as P

K = 128
V = 256
CONV = 4
GROUP = 128
MAXLEN = 4096
RIM = 16


def mat_dot(left, right):
    return jnp.dot(left, right, preferred_element_type=jnp.float32)


def rms_scale(values, scale_gain):
    return (
        values * lax.rsqrt(jnp.mean(values * values, axis=-1, keepdims=True) + 1e-06) * scale_gain
    )


def seq_begin(lengths, positions):
    number = lengths.shape[0]
    earlier = jnp.arange(number)[None, :] < jnp.arange(number)[:, None]
    offsets = jnp.sum(jnp.where(earlier, lengths[None, :], 0), axis=1)
    chosen = jnp.where(offsets[None, :] <= positions[:, None], offsets[None, :], 0)
    return jnp.max(chosen, axis=1)


MESH = pl.DeviceIdType.MESH
INNER = 2


def on_axis(axis, index):
    return {axis: index}


def halves(axis):
    me = lax.axis_index(axis)
    return me, lax.div(me, INNER), lax.rem(me, INNER)


def entry_barrier(axes, everyone=False):
    barrier = pltpu.get_barrier_semaphore()
    total = 0
    for axis, count in axes:
        me, outer, inner = halves(axis)
        outers = count // INNER
        peers = [outer * INNER + (1 - inner)]
        for d in range(1, outers):
            peers.append(lax.rem(outer + d, outers) * INNER + inner)
        if everyone:
            peers = [lax.rem(me + d, count) for d in range(1, count)]
        for peer in peers:
            pl.semaphore_signal(
                barrier, inc=1, device_id=on_axis(axis, peer), device_id_type=MESH
            )
        total += len(peers)
    pl.semaphore_wait(barrier, total)


class Gather:
    def __init__(self, axis, count, buf, send, recv, own=None, part=None):
        self.axis, self.count, self.buf, self.send, self.recv = axis, count, buf, send, recv
        self.outers = count // INNER
        self.me, self.outer, self.inner = halves(axis)
        self.part = part
        if own is None:
            self.own = self.slot(self.me)
        else:
            self.own = own if part is None else own.at[pl.ds(*part)]

    def slot(self, index):
        if self.part is None:
            return self.buf.at[index]
        return self.buf.at[index, pl.ds(*self.part)]

    def block(self, d, across):
        outer = lax.rem(self.outer + self.outers - d, self.outers)
        return outer * INNER + ((1 - self.inner) if across else self.inner)

    def copy(self, d, forward):
        across = self.outer * INNER + 1 - self.inner
        if forward:
            index = self.block(d, False)
            src, target, sem = self.slot(index), across, self.outers - 1 + d
        else:
            index, src = self.me, self.own
            target = across
            if d:
                target = lax.rem(self.outer + d, self.outers) * INNER + self.inner
            sem = d
        return pltpu.make_async_remote_copy(
            src_ref=src,
            dst_ref=self.slot(index),
            send_sem=self.send.at[sem],
            recv_sem=self.recv.at[index],
            device_id=on_axis(self.axis, target),
            device_id_type=MESH,
        )

    def start(self):
        for d in list(range(1, self.outers)) + [0]:
            self.copy(d, False).start()

    def arrive(self, index):
        pltpu.make_async_remote_copy(
            src_ref=self.slot(index),
            dst_ref=self.slot(index),
            send_sem=self.send.at[0],
            recv_sem=self.recv.at[index],
            device_id=on_axis(self.axis, self.outer * INNER + 1 - self.inner),
            device_id_type=MESH,
        ).wait_recv()

    def forward(self, d):
        index = self.block(d, False)
        self.arrive(index)
        self.copy(d, True).start()
        return index

    def forward_all(self):
        for d in range(1, self.outers):
            self.forward(d)

    def arrive_all(self):
        for d in range(self.outers):
            self.arrive(self.block(d, True))

    def finish(self):
        for d in range(self.outers):
            self.copy(d, False).wait_send()
        for d in range(1, self.outers):
            self.copy(d, True).wait_send()


class Scatter:
    def __init__(self, axis, count, out, stage, send2, stage2, sems, full=None, part=None):
        self.axis, self.count, self.full, self.part = axis, count, full, part
        self.outers = count // INNER
        self.me, self.outer, self.inner = halves(axis)
        self.out, self.stage, self.send2, self.stage2 = out, stage, send2, stage2
        self.send_a, self.recv_a, self.send_b, self.recv_b = sems

    def target(self, d, across):
        outer = lax.rem(self.outer + d, self.outers)
        return outer * INNER + ((1 - self.inner) if across else self.inner)

    def own(self, d):
        if self.part is None:
            return self.full[self.target(d, False)].astype(jnp.float32)
        return self.full[self.target(d, False), pl.ds(*self.part)].astype(jnp.float32)

    def first(self, d):
        if self.full is None:
            src = self.out.at[d]
        elif self.part is None:
            src = self.full.at[self.target(d, True)]
        else:
            src = self.full.at[self.target(d, True), pl.ds(*self.part)]
        return pltpu.make_async_remote_copy(
            src_ref=src,
            dst_ref=self.stage.at[d],
            send_sem=self.send_a.at[d],
            recv_sem=self.recv_a.at[d],
            device_id=on_axis(self.axis, self.outer * INNER + 1 - self.inner),
            device_id_type=MESH,
        )

    def second(self, d):
        return pltpu.make_async_remote_copy(
            src_ref=self.send2.at[d - 1],
            dst_ref=self.stage2.at[d - 1],
            send_sem=self.send_b.at[d - 1],
            recv_sem=self.recv_b.at[d - 1],
            device_id=on_axis(self.axis, self.target(d, False)),
            device_id_type=MESH,
        )

    def send_across(self, d):
        self.first(d).start()

    def take_across(self, d):
        self.first(d).wait_recv()

    def send_outer(self, d):
        self.second(d).start()

    def take_outer(self, d):
        self.second(d).wait_recv()

    def order(self):
        return list(range(1, self.outers)) + [0]

    def start(self):
        for d in self.order():
            self.send_across(d)

    def turn(self, out):
        for d in self.order():
            self.take_across(d)
            total = self.own(d) + self.stage[d].astype(jnp.float32)
            if d:
                self.send2[d - 1] = total.astype(jnp.bfloat16)
                self.send_outer(d)
            else:
                self.write(out, total, False)

    def write(self, out, total, add):
        at = pl.ds(0, out.shape[0]) if self.part is None else pl.ds(*self.part)
        out[at, :] = (out[at, :] + total) if add else total

    def close(self, out):
        total = None
        for d in range(1, self.outers):
            self.take_outer(d)
            piece = self.stage2[d - 1].astype(jnp.float32)
            total = piece if total is None else total + piece
        if total is not None:
            self.write(out, total, True)

    def finish(self):
        for d in range(self.outers):
            self.first(d).wait_send()
        for d in range(1, self.outers):
            self.second(d).wait_send()


def parts_of(rows, pieces):
    size = rows // pieces
    if rows % pieces or size % 16:
        return [None]
    return [(at * size, size) for at in range(pieces)]


def scatter_scratch(count, rows, cols, dtype=jnp.bfloat16, full=False):
    outers = count // INNER
    own = [] if full else [pltpu.VMEM((outers, rows, cols), dtype)]
    return own + [
        pltpu.VMEM((outers, rows, cols), dtype),
        pltpu.VMEM((max(outers - 1, 1), rows, cols), dtype),
        pltpu.VMEM((max(outers - 1, 1), rows, cols), dtype),
        pltpu.SemaphoreType.DMA((outers,)),
        pltpu.SemaphoreType.DMA((outers,)),
        pltpu.SemaphoreType.DMA((max(outers - 1, 1),)),
        pltpu.SemaphoreType.DMA((max(outers - 1, 1),)),
    ]


def comm_params(ident, vmem_mb):
    return pltpu.CompilerParams(
        collective_id=ident, has_side_effects=True, vmem_limit_bytes=vmem_mb * 2**20
    )


def front_kernel(tp_count, fsdp_count, number, splits, *refs):
    bf16, f32 = jnp.bfloat16, jnp.float32
    refs = list(refs)

    def take(count):
        out = refs[:count]
        del refs[:count]
        return out

    tok_any, small_any = take(2)
    shards = take(number)
    n1_ref, small_ref = take(2)
    wholes = take(number)
    mixed_ref, gate_ref = take(2)
    tok_rows, gain_ref, local_sems = take(3)
    pieces = [take(2) for _ in range(2 + sum(len(split) for split in splits))]
    me_tp, me = lax.axis_index("tp"), lax.axis_index("fsdp")
    locals_ = [
        pltpu.make_async_copy(src, dst, local_sems.at[k])
        for k, (src, dst) in enumerate(
            [(tok_any, tok_rows.at[me_tp]), (small_any, small_ref.at[me])]
            + [(shard, whole.at[me]) for shard, whole in zip(shards, wholes)]
        )
    ]
    for copy in locals_:
        copy.start()
    entry_barrier([("fsdp", fsdp_count), ("tp", tp_count)])
    tok = Gather("tp", tp_count, tok_rows, pieces[0][0], pieces[0][1], own=tok_any)
    small = Gather("fsdp", fsdp_count, small_ref, pieces[1][0], pieces[1][1], own=small_any)
    groups, at = [], 2
    for shard, whole, split in zip(shards, wholes, splits):
        group = []
        for part in split:
            sems = pieces[at]
            at += 1
            group.append(
                Gather("fsdp", fsdp_count, whole, sems[0], sems[1], own=shard, part=part)
            )
        groups.append(group)
    items = [item for group in groups for item in group]
    depth = 3
    small.start()
    tok.start()
    for item in items[:depth]:
        item.start()
    small.forward_all()
    tok.forward_all()

    def pump(k):
        items[k].forward_all()
        if k + depth < len(items):
            items[k + depth].start()

    pumped = 0
    pump(0)
    pumped = 1
    small.arrive_all()
    tok.arrive_all()
    for copy in locals_:
        copy.wait()
    width = n1_ref.shape[2]
    share = width // fsdp_count
    for f in range(fsdp_count):
        gain_ref[0:1, f * share : (f + 1) * share] = small_ref[f, 0:1, 0:share]
    for b in range(tp_count):
        rows = tok_rows[b].astype(f32)
        root = lax.rsqrt(jnp.mean(rows * rows, axis=-1, keepdims=True) + 1e-06)
        n1_ref[b] = (rows * root * gain_ref[...]).astype(bf16)
        if b % 2 and pumped < len(items):
            pump(pumped)
            pumped += 1
    column = 0
    tall = tok_rows.shape[1]
    for k, (group, whole) in enumerate(zip(groups, wholes)):
        ahead = sum(len(part) for part in groups[: k + 2])
        while pumped < ahead:
            pump(pumped)
            pumped += 1
        for item in group:
            item.arrive_all()
        weight = whole[...].reshape(width, whole.shape[2])
        cols = whole.shape[2]
        for b in range(tp_count):
            product = dot_nn(n1_ref[b], weight)
            rows = pl.ds(b * tall, tall)
            if k + 1 < number:
                mixed_ref[rows, column : column + cols] = product.astype(bf16)
            else:
                gate_ref[rows, :] = product
        column += cols
    for item in [small, tok] + items:
        item.finish()


def front_all(tokens, small, shards, ident):
    tp_count, fsdp_count = lax.axis_size("tp"), lax.axis_size("fsdp")
    rows, width = tokens.shape
    f32, bf16 = jnp.float32, jnp.bfloat16
    shape = jax.ShapeDtypeStruct
    dma = pltpu.SemaphoreType.DMA
    vmem = pl.BlockSpec(memory_space=pltpu.VMEM)
    splits = [
        parts_of(shard.shape[0], 2 if shard.shape[1] > 2 * K else 1) for shard in shards
    ]
    mixed_cols = sum(shard.shape[1] for shard in shards[:-1])
    outs = (
        [
            shape((tp_count, rows, width), bf16),
            shape((fsdp_count,) + small.shape, f32),
        ]
        + [shape((fsdp_count,) + shard.shape, bf16) for shard in shards]
        + [
            shape((tp_count * rows, mixed_cols), bf16),
            shape((tp_count * rows, shards[-1].shape[1]), f32),
        ]
    )
    scratch = [
        pltpu.VMEM((tp_count, rows, width), bf16),
        pltpu.VMEM((1, width), f32),
        dma((2 + len(shards),)),
        dma((tp_count - 1,)),
        dma((tp_count,)),
    ]
    for _ in range(1 + sum(len(split) for split in splits)):
        scratch += [dma((fsdp_count - 1,)), dma((fsdp_count,))]
    return pl.pallas_call(
        functools.partial(front_kernel, tp_count, fsdp_count, len(shards), splits),
        out_shape=outs,
        in_specs=[pl.BlockSpec(memory_space=pl.ANY)] * (2 + len(shards)),
        out_specs=[vmem] * len(outs),
        scratch_shapes=scratch,
        compiler_params=comm_params(ident, 48),
        name="front",
    )(tokens, small, *shards)


def dot_nn(left, right):
    return lax.dot_general(
        left, right, (((1,), (0,)), ((), ())), preferred_element_type=jnp.float32
    )


def dot_nt(left, right):
    return lax.dot_general(
        left, right, (((1,), (1,)), ((), ())), preferred_element_type=jnp.float32
    )


def dot_tn(left, right):
    return lax.dot_general(
        left, right, (((0,), (0,)), ((), ())), preferred_element_type=jnp.float32
    )


def ffn_kernel(
    count,
    nm_ref,
    tok_ref,
    cot_ref,
    out_w_ref,
    gain_ref,
    cot_any,
    gate_any,
    up_any,
    down_any,
    output_ref,
    d_hidden_ref,
    d_mixer_ref,
    g_gate_ref,
    g_up_ref,
    g_down_ref,
    g_out_ref,
    g_gain_ref,
    cot_rows,
    gate_w,
    up_w,
    down_w,
    n2,
    dh,
    act_s,
    dgate_s,
    dup_s,
    hidden_s,
    dact_s,
    load_sem,
    n2_send,
    n2_recv,
    dh_send,
    dh_recv,
    *scatters,
):
    bf16, f32 = jnp.bfloat16, jnp.float32
    loads = [
        pltpu.make_async_copy(src, dst, load_sem.at[k])
        for k, (src, dst) in enumerate(
            ((cot_any, cot_rows), (down_any, down_w), (gate_any, gate_w), (up_any, up_w))
        )
    ]
    for load in loads:
        load.start()
    entry_barrier([("tp", count)])
    outers = count // INNER
    sets = [scatters[8 * k : 8 * k + 8] for k in range(3)]
    mix_s, dn_s, ffn_s = [
        Scatter("tp", count, s[0], s[1], s[2], s[3], s[4:]) for s in sets
    ]
    order = list(range(1, outers)) + [0]

    for d in order:
        mix_s.out[d] = dot_nt(nm_ref[mix_s.target(d, True)], out_w_ref[...]).astype(bf16)
        mix_s.send_across(d)
    for d in order:
        part = dot_nt(nm_ref[mix_s.target(d, False)], out_w_ref[...])
        mix_s.take_across(d)
        if d:
            mix_s.send2[d - 1] = (part + mix_s.stage[d].astype(f32)).astype(bf16)
            mix_s.send_outer(d)
        else:
            hidden_s[...] = part + mix_s.stage[0].astype(f32) + tok_ref[...].astype(f32)
    loads[0].wait()
    loads[1].wait()
    for b in range(count):
        dact_s[b] = dot_nn(cot_rows[b], down_w[...])
    total = hidden_s[...]
    for d in range(1, outers):
        mix_s.take_outer(d)
        total = total + mix_s.stage2[d - 1].astype(f32)
    hidden_s[...] = total
    root = lax.rsqrt(jnp.mean(total * total, axis=-1, keepdims=True) + 1e-06)
    me = mix_s.me
    n2[me] = (total * root * gain_ref[...]).astype(bf16)
    gather = Gather("tp", count, n2, n2_send, n2_recv)
    gather.start()
    loads[2].wait()
    loads[3].wait()

    def block_ffn(b):
        rows = n2[b]
        gate_pre = dot_nn(rows, gate_w[...])
        up_pre = dot_nn(rows, up_w[...])
        sig = jax.nn.sigmoid(gate_pre)
        silu = gate_pre * sig
        d_active = dact_s[b]
        d_gate = (d_active * up_pre * (sig + silu * (1.0 - sig))).astype(bf16)
        d_up = (d_active * silu).astype(bf16)
        dgate_s[b] = d_gate
        dup_s[b] = d_up
        act_s[b] = (silu * up_pre).astype(bf16)
        return dot_nt(d_gate, gate_w[...]) + dot_nt(d_up, up_w[...])

    own_part = block_ffn(me)
    hold = {0: own_part}
    across = gather.block(0, True)
    gather.arrive(across)
    dn_s.out[0] = block_ffn(across).astype(bf16)
    dn_s.send_across(0)
    for d in range(1, outers):
        gather.forward(d)
    for d in range(1, outers):
        index = gather.block(d, True)
        gather.arrive(index)
        back = outers - d
        dn_s.out[back] = block_ffn(index).astype(bf16)
        dn_s.send_across(back)
    for d in range(1, outers):
        index = gather.block(d, False)
        back = outers - d
        part = block_ffn(index)
        dn_s.take_across(back)
        dn_s.send2[back - 1] = (part + dn_s.stage[back].astype(f32)).astype(bf16)
        dn_s.send_outer(back)
    for d in order:
        b = ffn_s.target(d, True)
        ffn_s.out[d] = dot_nt(act_s[b], down_w[...]).astype(bf16)
        ffn_s.send_across(d)
    g_cols = 256

    def down_grad(k, carry):
        cols = pl.ds(pl.multiple_of(k * g_cols, g_cols), g_cols)
        total = dot_tn(cot_rows[0, :, cols], act_s[0])
        for b in range(1, count):
            total = total + dot_tn(cot_rows[b, :, cols], act_s[b])
        g_down_ref[cols, :] = total.astype(bf16)
        return carry

    width = n2.shape[2]
    lax.fori_loop(0, width // g_cols, down_grad, 0)
    dn_s.take_across(0)
    d_norm = own_part + dn_s.stage[0].astype(f32)
    for d in range(1, outers):
        dn_s.take_outer(d)
        d_norm = d_norm + dn_s.stage2[d - 1].astype(f32)
    hidden = hidden_s[...]
    root = lax.rsqrt(jnp.mean(hidden * hidden, axis=-1, keepdims=True) + 1e-06)
    scaled = hidden * root
    g_gain_ref[...] = jnp.sum(d_norm * scaled, axis=0, keepdims=True)
    pulled = d_norm * gain_ref[...]
    d_hidden = cot_ref[...].astype(f32) + root * (
        pulled - scaled * jnp.mean(pulled * scaled, axis=-1, keepdims=True)
    )
    d_hidden_ref[...] = d_hidden
    dh[me] = d_hidden.astype(bf16)
    gather2 = Gather("tp", count, dh, dh_send, dh_recv)
    gather2.start()
    for d in order:
        part = dot_nt(act_s[ffn_s.target(d, False)], down_w[...])
        ffn_s.take_across(d)
        if d:
            ffn_s.send2[d - 1] = (part + ffn_s.stage[d].astype(f32)).astype(bf16)
            ffn_s.send_outer(d)
        else:
            output_ref[...] = hidden_s[...] + part + ffn_s.stage[0].astype(f32)

    def gate_grad(k, carry):
        cols = pl.ds(pl.multiple_of(k * g_cols, g_cols), g_cols)
        gate_total = dot_tn(n2[0, :, cols], dgate_s[0])
        up_total = dot_tn(n2[0, :, cols], dup_s[0])
        for b in range(1, count):
            gate_total = gate_total + dot_tn(n2[b, :, cols], dgate_s[b])
            up_total = up_total + dot_tn(n2[b, :, cols], dup_s[b])
        g_gate_ref[cols, :] = gate_total.astype(bf16)
        g_up_ref[cols, :] = up_total.astype(bf16)
        return carry

    lax.fori_loop(0, width // g_cols, gate_grad, 0)
    for d in range(1, outers):
        gather2.forward(d)
    for d in range(outers):
        gather2.arrive(gather2.block(d, True))
    for b in range(count):
        d_mixer_ref[b] = dot_nn(dh[b], out_w_ref[...])

    def out_grad(k, carry):
        cols = pl.ds(pl.multiple_of(k * g_cols, g_cols), g_cols)
        total = dot_tn(dh[0, :, cols], nm_ref[0])
        for b in range(1, count):
            total = total + dot_tn(dh[b, :, cols], nm_ref[b])
        g_out_ref[cols, :] = total.astype(bf16)
        return carry

    lax.fori_loop(0, width // g_cols, out_grad, 0)
    for d in range(1, outers):
        ffn_s.take_outer(d)
        output_ref[...] = output_ref[...] + ffn_s.stage2[d - 1].astype(f32)
    for part in (mix_s, gather, dn_s, ffn_s, gather2):
        part.finish()


def ffn_all(nm, tokens, cotangent, out_w, gain, cot_rows, gate_w, up_w, down_w, ident):
    count = lax.axis_size("tp")
    rows, width = tokens.shape
    hidden = gate_w.shape[1]
    values = out_w.shape[1]
    f32, bf16 = jnp.float32, jnp.bfloat16
    vmem = pl.BlockSpec(memory_space=pltpu.VMEM)
    anys = pl.BlockSpec(memory_space=pl.ANY)
    dma = pltpu.SemaphoreType.DMA
    outs = [
        jax.ShapeDtypeStruct((rows, width), f32),
        jax.ShapeDtypeStruct((rows, width), f32),
        jax.ShapeDtypeStruct((count, rows, values), f32),
        jax.ShapeDtypeStruct((width, hidden), bf16),
        jax.ShapeDtypeStruct((width, hidden), bf16),
        jax.ShapeDtypeStruct((width, hidden), bf16),
        jax.ShapeDtypeStruct((width, values), bf16),
        jax.ShapeDtypeStruct((1, width), f32),
    ]
    scratch = [
        pltpu.VMEM((count, rows, width), bf16),
        pltpu.VMEM((width, hidden), bf16),
        pltpu.VMEM((width, hidden), bf16),
        pltpu.VMEM((width, hidden), bf16),
        pltpu.VMEM((count, rows, width), bf16),
        pltpu.VMEM((count, rows, width), bf16),
        pltpu.VMEM((count, rows, hidden), bf16),
        pltpu.VMEM((count, rows, hidden), bf16),
        pltpu.VMEM((count, rows, hidden), bf16),
        pltpu.VMEM((rows, width), f32),
        pltpu.VMEM((count, rows, hidden), f32),
        dma((4,)),
        dma((count - 1,)),
        dma((count,)),
        dma((count - 1,)),
        dma((count,)),
    ]
    for _ in range(3):
        scratch += scatter_scratch(count, rows, width)
    return pl.pallas_call(
        functools.partial(ffn_kernel, count),
        out_shape=outs,
        in_specs=[vmem] * 5 + [anys] * 4,
        out_specs=[vmem] * len(outs),
        scratch_shapes=scratch,
        compiler_params=comm_params(ident, 58),
        name="ffn",
    )(nm, tokens, cotangent, out_w, gain, cot_rows, gate_w, up_w, down_w)


def exchange_small(axis, count, src, buf, send, recv, spread):
    me = lax.axis_index(axis)
    copies = []
    for d in range(1, count):
        peer = lax.rem(me + d, count)
        copy = pltpu.make_async_remote_copy(
            src_ref=src.at[peer] if spread else src,
            dst_ref=buf.at[d - 1],
            send_sem=send.at[d - 1],
            recv_sem=recv.at[d - 1],
            device_id=on_axis(axis, peer),
            device_id_type=MESH,
        )
        copy.start()
        copies.append(copy)
    return copies


def last_kernel(tp_count, fsdp_count, widths, *refs):
    bf16, f32 = jnp.bfloat16, jnp.float32
    refs = list(refs)

    def take(number):
        out = refs[:number]
        del refs[:number]
        return out

    number = len(widths)
    d_raw_ref, n1_ref, tok_ref, gain_ref, d_hidden_ref, small_ref = take(6)
    weights = take(number)
    d_tok_ref, small_own_ref, small_all_ref = take(3)
    outs = take(number)
    small_send, small_buf, small_buf2 = take(3)
    small_sems = take(4)
    dn = take(8)
    fulls = take(number)
    sets = [take(7) for _ in range(number)]
    entry_barrier([("fsdp", fsdp_count), ("tp", tp_count)], everyone=True)
    dn_s = Scatter("tp", tp_count, dn[0], dn[1], dn[2], dn[3], dn[4:])
    sums = [
        Scatter("fsdp", fsdp_count, None, s[0], s[1], s[2], s[3:], full=full)
        for s, full in zip(sets, fulls)
    ]
    width = n1_ref.shape[2]
    depth = width // fsdp_count
    chunk = max(256, depth)
    per = chunk // depth
    starts = [sum(widths[:k]) for k in range(number)]

    def weight_grad(item):
        full, at, size = fulls[item], starts[item], widths[item]

        def step(k, carry):
            cols = pl.ds(pl.multiple_of(k * chunk, chunk), chunk)
            total = dot_tn(n1_ref[0, :, cols], d_raw_ref[0, :, at : at + size])
            for b in range(1, tp_count):
                total = total + dot_tn(n1_ref[b, :, cols], d_raw_ref[b, :, at : at + size])
            for j in range(per):
                full[k * per + j] = total[j * depth : (j + 1) * depth].astype(bf16)
            return carry

        lax.fori_loop(0, width // chunk, step, 0)

    def input_grad(b):
        total = None
        for item in range(number):
            at, size = starts[item], widths[item]
            weight = weights[item][...].reshape(width, size)
            piece = dot_nt(d_raw_ref[b, :, at : at + size], weight)
            total = piece if total is None else total + piece
        return total

    turns = list(reversed(range(number)))
    weight_grad(turns[0])
    sums[turns[0]].start()
    for d in dn_s.order():
        dn_s.out[d] = input_grad(dn_s.target(d, True)).astype(bf16)
        dn_s.send_across(d)
    weight_grad(turns[1])
    sums[turns[1]].start()
    held = None
    for d in dn_s.order():
        part = input_grad(dn_s.target(d, False))
        dn_s.take_across(d)
        if d:
            dn_s.send2[d - 1] = (part + dn_s.stage[d].astype(f32)).astype(bf16)
            dn_s.send_outer(d)
        else:
            held = part + dn_s.stage[0].astype(f32)
    d_tok_ref[...] = held
    sums[turns[0]].turn(outs[turns[0]])
    for k in range(2, number):
        weight_grad(turns[k])
        sums[turns[k]].start()
        sums[turns[k - 1]].turn(outs[turns[k - 1]])
    held = d_tok_ref[...]
    for d in range(1, dn_s.outers):
        dn_s.take_outer(d)
        held = held + dn_s.stage2[d - 1].astype(f32)
    tokens = tok_ref[...].astype(f32)
    root = lax.rsqrt(jnp.mean(tokens * tokens, axis=-1, keepdims=True) + 1e-06)
    scaled = tokens * root
    gain_part = jnp.sum(held * scaled, axis=0, keepdims=True)
    pulled = held * gain_ref[...]
    d_tok_ref[...] = d_hidden_ref[...] + root * (
        pulled - scaled * jnp.mean(pulled * scaled, axis=-1, keepdims=True)
    )
    small_send[...] = small_ref[...]
    for f in range(fsdp_count):
        small_send[f, 0:1, 0:depth] = gain_part[:, f * depth : (f + 1) * depth]
    copies = exchange_small(
        "fsdp", fsdp_count, small_send, small_buf, small_sems[0], small_sems[1], True
    )
    sums[turns[-1]].turn(outs[turns[-1]])
    small_sum = small_send[lax.axis_index("fsdp")]
    for d, copy in enumerate(copies):
        copy.wait_recv()
        small_sum = small_sum + small_buf[d]
    small_own_ref[...] = small_sum
    copies2 = exchange_small(
        "tp", tp_count, small_own_ref, small_buf2, small_sems[2], small_sems[3], False
    )
    for k in turns:
        sums[k].close(outs[k])
    for d, copy in enumerate(copies2):
        copy.wait_recv()
        small_sum = small_sum + small_buf2[d]
    small_all_ref[...] = small_sum
    for copy in copies + copies2:
        copy.wait_send()
    for item in [dn_s] + sums:
        item.finish()


def last_all(d_raw, n1, tokens, gain, d_hidden, small, weights, ident):
    tp_count, fsdp_count = lax.axis_size("tp"), lax.axis_size("fsdp")
    rows, width = tokens.shape
    widths = [weight.shape[2] for weight in weights]
    depth = width // fsdp_count
    f32, bf16 = jnp.float32, jnp.bfloat16
    vmem = pl.BlockSpec(memory_space=pltpu.VMEM)
    dma = pltpu.SemaphoreType.DMA
    outs = [
        jax.ShapeDtypeStruct((rows, width), f32),
        jax.ShapeDtypeStruct(small.shape[1:], f32),
        jax.ShapeDtypeStruct(small.shape[1:], f32),
    ] + [jax.ShapeDtypeStruct((depth, size), f32) for size in widths]
    scratch = [
        pltpu.VMEM(small.shape, f32),
        pltpu.VMEM((fsdp_count - 1,) + small.shape[1:], f32),
        pltpu.VMEM((tp_count - 1,) + small.shape[1:], f32),
        dma((fsdp_count - 1,)),
        dma((fsdp_count - 1,)),
        dma((tp_count - 1,)),
        dma((tp_count - 1,)),
    ]
    scratch += scatter_scratch(tp_count, rows, width)
    scratch += [pltpu.VMEM((fsdp_count, depth, size), bf16) for size in widths]
    for size in widths:
        scratch += scatter_scratch(fsdp_count, depth, size, full=True)
    return pl.pallas_call(
        functools.partial(last_kernel, tp_count, fsdp_count, widths),
        out_shape=outs,
        in_specs=[vmem] * (6 + len(weights)),
        out_specs=[vmem] * len(outs),
        scratch_shapes=scratch,
        compiler_params=comm_params(ident, 58),
        name="last",
    )(d_raw, n1, tokens, gain, d_hidden, small, *weights)


def split_two(value):
    top = value.astype(jnp.bfloat16)
    return top, (value - top.astype(jnp.float32)).astype(jnp.bfloat16)


def dot_three(left, right, dot):
    (a, b), (c, d) = split_two(left), split_two(right)
    return dot(a, c) + (dot(a, d) + dot(b, c))


def half(value):
    return value.astype(jnp.bfloat16)


def triangles():
    row = lax.broadcasted_iota(jnp.int32, (GROUP, GROUP), 0)
    col = lax.broadcasted_iota(jnp.int32, (GROUP, GROUP), 1)
    return row, col


def pair_mask(row, col, step):
    shift = step.bit_length() - 1
    high_row, high_col = row >> shift, col >> shift
    return ((high_row >> 1) == (high_col >> 1)) & (high_row > high_col)


def unit_inverses(lowers):
    row, col = triangles()
    eye = (row == col).astype(jnp.float32)
    mask = pair_mask(row, col, 1)
    inverses = [eye - jnp.where(mask, lower, 0.0) for lower in lowers]
    step = 2
    while step < GROUP:
        mask = pair_mask(row, col, step)
        corners = [half(jnp.where(mask, lower, 0.0)) for lower in lowers]
        tops = [half(inverse) for inverse in inverses]
        inner = [half(dot_nn(top, corner)) for top, corner in zip(tops, corners)]
        inverses = [
            inverse - dot_nn(left, top) for inverse, left, top in zip(inverses, inner, tops)
        ]
        step = step * 2
    rest = [
        eye - inverse - dot_three(lower, inverse, dot_nn)
        for inverse, lower in zip(inverses, lowers)
    ]
    return [
        inverse + dot_nn(half(inverse), half(gap)) for inverse, gap in zip(inverses, rest)
    ]


def conv_rows(padded, taps, ranges):
    rim = padded.shape[0] - GROUP
    total = taps[0:1] * padded[rim:]
    for lag in range(1, CONV):
        total = total + taps[lag : lag + 1] * (
            pltpu.roll(padded, lag, 0)[rim:] * ranges[lag - 1]
        )
    return total


def unit_norm(values):
    return lax.rsqrt(jnp.sum(values * values, axis=-1, keepdims=True) + 1e-06)


def soft_plus(value):
    return jnp.maximum(value, 0.0) + jnp.log1p(jnp.exp(-jnp.abs(value)))


class Chunk:
    def __init__(self, refs, head, heads, n, first_place):
        padded_ref, taps_ref, bd_ref, begin_ref, rate_ref, shift_ref = refs
        at_beta = heads * V + head
        self.head, self.n = head, n
        cols = (
            (head * K, K),
            (heads * K + head * K, K),
            (2 * heads * K + head * V, V),
        )
        self.cols = cols
        if isinstance(n, int):
            rows, padded_rows = pl.ds(n * GROUP, GROUP), pl.ds(n * GROUP, GROUP + RIM)
        else:
            start = pl.multiple_of(n * GROUP, GROUP)
            rows, padded_rows = pl.ds(start, GROUP), pl.ds(start, GROUP + RIM)
        self.rows = rows
        row, col = triangles()
        begin = begin_ref[rows, :]
        base = first_place + n * GROUP
        place = base + lax.broadcasted_iota(jnp.int32, (GROUP, 1), 0)
        self.ranges = [
            (place - lag >= begin).astype(jnp.float32) for lag in range(1, CONV)
        ]
        self.padded = [
            padded_ref[padded_rows, at : at + size].astype(jnp.float32) for at, size in cols
        ]
        self.taps = [taps_ref[:, at : at + size] for at, size in cols]
        self.pres = [
            conv_rows(padded, taps, self.ranges)
            for padded, taps in zip(self.padded, self.taps)
        ]
        self.sigs = [jax.nn.sigmoid(pre) for pre in self.pres]
        query, key, self.value = [pre * sig for pre, sig in zip(self.pres, self.sigs)]
        self.query_root, self.key_root = unit_norm(query), unit_norm(key)
        self.query = query * (self.query_root * K ** (-0.5))
        self.key = key * self.key_root
        self.beta = jax.nn.sigmoid(bd_ref[rows, at_beta : at_beta + 1])
        self.decay_in = bd_ref[rows, at_beta + heads : at_beta + heads + 1] + shift_ref[head]
        self.rate = rate_ref[head]
        decay = self.rate * soft_plus(self.decay_in)
        self.decay = decay
        lower = row >= col
        decay_row = jnp.sum(jnp.where(row == col, decay, 0.0), axis=0, keepdims=True)
        cumul = jnp.sum(jnp.where(lower, decay_row, 0.0), axis=1, keepdims=True)
        cumul_row = jnp.sum(jnp.where(row <= col, decay, 0.0), axis=0, keepdims=True)
        same = (begin <= base + col) & lower
        self.factor = jnp.where(same, jnp.exp(jnp.where(same, cumul - cumul_row, 0.0)), 0.0)
        self.carry = jnp.where(begin < base, jnp.exp(cumul), 0.0)
        self.scale = self.carry[GROUP - 1 :, :]
        last_alive = begin[GROUP - 1 :, :] <= place
        gap = cumul[GROUP - 1 :, :] - cumul
        self.last = jnp.where(last_alive, jnp.exp(jnp.where(last_alive, gap, 0.0)), 0.0)
        self.key_last = self.key * self.last
        self.weights = jnp.where(row > col, self.factor, 0.0)

    def sides(self):
        return jnp.concatenate(
            [self.beta * self.value, (self.beta * self.carry) * self.key], axis=1
        )


def mixer_kernel(heads, blocks, tp_count, fsdp_count, wide, splits, *refs):
    bf16, f32 = jnp.bfloat16, jnp.float32
    refs = list(refs)

    def take(number):
        out = refs[:number]
        del refs[:number]
        return out

    weight_count = len(splits)
    mixed_any, gate_ref, taps_ref, begin_ref, rate_ref, shift_ref, norm_ref = take(7)
    cot_any = take(1)[0]
    shards = take(weight_count)
    normed_ref, inv_ref, side_ref, query_ref, score_ref, state_ref, update_ref, out_ref = take(8)
    maps, scales, padded, pairs, cot_rows = take(5)
    wholes = take(weight_count)
    prefix, own_pair, rim_sems, load_sem, pair_send, pair_recv, cot_sems, cot_send, cot_recv = take(9)
    weight_sems = take(weight_count)
    piece_sems = [take(2) for _ in range(sum(len(split) for split in splits))]
    rows = blocks * GROUP
    mine = lax.axis_index("fsdp")
    load = pltpu.make_async_copy(mixed_any, padded.at[pl.ds(RIM, rows)], load_sem)
    load.start()
    entry_barrier([("fsdp", fsdp_count), ("tp", tp_count)], everyone=True)
    rim = pltpu.make_async_remote_copy(
        src_ref=mixed_any.at[pl.ds(rows - RIM, RIM)],
        dst_ref=padded.at[pl.ds(0, RIM)],
        send_sem=rim_sems.at[0],
        recv_sem=rim_sems.at[1],
        device_id=on_axis("fsdp", lax.rem(mine + 1, fsdp_count)),
        device_id_type=MESH,
    )
    rim.start()
    gathers, locals_ = [], []
    for k in range(weight_count):
        copy = pltpu.make_async_copy(shards[k], wholes[k].at[mine], weight_sems[k])
        copy.start()
        locals_.append(copy)
        for part in splits[k]:
            sems = piece_sems[len(gathers)]
            gathers.append(
                Gather(
                    "fsdp", fsdp_count, wholes[k], sems[0], sems[1], own=shards[k], part=part
                )
            )
    depth = 3
    for gather in gathers[:depth]:
        gather.start()
    cot = Gather("tp", tp_count, cot_rows, cot_send, cot_recv, own=cot_any)
    cot.start()
    cot_local = pltpu.make_async_copy(cot_any, cot_rows.at[cot.me], cot_sems)
    cot_local.start()
    load.wait()
    rim.wait()
    first_place = mine * rows
    source = (padded, taps_ref, gate_ref, begin_ref, rate_ref, shift_ref)
    row, col = triangles()
    turns = blocks // wide

    def pump(k):
        if k < len(gathers):
            gathers[k].forward_all()
            if k + depth < len(gathers):
                gathers[k + depth].start()

    for h in range(heads):
        own_pair[h] = jnp.concatenate(
            [(row == col).astype(f32), jnp.zeros((K, V), f32)], axis=1
        )

    def front(step, carry):
        units = [
            Chunk(source, h, heads, step * wide + j, first_place)
            for j in range(wide)
            for h in range(heads)
        ]
        lowers = [
            unit.beta * dot_three(unit.key, unit.key, dot_nt) * unit.weights for unit in units
        ]
        inverses = [half(inverse) for inverse in unit_inverses(lowers)]
        solved = [dot_nn(inv, half(unit.sides())) for inv, unit in zip(inverses, units)]
        for unit, inv, sides in zip(units, inverses, solved):
            h, n = unit.head, unit.n
            inv_ref[h, n] = inv
            side_ref[h, n] = sides
            query_ref[h, n] = half(unit.query * unit.carry)
            score_ref[h, n] = half(
                dot_nt(half(unit.query), half(unit.key)) * unit.factor
            )
            driven = dot_tn(half(unit.key_last), half(sides))
            maps[h, n] = driven[:, V:]
            scales[h, n] = jnp.broadcast_to(unit.scale, (8, 128))
            pair = own_pair[h]
            prefix[h, n] = pair
            moved = dot_three(driven[:, V:], pair, dot_nn)
            drive = jnp.concatenate([jnp.zeros((K, K), f32), driven[:, :V]], axis=1)
            own_pair[h] = unit.scale * pair + drive - moved

        for k in range(turns - 1):

            @pl.when(step == k)
            def _(k=k):
                if k == 0:
                    cot.forward_all()
                    pump(0)
                else:
                    pump(2 * k - 1)
                    pump(2 * k)

        return carry

    lax.fori_loop(0, turns, front, 0)
    for h in range(heads):
        pairs[mine, pl.ds(h * K, K), :] = half(own_pair[h])
    ring = Gather("fsdp", fsdp_count, pairs, pair_send, pair_recv)
    ring.start()
    ring.forward_all()
    ring.arrive_all()
    done = 2 * (turns - 1) - 1
    for k in range(done, len(gathers)):
        pump(k)
    hops = min(fsdp_count - 1, -(-MAXLEN // rows))
    states = [jnp.zeros((K, V), f32) for _ in range(heads)]
    for hop in range(hops, 0, -1):
        spot = jnp.maximum(mine - hop, 0)
        for h in range(heads):
            piece = pairs[spot, pl.ds(h * K, K), :]
            top, low = split_two(states[h])
            new = dot_nn(piece[:, :K], top) + dot_nn(piece[:, :K], low)
            states[h] = jnp.where(mine >= hop, new + piece[:, K:].astype(f32), states[h])

    def back(n, carry):
        at = pl.ds(pl.multiple_of(n * GROUP, GROUP), GROUP)
        for h in range(heads):
            pair = prefix[h, n]
            start = half(dot_three(pair[:, :K], states[h], dot_nn) + pair[:, K:])
            state_ref[h, n] = start
            sides = side_ref[h, n]
            update = half(sides[:, :V] - dot_nn(half(sides[:, V:]), start))
            update_ref[h, n] = update
            out = dot_nn(query_ref[h, n], start) + dot_nn(score_ref[h, n], update)
            out_ref[h, n] = out
            gate = gate_ref[at, h * V : (h + 1) * V]
            root = lax.rsqrt(jnp.mean(out * out, axis=-1, keepdims=True) + 1e-06)
            normed_ref[at, h * V : (h + 1) * V] = half(
                out * root * norm_ref[...] * (gate * jax.nn.sigmoid(gate))
            )
        return carry

    lax.fori_loop(0, blocks, back, 0)
    cot.arrive_all()
    for gather in gathers:
        gather.arrive_all()
    for copy in locals_ + [cot_local]:
        copy.wait()
    for gather in gathers + [ring, cot]:
        gather.finish()


def mixer_all(mixed, gate, taps, begins, rate, shift, norm, cotangent, shards, ident):
    tp_count, fsdp_count = lax.axis_size("tp"), lax.axis_size("fsdp")
    heads = rate.shape[0]
    splits = [parts_of(shard.shape[0], 2) for shard in shards]
    rows = mixed.shape[0]
    blocks = rows // GROUP
    wide = 2 if blocks % 2 == 0 else 1
    f32, bf16 = jnp.float32, jnp.bfloat16
    vmem = pl.BlockSpec(memory_space=pltpu.VMEM)
    smem = pl.BlockSpec(memory_space=pltpu.SMEM)
    anys = pl.BlockSpec(memory_space=pl.ANY)
    dma = pltpu.SemaphoreType.DMA
    shape = jax.ShapeDtypeStruct
    outs = [
        shape((rows, heads * V), bf16),
        shape((heads, blocks, GROUP, GROUP), bf16),
        shape((heads, blocks, GROUP, V + K), f32),
        shape((heads, blocks, GROUP, K), bf16),
        shape((heads, blocks, GROUP, GROUP), bf16),
        shape((heads, blocks, K, V), bf16),
        shape((heads, blocks, GROUP, V), bf16),
        shape((heads, blocks, GROUP, V), f32),
        shape((heads, blocks, K, K), f32),
        shape((heads, blocks, 8, 128), f32),
        shape((rows + RIM, mixed.shape[1]), bf16),
        shape((fsdp_count, heads * K, K + V), bf16),
        shape((tp_count,) + cotangent.shape, bf16),
    ] + [shape((fsdp_count,) + shard.shape, shard.dtype) for shard in shards]
    scratch = [
        pltpu.VMEM((heads, blocks, K, K + V), f32),
        pltpu.VMEM((heads, K, K + V), f32),
        dma((2,)),
        dma,
        dma((fsdp_count - 1,)),
        dma((fsdp_count,)),
        dma,
        dma((tp_count - 1,)),
        dma((tp_count,)),
    ]
    scratch += [dma] * len(shards)
    for _ in range(sum(len(split) for split in splits)):
        scratch += [dma((fsdp_count - 1,)), dma((fsdp_count,))]
    return pl.pallas_call(
        functools.partial(
            mixer_kernel, heads, blocks, tp_count, fsdp_count, wide, splits
        ),
        out_shape=outs,
        in_specs=[anys] + [vmem] * 3 + [smem] * 2 + [vmem] + [anys] * (1 + len(shards)),
        out_specs=[vmem] * 12 + [anys] * (1 + len(shards)),
        scratch_shapes=scratch,
        compiler_params=comm_params(ident, 56),
        name="mixer",
    )(mixed, gate, taps, begins, rate, shift, norm, cotangent, *shards)


def mixer_grad_kernel(heads, blocks, tp_count, fsdp_count, splits, *refs):
    bf16, f32 = jnp.bfloat16, jnp.float32
    refs = list(refs)

    def take(number):
        out = refs[:number]
        del refs[:number]
        return out

    extra_count = len(splits)
    padded, gate_ref, taps_ref, begin_ref, rate_ref, shift_ref, norm_ref = take(7)
    inv_ref, side_ref, query_ref, score_ref, state_ref, update_ref, out_ref = take(7)
    maps, scales, pairs, dm_ref = take(4)
    extras = take(extra_count)
    d_raw_ref, g_taps_ref, g_decay_ref, g_norm_ref = take(4)
    extra_outs = take(extra_count)
    d_out, base, local, d_state, halo, tail, d_all, rim_buf = take(8)
    rim_sems, ring_send, ring_recv = take(3)
    rows = blocks * GROUP
    mine = lax.axis_index("fsdp")
    first_place = mine * rows
    mixed_cols = 2 * heads * K + heads * V
    entry_barrier([("fsdp", fsdp_count)], everyone=True)
    sums, sum_outs = [], []
    for extra, out, split in zip(extras, extra_outs, splits):
        for part in split:
            s = take(7)
            sums.append(
                Scatter(
                    "fsdp", fsdp_count, None, s[0], s[1], s[2], s[3:], full=extra, part=part
                )
            )
            sum_outs.append(out)
    depth = 3
    for item in sums[:depth]:
        item.start()

    def pump(k):
        if k < len(sums):
            if k + depth < len(sums):
                sums[k + depth].start()
            sums[k].turn(sum_outs[k])

    g_norm_ref[...] = jnp.zeros_like(g_norm_ref)
    g_taps_ref[...] = jnp.zeros_like(g_taps_ref)
    g_decay_ref[...] = jnp.zeros_like(g_decay_ref)
    halo[...] = jnp.zeros_like(halo)
    source = (padded, taps_ref, gate_ref, begin_ref, rate_ref, shift_ref)
    row, col = triangles()

    def first(n, carry):
        at = pl.ds(pl.multiple_of(n * GROUP, GROUP), GROUP)
        for h in range(heads):
            cols = slice(h * V, (h + 1) * V)
            out = out_ref[h, n]
            root = lax.rsqrt(jnp.mean(out * out, axis=-1, keepdims=True) + 1e-06)
            normed = out * root
            gate = gate_ref[at, cols]
            sig = jax.nn.sigmoid(gate)
            silu = gate * sig
            given = dm_ref[at, cols]
            g_norm_ref[...] += jnp.sum(given * normed * silu, axis=0, keepdims=True)
            pulled = given * norm_ref[...]
            d_raw_ref[at, mixed_cols + h * V : mixed_cols + (h + 1) * V] = half(
                pulled * normed * (sig + silu * (1.0 - sig))
            )
            pulled = pulled * silu
            grad = root * (pulled - normed * jnp.mean(pulled * normed, axis=-1, keepdims=True))
            grad = half(grad)
            d_out[h, n] = grad
            through = dot_tn(score_ref[h, n], grad)
            base[h, n] = through
            key_part = half(side_ref[h, n][:, V:])
            local[h, n] = dot_tn(query_ref[h, n], grad) - dot_tn(key_part, half(through))
        return carry

    lax.fori_loop(0, blocks, first, 0)
    pump(0)

    def pull_state(n, h, grad):
        scale = scales[h, n][0:1, 0:1]
        return scale * grad + local[h, n] - dot_three(maps[h, n], grad, dot_tn)

    for h in range(heads):
        d_state[h] = jnp.zeros((K, V), f32)

    def chain(step, carry):
        n = blocks - 1 - step
        for h in range(heads):
            d_state[h] = pull_state(n, h, d_state[h])
        return carry

    lax.fori_loop(0, blocks, chain, 0)
    for h in range(heads):
        d_all[mine, pl.ds(h * K, K), :] = half(d_state[h])
    ring = Gather("fsdp", fsdp_count, d_all, ring_send, ring_recv)
    ring.start()
    pump(1)
    ring.forward_all()
    pump(2)
    ring.arrive_all()
    hops = min(fsdp_count - 1, -(-MAXLEN // rows))
    for h in range(heads):
        grad = jnp.zeros((K, V), f32)
        for hop in range(hops, 0, -1):
            spot = jnp.minimum(mine + hop, fsdp_count - 1)
            piece = pairs[spot, pl.ds(h * K, K), :][:, :K]
            top, low = split_two(grad)
            new = dot_tn(piece, top) + dot_tn(piece, low)
            new = new + d_all[spot, pl.ds(h * K, K), :].astype(f32)
            grad = jnp.where(mine + hop < fsdp_count, new, grad)
        d_state[h] = grad

    def second(step, carry):
        n = blocks - 1 - step
        at = pl.ds(pl.multiple_of(n * GROUP, GROUP), GROUP)
        lane = lax.broadcasted_iota(jnp.int32, (1, g_decay_ref.shape[1]), 1)
        smalls = []
        for h in range(heads):
            unit = Chunk(source, h, heads, n, first_place)
            query, key, key_last = half(unit.query), half(unit.key), half(unit.key_last)
            after = d_state[h]
            d_state[h] = pull_state(n, h, after)
            after_half = half(after)
            state, grad, update = state_ref[h, n], d_out[h, n], update_ref[h, n]
            sides = side_ref[h, n]
            d_update = half(base[h, n] + dot_nn(key_last, after_half))
            d_key_part = -dot_nt(d_update, state)
            read = dot_nt(grad, state)
            d_query = unit.carry * read
            d_carry = jnp.sum(read * unit.query, axis=1, keepdims=True)
            d_scores = dot_nt(grad, update)
            d_key_last = dot_nt(update, after_half)
            d_scale = jnp.sum(
                jnp.sum(after * state.astype(f32), axis=1, keepdims=True), axis=0, keepdims=True
            )
            d_sides = dot_tn(
                inv_ref[h, n], jnp.concatenate([d_update, half(d_key_part)], axis=1)
            )
            d_lower = -dot_nt(half(d_sides), half(sides))
            gram = dot_nt(key, key) * unit.weights
            pulled = d_lower * gram
            d_beta = jnp.sum(pulled, axis=1, keepdims=True)
            moved = unit.beta * pulled + d_scores * score_ref[h, n].astype(f32)
            d_gram = half(d_lower * (unit.beta * unit.weights))
            d_qk = half(d_scores * unit.factor)
            d_query = d_query + dot_nn(d_qk, key)
            d_key = dot_tn(d_qk, query) + dot_nn(d_gram, key) + dot_tn(d_gram, key)
            d_key = d_key + d_key_last * unit.last
            d_last = jnp.sum(d_key_last * unit.key_last, axis=1, keepdims=True)
            d_value_side, d_key_side = d_sides[:, :V], d_sides[:, V:]
            d_beta = d_beta + jnp.sum(d_value_side * unit.value, axis=1, keepdims=True)
            d_value = unit.beta * d_value_side
            mixed_side = jnp.sum(d_key_side * unit.key, axis=1, keepdims=True)
            d_key = d_key + (unit.beta * unit.carry) * d_key_side
            d_beta = d_beta + unit.carry * mixed_side
            d_carry = d_carry + unit.beta * mixed_side
            at_end = lax.broadcasted_iota(jnp.int32, (GROUP, 1), 0) == GROUP - 1
            d_carry = d_carry + jnp.where(at_end, d_scale, 0.0)
            d_cumul = d_carry * unit.carry - d_last
            d_cumul = d_cumul + jnp.where(
                at_end, jnp.sum(d_last, axis=0, keepdims=True), 0.0
            )
            d_cumul = d_cumul + jnp.sum(moved, axis=1, keepdims=True)
            d_row = jnp.sum(jnp.where(row == col, d_cumul, 0.0), axis=0, keepdims=True)
            d_row = d_row - jnp.sum(moved, axis=0, keepdims=True)
            d_decay = jnp.sum(jnp.where(col >= row, d_row, 0.0), axis=1, keepdims=True)
            d_decay_in = d_decay * unit.rate * jax.nn.sigmoid(unit.decay_in)
            log_sum = jnp.sum(d_decay * unit.decay, axis=0, keepdims=True)
            bias_sum = jnp.sum(d_decay_in, axis=0, keepdims=True)
            g_decay_ref[...] += jnp.where(lane == h, log_sum, 0.0) + jnp.where(
                lane == heads + h, bias_sum, 0.0
            )
            smalls.append((d_beta * unit.beta * (1.0 - unit.beta), d_decay_in))
            unscaled = unit.query * K**0.5
            d_query = d_query * K ** (-0.5)
            d_query = unit.query_root * (
                d_query - unscaled * jnp.sum(d_query * unscaled, axis=1, keepdims=True)
            )
            d_key = unit.key_root * (
                d_key - unit.key * jnp.sum(d_key * unit.key, axis=1, keepdims=True)
            )
            for part, given in enumerate((d_query, d_key, d_value)):
                start, size = unit.cols[part]
                sig, pre = unit.sigs[part], unit.pres[part]
                d_pre = given * sig * (1.0 + pre * (1.0 - sig))
                taps, spread = unit.taps[part], unit.padded[part]
                total = taps[0:1] * d_pre
                edge = jnp.zeros((RIM, size), f32)
                grads = [jnp.sum(d_pre * spread[RIM:], axis=0, keepdims=True)]
                whole = jnp.concatenate([edge, total], axis=0)
                for lag in range(1, CONV):
                    masked = d_pre * unit.ranges[lag - 1]
                    grads.append(
                        jnp.sum(
                            masked * pltpu.roll(spread, lag, 0)[RIM:], axis=0, keepdims=True
                        )
                    )
                    ext = jnp.concatenate([edge, taps[lag : lag + 1] * masked], axis=0)
                    whole = whole + pltpu.roll(ext, GROUP + RIM - lag, 0)
                for lag in range(CONV):
                    g_taps_ref[lag : lag + 1, start : start + size] += grads[lag]
                body = whole[RIM:]
                ended = body[GROUP - RIM :] + halo[:, start : start + size]
                halo[:, start : start + size] = whole[:RIM]
                body = jnp.concatenate([body[: GROUP - RIM], ended], axis=0)
                d_raw_ref[at, start : start + size] = half(body)

                @pl.when(step == 0)
                def _():
                    tail[:, start : start + size] = ended

        spot = lax.broadcasted_iota(jnp.int32, (GROUP, 2 * heads), 1)
        joined = jnp.zeros((GROUP, 2 * heads), f32)
        for h, (d_beta, d_decay_in) in enumerate(smalls):
            joined = joined + jnp.where(spot == h, d_beta, 0.0)
            joined = joined + jnp.where(spot == heads + h, d_decay_in, 0.0)
        d_raw_ref[at, mixed_cols + heads * V :] = half(joined)
        for k in range(3, len(sums)):

            @pl.when(step == min(k - 3, blocks - 1))
            def _(k=k):
                pump(k)

        return carry

    lax.fori_loop(0, blocks, second, 0)
    rim = pltpu.make_async_remote_copy(
        src_ref=halo,
        dst_ref=rim_buf,
        send_sem=rim_sems.at[0],
        recv_sem=rim_sems.at[1],
        device_id=on_axis("fsdp", lax.rem(mine + fsdp_count - 1, fsdp_count)),
        device_id_type=MESH,
    )
    rim.start()
    for item, out in zip(sums, sum_outs):
        item.close(out)
    rim.wait()
    d_raw_ref[rows - RIM : rows, 0:mixed_cols] = half(tail[...] + rim_buf[...])
    for item in sums + [ring]:
        item.finish()


def mixer_grad_all(
    padded, gate, taps, begins, rate, shift, norm, saved, pairs, d_mixer, extras, ident
):
    tp_count, fsdp_count = lax.axis_size("tp"), lax.axis_size("fsdp")
    heads = rate.shape[0]
    splits = [parts_of(extra.shape[1], 2) for extra in extras]
    rows = gate.shape[0]
    blocks = rows // GROUP
    mixed_cols = padded.shape[1]
    f32, bf16 = jnp.float32, jnp.bfloat16
    vmem = pl.BlockSpec(memory_space=pltpu.VMEM)
    smem = pl.BlockSpec(memory_space=pltpu.SMEM)
    dma = pltpu.SemaphoreType.DMA
    shape = jax.ShapeDtypeStruct
    outs = [
        shape((rows, mixed_cols + heads * V + 2 * heads), bf16),
        shape((CONV, mixed_cols), f32),
        shape((1, 128), f32),
        shape((1, V), f32),
    ] + [shape(extra.shape[1:], f32) for extra in extras]
    scratch = [
        pltpu.VMEM((heads, blocks, GROUP, V), bf16),
        pltpu.VMEM((heads, blocks, GROUP, V), f32),
        pltpu.VMEM((heads, blocks, K, V), f32),
        pltpu.VMEM((heads, K, V), f32),
        pltpu.VMEM((RIM, mixed_cols), f32),
        pltpu.VMEM((RIM, mixed_cols), f32),
        pltpu.VMEM((fsdp_count, heads * K, V), bf16),
        pltpu.VMEM((RIM, mixed_cols), f32),
        dma((2,)),
        dma((fsdp_count - 1,)),
        dma((fsdp_count,)),
    ]
    for extra, split in zip(extras, splits):
        for part in split:
            size = extra.shape[1] if part is None else part[1]
            scratch += scatter_scratch(fsdp_count, size, extra.shape[2], full=True)
    return pl.pallas_call(
        functools.partial(
            mixer_grad_kernel, heads, blocks, tp_count, fsdp_count, splits
        ),
        out_shape=outs,
        in_specs=[vmem] * 4 + [smem] * 2 + [vmem] * (12 + len(extras)),
        out_specs=[vmem] * len(outs),
        scratch_shapes=scratch,
        compiler_params=comm_params(ident, 60),
        name="mixer_grad",
    )(padded, gate, taps, begins, rate, shift, norm, *saved, pairs, d_mixer, *extras)


def shards(
    tokens,
    lengths,
    attn_gain,
    w_query,
    w_key,
    w_value,
    w_gate_out,
    w_beta,
    w_decay,
    conv_query,
    conv_key,
    conv_value,
    decay_log,
    decay_bias,
    out_gain,
    w_out,
    ffn_gain,
    w_ffn_gate,
    w_ffn_up,
    w_ffn_down,
    cotangent,
):
    count = lax.axis_size("fsdp")
    shard_rows = tokens.shape[0]
    query_cols, value_cols = w_query.shape[1], w_value.shape[1]
    hidden_cols = w_ffn_gate.shape[1]
    head_count = query_cols // K
    mixed_cols = 2 * query_cols + value_cols
    raw_cols = mixed_cols + value_cols

    tp_count = lax.axis_size("tp")
    width = tokens.shape[1]
    small_list = (attn_gain, ffn_gain, out_gain, conv_query, conv_key, conv_value)
    small = jnp.concatenate([part.astype(jnp.float32).reshape(-1) for part in small_list])
    small_width = -(-small.shape[0] // 1024) * 1024
    small = jnp.pad(small, (0, small_width - small.shape[0])).reshape(8, -1)
    gate_shard = jnp.concatenate([w_gate_out, w_beta, w_decay], axis=1)
    normed_blocks, small, *mixer_w, mixed_raw, gate_raw = front_all(
        tokens, small, [w_query, w_key, w_value, gate_shard], 0
    )
    small = small.reshape(count, -1)
    smalls, at = ([], 0)
    for part in small_list:
        piece = small[:, at : at + part.size]
        at = at + part.size
        if part.ndim == 3:
            piece = piece.reshape((count,) + part.shape).transpose(1, 2, 0, 3)
            smalls.append(piece.reshape(part.shape[0], part.shape[1], -1))
        else:
            smalls.append(piece.reshape(-1))
    gain_one, gain_two, norm_out, query_taps, key_taps, value_taps = smalls
    row_count = mixed_raw.shape[0]
    positions = lax.axis_index("fsdp") * row_count + jnp.arange(row_count, dtype=jnp.int32)
    begins = seq_begin(lengths, positions)
    taps = jnp.concatenate(
        [part.reshape(CONV, -1) for part in (query_taps, key_taps, value_taps)], axis=1
    )
    common = (
        gate_raw,
        taps,
        begins.reshape(-1, 1),
        -jnp.exp(decay_log),
        decay_bias,
        norm_out.reshape(1, -1),
    )
    normed_mixer, *saved, padded, pairs, cot_blocks, out_t, ffn_gate_w, ffn_up_w, down_t = (
        mixer_all(
            mixed_raw,
            *common,
            cotangent,
            [w_out.T, w_ffn_gate, w_ffn_up, w_ffn_down.T],
            1,
        )
    )
    out_t, ffn_gate_w, ffn_up_w, down_t = [
        part.reshape(width, -1) for part in (out_t, ffn_gate_w, ffn_up_w, down_t)
    ]
    (
        output,
        d_hidden,
        d_mixer,
        g_gate,
        g_up,
        g_down,
        g_out,
        gain_two_part,
    ) = ffn_all(
        normed_mixer.reshape(tp_count, shard_rows, -1),
        tokens,
        cotangent,
        out_t,
        gain_two.reshape(1, -1),
        cot_blocks,
        ffn_gate_w,
        ffn_up_w,
        down_t,
        2,
    )
    d_mixer = d_mixer.reshape(row_count, -1)
    gain_two_part = gain_two_part.reshape(-1)

    d_raw, g_taps, g_decay, norm_out_part, *grads_ffn = mixer_grad_all(
        padded,
        *common,
        saved,
        pairs,
        d_mixer,
        [part.reshape(count, width // count, -1) for part in (g_out, g_gate, g_up, g_down)],
        3,
    )
    grad_out_t, grad_w_ffn_gate, grad_w_ffn_up, grad_down_t = grads_ffn
    d_taps = [
        part.reshape(CONV, head_count, -1)
        for part in jnp.split(g_taps, (query_cols, 2 * query_cols), axis=1)
    ]
    decay_pair = g_decay[0, : 2 * head_count]

    def spread(taps):
        taps = taps.reshape(taps.shape[0], taps.shape[1], count, -1)
        return taps.transpose(2, 0, 1, 3).reshape(count, -1)

    small_parts = [
        gain_two_part.reshape(count, -1),
        norm_out_part.reshape(count, -1),
        spread(d_taps[0]),
        spread(d_taps[1]),
        spread(d_taps[2]),
        jnp.broadcast_to(decay_pair[None, :], (count, decay_pair.shape[0])),
    ]
    small_cat = jnp.concatenate(small_parts, axis=1)
    lanes = -(-max(small_cat.shape[1], 7 * (width // count)) // (7 * 128)) * 128
    small_cat = jnp.pad(small_cat, ((0, 0), (lanes, 7 * lanes - small_cat.shape[1])))
    d_tokens, small_own, small_all, *grads_mixer = last_all(
        d_raw.reshape(tp_count, shard_rows, -1),
        normed_blocks,
        tokens,
        gain_one.reshape(1, -1),
        d_hidden,
        small_cat.reshape(count, 8, lanes),
        mixer_w,
        4,
    )
    grad_w_ffn_down = grad_down_t.T
    grad_w_out = grad_out_t.T
    grads_w = grads_mixer[:3] + jnp.split(
        grads_mixer[3], (value_cols, value_cols + head_count), axis=1
    )
    small_cuts, at = ([], lanes)
    for part in small_parts:
        small_cuts.append(at)
        at = at + part.shape[1]
    small_cuts.append(at)
    own_parts = jnp.split(small_own.reshape(-1), small_cuts)
    all_parts = jnp.split(small_all.reshape(-1), small_cuts)
    small_out = [
        small_all[0, : width // count],
        all_parts[1],
        all_parts[2],
        own_parts[3],
        own_parts[4],
        own_parts[5],
        own_parts[6],
    ]
    return (
        output,
        d_tokens,
        small_out[0],
        *grads_w,
        small_out[3].reshape(conv_query.shape),
        small_out[4].reshape(conv_key.shape),
        small_out[5].reshape(conv_value.shape),
        small_out[6][:head_count],
        small_out[6][head_count:],
        small_out[2],
        grad_w_out,
        small_out[1],
        grad_w_ffn_gate,
        grad_w_ffn_up,
        grad_w_ffn_down,
    )


def solution(mesh):
    placed = (
        P(("fsdp", "tp"), None),
        P(),
        P("fsdp"),
        P("fsdp", "tp"),
        P("fsdp", "tp"),
        P("fsdp", "tp"),
        P("fsdp", "tp"),
        P("fsdp", "tp"),
        P("fsdp", "tp"),
        P(None, "tp", "fsdp"),
        P(None, "tp", "fsdp"),
        P(None, "tp", "fsdp"),
        P("tp"),
        P("tp"),
        P("fsdp"),
        P("tp", "fsdp"),
        P("fsdp"),
        P("fsdp", "tp"),
        P("fsdp", "tp"),
        P("tp", "fsdp"),
        P(("fsdp", "tp"), None),
    )
    return jax.shard_map(
        shards,
        mesh=mesh,
        in_specs=placed,
        out_specs=(
            P(("fsdp", "tp"), None),
            P(("fsdp", "tp"), None),
            P("fsdp"),
            P("fsdp", "tp"),
            P("fsdp", "tp"),
            P("fsdp", "tp"),
            P("fsdp", "tp"),
            P("fsdp", "tp"),
            P("fsdp", "tp"),
            P(None, "tp", "fsdp"),
            P(None, "tp", "fsdp"),
            P(None, "tp", "fsdp"),
            P("tp"),
            P("tp"),
            P("fsdp"),
            P("tp", "fsdp"),
            P("fsdp"),
            P("fsdp", "tp"),
            P("fsdp", "tp"),
            P("tp", "fsdp"),
        ),
        check_vma=False,
    )
```

```python
import functools

import jax
import jax.numpy as jnp
from jax import lax
from jax.experimental import pallas as pl
from jax.experimental.pallas import tpu as pltpu
from jax.sharding import PartitionSpec as P

K = 128
V = 256
CONV = 4
GROUP = 128
MAXLEN = 4096
RIM = 16


def mat_dot(left, right):
    return jnp.dot(left, right, preferred_element_type=jnp.float32)


def rms_scale(values, scale_gain):
    return (
        values * lax.rsqrt(jnp.mean(values * values, axis=-1, keepdims=True) + 1e-06) * scale_gain
    )


def seq_begin(lengths, positions):
    number = lengths.shape[0]
    earlier = jnp.arange(number)[None, :] < jnp.arange(number)[:, None]
    offsets = jnp.sum(jnp.where(earlier, lengths[None, :], 0), axis=1)
    chosen = jnp.where(offsets[None, :] <= positions[:, None], offsets[None, :], 0)
    return jnp.max(chosen, axis=1)


MESH = pl.DeviceIdType.MESH
INNER = 2


def on_axis(axis, index):
    return {axis: index}


def halves(axis):
    me = lax.axis_index(axis)
    return me, lax.div(me, INNER), lax.rem(me, INNER)


def entry_barrier(axes, everyone=False):
    barrier = pltpu.get_barrier_semaphore()
    total = 0
    for axis, count in axes:
        me, outer, inner = halves(axis)
        outers = count // INNER
        peers = [outer * INNER + (1 - inner)]
        for d in range(1, outers):
            peers.append(lax.rem(outer + d, outers) * INNER + inner)
        if everyone:
            peers = [lax.rem(me + d, count) for d in range(1, count)]
        for peer in peers:
            pl.semaphore_signal(
                barrier, inc=1, device_id=on_axis(axis, peer), device_id_type=MESH
            )
        total += len(peers)
    pl.semaphore_wait(barrier, total)


class Gather:
    def __init__(self, axis, count, buf, send, recv, own=None, part=None):
        self.axis, self.count, self.buf, self.send, self.recv = axis, count, buf, send, recv
        self.outers = count // INNER
        self.me, self.outer, self.inner = halves(axis)
        self.part = part
        if own is None:
            self.own = self.slot(self.me)
        else:
            self.own = own if part is None else own.at[pl.ds(*part)]

    def slot(self, index):
        if self.part is None:
            return self.buf.at[index]
        return self.buf.at[index, pl.ds(*self.part)]

    def block(self, d, across):
        outer = lax.rem(self.outer + self.outers - d, self.outers)
        return outer * INNER + ((1 - self.inner) if across else self.inner)

    def copy(self, d, forward):
        across = self.outer * INNER + 1 - self.inner
        if forward:
            index = self.block(d, False)
            src, target, sem = self.slot(index), across, self.outers - 1 + d
        else:
            index, src = self.me, self.own
            target = across
            if d:
                target = lax.rem(self.outer + d, self.outers) * INNER + self.inner
            sem = d
        return pltpu.make_async_remote_copy(
            src_ref=src,
            dst_ref=self.slot(index),
            send_sem=self.send.at[sem],
            recv_sem=self.recv.at[index],
            device_id=on_axis(self.axis, target),
            device_id_type=MESH,
        )

    def start(self):
        for d in list(range(1, self.outers)) + [0]:
            self.copy(d, False).start()

    def arrive(self, index):
        pltpu.make_async_remote_copy(
            src_ref=self.slot(index),
            dst_ref=self.slot(index),
            send_sem=self.send.at[0],
            recv_sem=self.recv.at[index],
            device_id=on_axis(self.axis, self.outer * INNER + 1 - self.inner),
            device_id_type=MESH,
        ).wait_recv()

    def forward(self, d):
        index = self.block(d, False)
        self.arrive(index)
        self.copy(d, True).start()
        return index

    def forward_all(self):
        for d in range(1, self.outers):
            self.forward(d)

    def arrive_all(self):
        for d in range(self.outers):
            self.arrive(self.block(d, True))

    def finish(self):
        for d in range(self.outers):
            self.copy(d, False).wait_send()
        for d in range(1, self.outers):
            self.copy(d, True).wait_send()


class Scatter:
    def __init__(self, axis, count, out, stage, send2, stage2, sems, full=None, part=None):
        self.axis, self.count, self.full, self.part = axis, count, full, part
        self.outers = count // INNER
        self.me, self.outer, self.inner = halves(axis)
        self.out, self.stage, self.send2, self.stage2 = out, stage, send2, stage2
        self.send_a, self.recv_a, self.send_b, self.recv_b = sems

    def target(self, d, across):
        outer = lax.rem(self.outer + d, self.outers)
        return outer * INNER + ((1 - self.inner) if across else self.inner)

    def own(self, d):
        if self.part is None:
            return self.full[self.target(d, False)].astype(jnp.float32)
        return self.full[self.target(d, False), pl.ds(*self.part)].astype(jnp.float32)

    def first(self, d):
        if self.full is None:
            src = self.out.at[d]
        elif self.part is None:
            src = self.full.at[self.target(d, True)]
        else:
            src = self.full.at[self.target(d, True), pl.ds(*self.part)]
        return pltpu.make_async_remote_copy(
            src_ref=src,
            dst_ref=self.stage.at[d],
            send_sem=self.send_a.at[d],
            recv_sem=self.recv_a.at[d],
            device_id=on_axis(self.axis, self.outer * INNER + 1 - self.inner),
            device_id_type=MESH,
        )

    def second(self, d):
        return pltpu.make_async_remote_copy(
            src_ref=self.send2.at[d - 1],
            dst_ref=self.stage2.at[d - 1],
            send_sem=self.send_b.at[d - 1],
            recv_sem=self.recv_b.at[d - 1],
            device_id=on_axis(self.axis, self.target(d, False)),
            device_id_type=MESH,
        )

    def send_across(self, d):
        self.first(d).start()

    def take_across(self, d):
        self.first(d).wait_recv()

    def send_outer(self, d):
        self.second(d).start()

    def take_outer(self, d):
        self.second(d).wait_recv()

    def order(self):
        return list(range(1, self.outers)) + [0]

    def start(self):
        for d in self.order():
            self.send_across(d)

    def turn(self, out):
        for d in self.order():
            self.take_across(d)
            total = self.own(d) + self.stage[d].astype(jnp.float32)
            if d:
                self.send2[d - 1] = total.astype(jnp.bfloat16)
                self.send_outer(d)
            else:
                self.write(out, total, False)

    def write(self, out, total, add):
        at = pl.ds(0, out.shape[0]) if self.part is None else pl.ds(*self.part)
        out[at, :] = (out[at, :] + total) if add else total

    def close(self, out):
        total = None
        for d in range(1, self.outers):
            self.take_outer(d)
            piece = self.stage2[d - 1].astype(jnp.float32)
            total = piece if total is None else total + piece
        if total is not None:
            self.write(out, total, True)

    def finish(self):
        for d in range(self.outers):
            self.first(d).wait_send()
        for d in range(1, self.outers):
            self.second(d).wait_send()


def parts_of(rows, pieces):
    size = rows // pieces
    if rows % pieces or size % 16:
        return [None]
    return [(at * size, size) for at in range(pieces)]


def scatter_scratch(count, rows, cols, dtype=jnp.bfloat16, full=False):
    outers = count // INNER
    own = [] if full else [pltpu.VMEM((outers, rows, cols), dtype)]
    return own + [
        pltpu.VMEM((outers, rows, cols), dtype),
        pltpu.VMEM((max(outers - 1, 1), rows, cols), dtype),
        pltpu.VMEM((max(outers - 1, 1), rows, cols), dtype),
        pltpu.SemaphoreType.DMA((outers,)),
        pltpu.SemaphoreType.DMA((outers,)),
        pltpu.SemaphoreType.DMA((max(outers - 1, 1),)),
        pltpu.SemaphoreType.DMA((max(outers - 1, 1),)),
    ]


def comm_params(ident, vmem_mb):
    return pltpu.CompilerParams(
        collective_id=ident, has_side_effects=True, vmem_limit_bytes=vmem_mb * 2**20
    )


def front_kernel(tp_count, fsdp_count, number, splits, *refs):
    bf16, f32 = jnp.bfloat16, jnp.float32
    refs = list(refs)

    def take(count):
        out = refs[:count]
        del refs[:count]
        return out

    tok_any, small_any = take(2)
    shards = take(number)
    n1_ref, small_ref = take(2)
    wholes = take(number)
    mixed_ref, gate_ref = take(2)
    tok_rows, gain_ref, local_sems = take(3)
    pieces = [take(2) for _ in range(2 + sum(len(split) for split in splits))]
    me_tp, me = lax.axis_index("tp"), lax.axis_index("fsdp")
    locals_ = [
        pltpu.make_async_copy(src, dst, local_sems.at[k])
        for k, (src, dst) in enumerate(
            [(tok_any, tok_rows.at[me_tp]), (small_any, small_ref.at[me])]
            + [(shard, whole.at[me]) for shard, whole in zip(shards, wholes)]
        )
    ]
    for copy in locals_:
        copy.start()
    entry_barrier([("fsdp", fsdp_count), ("tp", tp_count)])
    tok = Gather("tp", tp_count, tok_rows, pieces[0][0], pieces[0][1], own=tok_any)
    small = Gather("fsdp", fsdp_count, small_ref, pieces[1][0], pieces[1][1], own=small_any)
    groups, at = [], 2
    for shard, whole, split in zip(shards, wholes, splits):
        group = []
        for part in split:
            sems = pieces[at]
            at += 1
            group.append(
                Gather("fsdp", fsdp_count, whole, sems[0], sems[1], own=shard, part=part)
            )
        groups.append(group)
    items = [item for group in groups for item in group]
    depth = 3
    small.start()
    tok.start()
    for item in items[:depth]:
        item.start()
    small.forward_all()
    tok.forward_all()

    def pump(k):
        items[k].forward_all()
        if k + depth < len(items):
            items[k + depth].start()

    pumped = 0
    pump(0)
    pumped = 1
    small.arrive_all()
    tok.arrive_all()
    for copy in locals_:
        copy.wait()
    width = n1_ref.shape[2]
    share = width // fsdp_count
    for f in range(fsdp_count):
        gain_ref[0:1, f * share : (f + 1) * share] = small_ref[f, 0:1, 0:share]
    for b in range(tp_count):
        rows = tok_rows[b].astype(f32)
        root = lax.rsqrt(jnp.mean(rows * rows, axis=-1, keepdims=True) + 1e-06)
        n1_ref[b] = (rows * root * gain_ref[...]).astype(bf16)
        if b % 2 and pumped < len(items):
            pump(pumped)
            pumped += 1
    column = 0
    tall = tok_rows.shape[1]
    for k, (group, whole) in enumerate(zip(groups, wholes)):
        ahead = sum(len(part) for part in groups[: k + 2])
        while pumped < ahead:
            pump(pumped)
            pumped += 1
        for item in group:
            item.arrive_all()
        weight = whole[...].reshape(width, whole.shape[2])
        cols = whole.shape[2]
        for b in range(tp_count):
            product = dot_nn(n1_ref[b], weight)
            rows = pl.ds(b * tall, tall)
            if k + 1 < number:
                mixed_ref[rows, column : column + cols] = product.astype(bf16)
            else:
                gate_ref[rows, :] = product
        column += cols
    for item in [small, tok] + items:
        item.finish()


def front_all(tokens, small, shards, ident):
    tp_count, fsdp_count = lax.axis_size("tp"), lax.axis_size("fsdp")
    rows, width = tokens.shape
    f32, bf16 = jnp.float32, jnp.bfloat16
    shape = jax.ShapeDtypeStruct
    dma = pltpu.SemaphoreType.DMA
    vmem = pl.BlockSpec(memory_space=pltpu.VMEM)
    splits = [
        parts_of(shard.shape[0], 2 if shard.shape[1] > 2 * K else 1) for shard in shards
    ]
    mixed_cols = sum(shard.shape[1] for shard in shards[:-1])
    outs = (
        [
            shape((tp_count, rows, width), bf16),
            shape((fsdp_count,) + small.shape, f32),
        ]
        + [shape((fsdp_count,) + shard.shape, bf16) for shard in shards]
        + [
            shape((tp_count * rows, mixed_cols), bf16),
            shape((tp_count * rows, shards[-1].shape[1]), f32),
        ]
    )
    scratch = [
        pltpu.VMEM((tp_count, rows, width), bf16),
        pltpu.VMEM((1, width), f32),
        dma((2 + len(shards),)),
        dma((tp_count - 1,)),
        dma((tp_count,)),
    ]
    for _ in range(1 + sum(len(split) for split in splits)):
        scratch += [dma((fsdp_count - 1,)), dma((fsdp_count,))]
    return pl.pallas_call(
        functools.partial(front_kernel, tp_count, fsdp_count, len(shards), splits),
        out_shape=outs,
        in_specs=[pl.BlockSpec(memory_space=pl.ANY)] * (2 + len(shards)),
        out_specs=[vmem] * len(outs),
        scratch_shapes=scratch,
        compiler_params=comm_params(ident, 48),
        name="front",
    )(tokens, small, *shards)


def dot_nn(left, right):
    return lax.dot_general(
        left, right, (((1,), (0,)), ((), ())), preferred_element_type=jnp.float32
    )


def dot_nt(left, right):
    return lax.dot_general(
        left, right, (((1,), (1,)), ((), ())), preferred_element_type=jnp.float32
    )


def dot_tn(left, right):
    return lax.dot_general(
        left, right, (((0,), (0,)), ((), ())), preferred_element_type=jnp.float32
    )


def ffn_kernel(
    count,
    fsdp_count,
    splits,
    nm_ref,
    tok_ref,
    cot_ref,
    out_w_ref,
    gain_ref,
    cot_any,
    gate_any,
    up_any,
    down_any,
    output_ref,
    d_hidden_ref,
    d_mixer_ref,
    g_gate_ref,
    g_up_ref,
    g_down_out,
    g_out_ref,
    g_gain_ref,
    cot_rows,
    gate_w,
    up_w,
    down_w,
    n2,
    dh,
    act_s,
    dgate_s,
    dup_s,
    hidden_s,
    dact_s,
    g_down_full,
    load_sem,
    up_sem,
    n2_send,
    n2_recv,
    dh_send,
    dh_recv,
    *scatters,
):
    bf16, f32 = jnp.bfloat16, jnp.float32
    loads = [
        pltpu.make_async_copy(src, dst, load_sem.at[k])
        for k, (src, dst) in enumerate(
            ((cot_any, cot_rows), (down_any, down_w), (gate_any, gate_w))
        )
    ]
    for load in loads:
        load.start()
    up_local = pltpu.make_async_copy(up_any, up_w.at[lax.axis_index("fsdp")], up_sem)
    up_local.start()
    entry_barrier([("fsdp", fsdp_count), ("tp", count)])
    outers = count // INNER
    scatters = list(scatters)
    ups, downs = [], []
    for part in splits:
        sems = scatters[:2]
        del scatters[:2]
        ups.append(
            Gather("fsdp", fsdp_count, up_w, sems[0], sems[1], own=up_any, part=part)
        )
    for part in splits:
        s = scatters[:7]
        del scatters[:7]
        downs.append(
            Scatter(
                "fsdp", fsdp_count, None, s[0], s[1], s[2], s[3:], full=g_down_full, part=part
            )
        )
    for item in ups:
        item.start()
    sets = [scatters[8 * k : 8 * k + 8] for k in range(3)]
    mix_s, dn_s, ffn_s = [
        Scatter("tp", count, s[0], s[1], s[2], s[3], s[4:]) for s in sets
    ]
    order = list(range(1, outers)) + [0]

    for d in order:
        mix_s.out[d] = dot_nt(nm_ref[mix_s.target(d, True)], out_w_ref[...]).astype(bf16)
        mix_s.send_across(d)
    for d in order:
        part = dot_nt(nm_ref[mix_s.target(d, False)], out_w_ref[...])
        mix_s.take_across(d)
        if d:
            mix_s.send2[d - 1] = (part + mix_s.stage[d].astype(f32)).astype(bf16)
            mix_s.send_outer(d)
        else:
            hidden_s[...] = part + mix_s.stage[0].astype(f32) + tok_ref[...].astype(f32)
    loads[0].wait()
    loads[1].wait()
    for b in range(count):
        dact_s[b] = dot_nn(cot_rows[b], down_w[...])
        if b == count // 2:
            ups[0].forward_all()
    for item in ups[1:]:
        item.forward_all()
    total = hidden_s[...]
    for d in range(1, outers):
        mix_s.take_outer(d)
        total = total + mix_s.stage2[d - 1].astype(f32)
    hidden_s[...] = total
    root = lax.rsqrt(jnp.mean(total * total, axis=-1, keepdims=True) + 1e-06)
    me = mix_s.me
    n2[me] = (total * root * gain_ref[...]).astype(bf16)
    gather = Gather("tp", count, n2, n2_send, n2_recv)
    gather.start()
    loads[2].wait()
    for item in ups:
        item.arrive_all()
    up_local.wait()
    tall, hidden_cols = gate_w.shape

    def up_whole():
        return up_w[...].reshape(tall, hidden_cols)


    def block_ffn(b):
        rows = n2[b]
        gate_pre = dot_nn(rows, gate_w[...])
        up_pre = dot_nn(rows, up_whole())
        sig = jax.nn.sigmoid(gate_pre)
        silu = gate_pre * sig
        d_active = dact_s[b]
        d_gate = (d_active * up_pre * (sig + silu * (1.0 - sig))).astype(bf16)
        d_up = (d_active * silu).astype(bf16)
        dgate_s[b] = d_gate
        dup_s[b] = d_up
        act_s[b] = (silu * up_pre).astype(bf16)
        return dot_nt(d_gate, gate_w[...]) + dot_nt(d_up, up_whole())

    own_part = block_ffn(me)
    hold = {0: own_part}
    across = gather.block(0, True)
    gather.arrive(across)
    dn_s.out[0] = block_ffn(across).astype(bf16)
    dn_s.send_across(0)
    for d in range(1, outers):
        gather.forward(d)
    for d in range(1, outers):
        index = gather.block(d, True)
        gather.arrive(index)
        back = outers - d
        dn_s.out[back] = block_ffn(index).astype(bf16)
        dn_s.send_across(back)
    for d in range(1, outers):
        index = gather.block(d, False)
        back = outers - d
        part = block_ffn(index)
        dn_s.take_across(back)
        dn_s.send2[back - 1] = (part + dn_s.stage[back].astype(f32)).astype(bf16)
        dn_s.send_outer(back)
    for d in order:
        b = ffn_s.target(d, True)
        ffn_s.out[d] = dot_nt(act_s[b], down_w[...]).astype(bf16)
        ffn_s.send_across(d)
    width = n2.shape[2]
    depth = width // fsdp_count
    g_cols = max(256, depth)
    per = g_cols // depth

    def down_grad(k, carry):
        cols = pl.ds(pl.multiple_of(k * g_cols, g_cols), g_cols)
        total = dot_tn(cot_rows[0, :, cols], act_s[0])
        for b in range(1, count):
            total = total + dot_tn(cot_rows[b, :, cols], act_s[b])
        for j in range(per):
            g_down_full[k * per + j] = total[j * depth : (j + 1) * depth].astype(bf16)
        return carry

    lax.fori_loop(0, width // g_cols, down_grad, 0)
    for item in downs:
        item.start()
    dn_s.take_across(0)
    d_norm = own_part + dn_s.stage[0].astype(f32)
    for d in range(1, outers):
        dn_s.take_outer(d)
        d_norm = d_norm + dn_s.stage2[d - 1].astype(f32)
    hidden = hidden_s[...]
    root = lax.rsqrt(jnp.mean(hidden * hidden, axis=-1, keepdims=True) + 1e-06)
    scaled = hidden * root
    g_gain_ref[...] = jnp.sum(d_norm * scaled, axis=0, keepdims=True)
    pulled = d_norm * gain_ref[...]
    d_hidden = cot_ref[...].astype(f32) + root * (
        pulled - scaled * jnp.mean(pulled * scaled, axis=-1, keepdims=True)
    )
    d_hidden_ref[...] = d_hidden
    dh[me] = d_hidden.astype(bf16)
    gather2 = Gather("tp", count, dh, dh_send, dh_recv)
    gather2.start()
    for d in order:
        part = dot_nt(act_s[ffn_s.target(d, False)], down_w[...])
        ffn_s.take_across(d)
        if d:
            ffn_s.send2[d - 1] = (part + ffn_s.stage[d].astype(f32)).astype(bf16)
            ffn_s.send_outer(d)
        else:
            output_ref[...] = hidden_s[...] + part + ffn_s.stage[0].astype(f32)

    def gate_grad(k, carry):
        cols = pl.ds(pl.multiple_of(k * g_cols, g_cols), g_cols)
        gate_total = dot_tn(n2[0, :, cols], dgate_s[0])
        up_total = dot_tn(n2[0, :, cols], dup_s[0])
        for b in range(1, count):
            gate_total = gate_total + dot_tn(n2[b, :, cols], dgate_s[b])
            up_total = up_total + dot_tn(n2[b, :, cols], dup_s[b])
        g_gate_ref[cols, :] = gate_total.astype(bf16)
        g_up_ref[cols, :] = up_total.astype(bf16)
        return carry

    lax.fori_loop(0, width // g_cols, gate_grad, 0)
    for d in range(1, outers):
        gather2.forward(d)
    for item in downs:
        item.turn(g_down_out)
    for d in range(outers):
        gather2.arrive(gather2.block(d, True))
    for b in range(count):
        d_mixer_ref[b] = dot_nn(dh[b], out_w_ref[...])

    def out_grad(k, carry):
        cols = pl.ds(pl.multiple_of(k * g_cols, g_cols), g_cols)
        total = dot_tn(dh[0, :, cols], nm_ref[0])
        for b in range(1, count):
            total = total + dot_tn(dh[b, :, cols], nm_ref[b])
        g_out_ref[cols, :] = total.astype(bf16)
        return carry

    lax.fori_loop(0, width // g_cols, out_grad, 0)
    for d in range(1, outers):
        ffn_s.take_outer(d)
        output_ref[...] = output_ref[...] + ffn_s.stage2[d - 1].astype(f32)
    for item in downs:
        item.close(g_down_out)
    for part in [mix_s, gather, dn_s, ffn_s, gather2] + ups + downs:
        part.finish()


def ffn_all(nm, tokens, cotangent, out_w, gain, cot_rows, gate_w, up_w, down_w, ident):
    count, fsdp_count = lax.axis_size("tp"), lax.axis_size("fsdp")
    rows, width = tokens.shape
    depth = width // fsdp_count
    splits = parts_of(depth, 2)
    hidden = gate_w.shape[1]
    values = out_w.shape[1]
    f32, bf16 = jnp.float32, jnp.bfloat16
    vmem = pl.BlockSpec(memory_space=pltpu.VMEM)
    anys = pl.BlockSpec(memory_space=pl.ANY)
    dma = pltpu.SemaphoreType.DMA
    outs = [
        jax.ShapeDtypeStruct((rows, width), f32),
        jax.ShapeDtypeStruct((rows, width), f32),
        jax.ShapeDtypeStruct((count, rows, values), f32),
        jax.ShapeDtypeStruct((width, hidden), bf16),
        jax.ShapeDtypeStruct((width, hidden), bf16),
        jax.ShapeDtypeStruct((depth, hidden), f32),
        jax.ShapeDtypeStruct((width, values), bf16),
        jax.ShapeDtypeStruct((1, width), f32),
    ]
    scratch = [
        pltpu.VMEM((count, rows, width), bf16),
        pltpu.VMEM((width, hidden), bf16),
        pltpu.VMEM((fsdp_count, depth, hidden), bf16),
        pltpu.VMEM((width, hidden), bf16),
        pltpu.VMEM((count, rows, width), bf16),
        pltpu.VMEM((count, rows, width), bf16),
        pltpu.VMEM((count, rows, hidden), bf16),
        pltpu.VMEM((count, rows, hidden), bf16),
        pltpu.VMEM((count, rows, hidden), bf16),
        pltpu.VMEM((rows, width), f32),
        pltpu.VMEM((count, rows, hidden), f32),
        pltpu.VMEM((fsdp_count, depth, hidden), bf16),
        dma((3,)),
        dma,
        dma((count - 1,)),
        dma((count,)),
        dma((count - 1,)),
        dma((count,)),
    ]
    for _ in splits:
        scratch += [dma((fsdp_count - 1,)), dma((fsdp_count,))]
    for part in splits:
        size = depth if part is None else part[1]
        scratch += scatter_scratch(fsdp_count, size, hidden, full=True)
    for _ in range(3):
        scratch += scatter_scratch(count, rows, width)
    return pl.pallas_call(
        functools.partial(ffn_kernel, count, fsdp_count, splits),
        out_shape=outs,
        in_specs=[vmem] * 5 + [anys] * 4,
        out_specs=[vmem] * len(outs),
        scratch_shapes=scratch,
        compiler_params=comm_params(ident, 58),
        name="ffn",
    )(nm, tokens, cotangent, out_w, gain, cot_rows, gate_w, up_w, down_w)


def exchange_small(axis, count, src, buf, send, recv, spread):
    me = lax.axis_index(axis)
    copies = []
    for d in range(1, count):
        peer = lax.rem(me + d, count)
        copy = pltpu.make_async_remote_copy(
            src_ref=src.at[peer] if spread else src,
            dst_ref=buf.at[d - 1],
            send_sem=send.at[d - 1],
            recv_sem=recv.at[d - 1],
            device_id=on_axis(axis, peer),
            device_id_type=MESH,
        )
        copy.start()
        copies.append(copy)
    return copies


def last_kernel(tp_count, fsdp_count, widths, *refs):
    bf16, f32 = jnp.bfloat16, jnp.float32
    refs = list(refs)

    def take(number):
        out = refs[:number]
        del refs[:number]
        return out

    number = len(widths)
    d_raw_ref, n1_ref, tok_ref, gain_ref, d_hidden_ref, small_ref = take(6)
    weights = take(number)
    d_tok_ref, small_own_ref, small_all_ref = take(3)
    outs = take(number)
    small_send, small_buf, small_buf2 = take(3)
    small_sems = take(4)
    dn = take(8)
    fulls = take(number)
    sets = [take(7) for _ in range(number)]
    entry_barrier([("fsdp", fsdp_count), ("tp", tp_count)], everyone=True)
    dn_s = Scatter("tp", tp_count, dn[0], dn[1], dn[2], dn[3], dn[4:])
    sums = [
        Scatter("fsdp", fsdp_count, None, s[0], s[1], s[2], s[3:], full=full)
        for s, full in zip(sets, fulls)
    ]
    width = n1_ref.shape[2]
    depth = width // fsdp_count
    chunk = max(256, depth)
    per = chunk // depth
    starts = [sum(widths[:k]) for k in range(number)]

    def weight_grad(item):
        full, at, size = fulls[item], starts[item], widths[item]

        def step(k, carry):
            cols = pl.ds(pl.multiple_of(k * chunk, chunk), chunk)
            total = dot_tn(n1_ref[0, :, cols], d_raw_ref[0, :, at : at + size])
            for b in range(1, tp_count):
                total = total + dot_tn(n1_ref[b, :, cols], d_raw_ref[b, :, at : at + size])
            for j in range(per):
                full[k * per + j] = total[j * depth : (j + 1) * depth].astype(bf16)
            return carry

        lax.fori_loop(0, width // chunk, step, 0)

    def input_grad(b):
        total = None
        for item in range(number):
            at, size = starts[item], widths[item]
            weight = weights[item][...].reshape(width, size)
            piece = dot_nt(d_raw_ref[b, :, at : at + size], weight)
            total = piece if total is None else total + piece
        return total

    turns = list(reversed(range(number)))
    weight_grad(turns[0])
    sums[turns[0]].start()
    for d in dn_s.order():
        dn_s.out[d] = input_grad(dn_s.target(d, True)).astype(bf16)
        dn_s.send_across(d)
    weight_grad(turns[1])
    sums[turns[1]].start()
    held = None
    for d in dn_s.order():
        part = input_grad(dn_s.target(d, False))
        dn_s.take_across(d)
        if d:
            dn_s.send2[d - 1] = (part + dn_s.stage[d].astype(f32)).astype(bf16)
            dn_s.send_outer(d)
        else:
            held = part + dn_s.stage[0].astype(f32)
    d_tok_ref[...] = held
    sums[turns[0]].turn(outs[turns[0]])
    for k in range(2, number):
        weight_grad(turns[k])
        sums[turns[k]].start()
        sums[turns[k - 1]].turn(outs[turns[k - 1]])
    held = d_tok_ref[...]
    for d in range(1, dn_s.outers):
        dn_s.take_outer(d)
        held = held + dn_s.stage2[d - 1].astype(f32)
    tokens = tok_ref[...].astype(f32)
    root = lax.rsqrt(jnp.mean(tokens * tokens, axis=-1, keepdims=True) + 1e-06)
    scaled = tokens * root
    gain_part = jnp.sum(held * scaled, axis=0, keepdims=True)
    pulled = held * gain_ref[...]
    d_tok_ref[...] = d_hidden_ref[...] + root * (
        pulled - scaled * jnp.mean(pulled * scaled, axis=-1, keepdims=True)
    )
    small_send[...] = small_ref[...]
    for f in range(fsdp_count):
        small_send[f, 0:1, 0:depth] = gain_part[:, f * depth : (f + 1) * depth]
    copies = exchange_small(
        "fsdp", fsdp_count, small_send, small_buf, small_sems[0], small_sems[1], True
    )
    sums[turns[-1]].turn(outs[turns[-1]])
    small_sum = small_send[lax.axis_index("fsdp")]
    for d, copy in enumerate(copies):
        copy.wait_recv()
        small_sum = small_sum + small_buf[d]
    small_own_ref[...] = small_sum
    copies2 = exchange_small(
        "tp", tp_count, small_own_ref, small_buf2, small_sems[2], small_sems[3], False
    )
    for k in turns:
        sums[k].close(outs[k])
    for d, copy in enumerate(copies2):
        copy.wait_recv()
        small_sum = small_sum + small_buf2[d]
    small_all_ref[...] = small_sum
    for copy in copies + copies2:
        copy.wait_send()
    for item in [dn_s] + sums:
        item.finish()


def last_all(d_raw, n1, tokens, gain, d_hidden, small, weights, ident):
    tp_count, fsdp_count = lax.axis_size("tp"), lax.axis_size("fsdp")
    rows, width = tokens.shape
    widths = [weight.shape[2] for weight in weights]
    depth = width // fsdp_count
    f32, bf16 = jnp.float32, jnp.bfloat16
    vmem = pl.BlockSpec(memory_space=pltpu.VMEM)
    dma = pltpu.SemaphoreType.DMA
    outs = [
        jax.ShapeDtypeStruct((rows, width), f32),
        jax.ShapeDtypeStruct(small.shape[1:], f32),
        jax.ShapeDtypeStruct(small.shape[1:], f32),
    ] + [jax.ShapeDtypeStruct((depth, size), f32) for size in widths]
    scratch = [
        pltpu.VMEM(small.shape, f32),
        pltpu.VMEM((fsdp_count - 1,) + small.shape[1:], f32),
        pltpu.VMEM((tp_count - 1,) + small.shape[1:], f32),
        dma((fsdp_count - 1,)),
        dma((fsdp_count - 1,)),
        dma((tp_count - 1,)),
        dma((tp_count - 1,)),
    ]
    scratch += scatter_scratch(tp_count, rows, width)
    scratch += [pltpu.VMEM((fsdp_count, depth, size), bf16) for size in widths]
    for size in widths:
        scratch += scatter_scratch(fsdp_count, depth, size, full=True)
    return pl.pallas_call(
        functools.partial(last_kernel, tp_count, fsdp_count, widths),
        out_shape=outs,
        in_specs=[vmem] * (6 + len(weights)),
        out_specs=[vmem] * len(outs),
        scratch_shapes=scratch,
        compiler_params=comm_params(ident, 58),
        name="last",
    )(d_raw, n1, tokens, gain, d_hidden, small, *weights)


def split_two(value):
    top = value.astype(jnp.bfloat16)
    return top, (value - top.astype(jnp.float32)).astype(jnp.bfloat16)


def dot_three(left, right, dot):
    (a, b), (c, d) = split_two(left), split_two(right)
    return dot(a, c) + (dot(a, d) + dot(b, c))


def half(value):
    return value.astype(jnp.bfloat16)


def triangles():
    row = lax.broadcasted_iota(jnp.int32, (GROUP, GROUP), 0)
    col = lax.broadcasted_iota(jnp.int32, (GROUP, GROUP), 1)
    return row, col


def pair_mask(row, col, step):
    shift = step.bit_length() - 1
    high_row, high_col = row >> shift, col >> shift
    return ((high_row >> 1) == (high_col >> 1)) & (high_row > high_col)


def unit_inverses(lowers):
    row, col = triangles()
    eye = (row == col).astype(jnp.float32)
    mask = pair_mask(row, col, 1)
    inverses = [eye - jnp.where(mask, lower, 0.0) for lower in lowers]
    step = 2
    while step < GROUP:
        mask = pair_mask(row, col, step)
        corners = [half(jnp.where(mask, lower, 0.0)) for lower in lowers]
        tops = [half(inverse) for inverse in inverses]
        inner = [half(dot_nn(top, corner)) for top, corner in zip(tops, corners)]
        inverses = [
            inverse - dot_nn(left, top) for inverse, left, top in zip(inverses, inner, tops)
        ]
        step = step * 2
    rest = [
        eye - inverse - dot_three(lower, inverse, dot_nn)
        for inverse, lower in zip(inverses, lowers)
    ]
    return [
        inverse + dot_nn(half(inverse), half(gap)) for inverse, gap in zip(inverses, rest)
    ]


def conv_rows(padded, taps, ranges):
    rim = padded.shape[0] - GROUP
    total = taps[0:1] * padded[rim:]
    for lag in range(1, CONV):
        total = total + taps[lag : lag + 1] * (
            pltpu.roll(padded, lag, 0)[rim:] * ranges[lag - 1]
        )
    return total


def unit_norm(values):
    return lax.rsqrt(jnp.sum(values * values, axis=-1, keepdims=True) + 1e-06)


def soft_plus(value):
    return jnp.maximum(value, 0.0) + jnp.log1p(jnp.exp(-jnp.abs(value)))


class Chunk:
    def __init__(self, refs, head, heads, n, first_place):
        padded_ref, taps_ref, bd_ref, begin_ref, rate_ref, shift_ref = refs
        at_beta = heads * V + head
        self.head, self.n = head, n
        cols = (
            (head * K, K),
            (heads * K + head * K, K),
            (2 * heads * K + head * V, V),
        )
        self.cols = cols
        if isinstance(n, int):
            rows, padded_rows = pl.ds(n * GROUP, GROUP), pl.ds(n * GROUP, GROUP + RIM)
        else:
            start = pl.multiple_of(n * GROUP, GROUP)
            rows, padded_rows = pl.ds(start, GROUP), pl.ds(start, GROUP + RIM)
        self.rows = rows
        row, col = triangles()
        begin = begin_ref[rows, :]
        base = first_place + n * GROUP
        place = base + lax.broadcasted_iota(jnp.int32, (GROUP, 1), 0)
        self.ranges = [
            (place - lag >= begin).astype(jnp.float32) for lag in range(1, CONV)
        ]
        self.padded = [
            padded_ref[padded_rows, at : at + size].astype(jnp.float32) for at, size in cols
        ]
        self.taps = [taps_ref[:, at : at + size] for at, size in cols]
        self.pres = [
            conv_rows(padded, taps, self.ranges)
            for padded, taps in zip(self.padded, self.taps)
        ]
        self.sigs = [jax.nn.sigmoid(pre) for pre in self.pres]
        query, key, self.value = [pre * sig for pre, sig in zip(self.pres, self.sigs)]
        self.query_root, self.key_root = unit_norm(query), unit_norm(key)
        self.query = query * (self.query_root * K ** (-0.5))
        self.key = key * self.key_root
        self.beta = jax.nn.sigmoid(bd_ref[rows, at_beta : at_beta + 1])
        self.decay_in = bd_ref[rows, at_beta + heads : at_beta + heads + 1] + shift_ref[head]
        self.rate = rate_ref[head]
        decay = self.rate * soft_plus(self.decay_in)
        self.decay = decay
        lower = row >= col
        decay_row = jnp.sum(jnp.where(row == col, decay, 0.0), axis=0, keepdims=True)
        cumul = jnp.sum(jnp.where(lower, decay_row, 0.0), axis=1, keepdims=True)
        cumul_row = jnp.sum(jnp.where(row <= col, decay, 0.0), axis=0, keepdims=True)
        same = (begin <= base + col) & lower
        self.factor = jnp.where(same, jnp.exp(jnp.where(same, cumul - cumul_row, 0.0)), 0.0)
        self.carry = jnp.where(begin < base, jnp.exp(cumul), 0.0)
        self.scale = self.carry[GROUP - 1 :, :]
        last_alive = begin[GROUP - 1 :, :] <= place
        gap = cumul[GROUP - 1 :, :] - cumul
        self.last = jnp.where(last_alive, jnp.exp(jnp.where(last_alive, gap, 0.0)), 0.0)
        self.key_last = self.key * self.last
        self.weights = jnp.where(row > col, self.factor, 0.0)

    def sides(self):
        return jnp.concatenate(
            [self.beta * self.value, (self.beta * self.carry) * self.key], axis=1
        )


def mixer_kernel(heads, blocks, tp_count, fsdp_count, wide, splits, *refs):
    bf16, f32 = jnp.bfloat16, jnp.float32
    refs = list(refs)

    def take(number):
        out = refs[:number]
        del refs[:number]
        return out

    weight_count = len(splits)
    mixed_any, gate_ref, taps_ref, begin_ref, rate_ref, shift_ref, norm_ref = take(7)
    cot_any = take(1)[0]
    shards = take(weight_count)
    normed_ref, inv_ref, side_ref, query_ref, score_ref, state_ref, update_ref, out_ref = take(8)
    maps, scales, padded, pairs, cot_rows = take(5)
    wholes = take(weight_count)
    prefix, own_pair, rim_sems, load_sem, pair_send, pair_recv, cot_sems, cot_send, cot_recv = take(9)
    weight_sems = take(weight_count)
    piece_sems = [take(2) for _ in range(sum(len(split) for split in splits))]
    rows = blocks * GROUP
    mine = lax.axis_index("fsdp")
    load = pltpu.make_async_copy(mixed_any, padded.at[pl.ds(RIM, rows)], load_sem)
    load.start()
    entry_barrier([("fsdp", fsdp_count), ("tp", tp_count)], everyone=True)
    rim = pltpu.make_async_remote_copy(
        src_ref=mixed_any.at[pl.ds(rows - RIM, RIM)],
        dst_ref=padded.at[pl.ds(0, RIM)],
        send_sem=rim_sems.at[0],
        recv_sem=rim_sems.at[1],
        device_id=on_axis("fsdp", lax.rem(mine + 1, fsdp_count)),
        device_id_type=MESH,
    )
    rim.start()
    gathers, locals_ = [], []
    for k in range(weight_count):
        copy = pltpu.make_async_copy(shards[k], wholes[k].at[mine], weight_sems[k])
        copy.start()
        locals_.append(copy)
        for part in splits[k]:
            sems = piece_sems[len(gathers)]
            gathers.append(
                Gather(
                    "fsdp", fsdp_count, wholes[k], sems[0], sems[1], own=shards[k], part=part
                )
            )
    depth = 3
    for gather in gathers[:depth]:
        gather.start()
    cot = Gather("tp", tp_count, cot_rows, cot_send, cot_recv, own=cot_any)
    cot.start()
    cot_local = pltpu.make_async_copy(cot_any, cot_rows.at[cot.me], cot_sems)
    cot_local.start()
    load.wait()
    rim.wait()
    first_place = mine * rows
    source = (padded, taps_ref, gate_ref, begin_ref, rate_ref, shift_ref)
    row, col = triangles()
    turns = blocks // wide

    def pump(k):
        if k < len(gathers):
            gathers[k].forward_all()
            if k + depth < len(gathers):
                gathers[k + depth].start()

    for h in range(heads):
        own_pair[h] = jnp.concatenate(
            [(row == col).astype(f32), jnp.zeros((K, V), f32)], axis=1
        )

    def front(step, carry):
        units = [
            Chunk(source, h, heads, step * wide + j, first_place)
            for j in range(wide)
            for h in range(heads)
        ]
        lowers = [
            unit.beta * dot_three(unit.key, unit.key, dot_nt) * unit.weights for unit in units
        ]
        inverses = [half(inverse) for inverse in unit_inverses(lowers)]
        solved = [dot_nn(inv, half(unit.sides())) for inv, unit in zip(inverses, units)]
        for unit, inv, sides in zip(units, inverses, solved):
            h, n = unit.head, unit.n
            inv_ref[h, n] = inv
            side_ref[h, n] = sides
            query_ref[h, n] = half(unit.query * unit.carry)
            score_ref[h, n] = half(
                dot_nt(half(unit.query), half(unit.key)) * unit.factor
            )
            driven = dot_tn(half(unit.key_last), half(sides))
            maps[h, n] = driven[:, V:]
            scales[h, n] = jnp.broadcast_to(unit.scale, (8, 128))
            pair = own_pair[h]
            prefix[h, n] = pair
            moved = dot_three(driven[:, V:], pair, dot_nn)
            drive = jnp.concatenate([jnp.zeros((K, K), f32), driven[:, :V]], axis=1)
            own_pair[h] = unit.scale * pair + drive - moved

        return carry

    lax.fori_loop(0, turns, front, 0)
    for h in range(heads):
        pairs[mine, pl.ds(h * K, K), :] = half(own_pair[h])
    ring = Gather("fsdp", fsdp_count, pairs, pair_send, pair_recv)
    ring.start()
    cot.forward_all()
    pump(0)
    ring.forward_all()
    pump(1)
    ring.arrive_all()
    hops = min(fsdp_count - 1, -(-MAXLEN // rows))
    states = [jnp.zeros((K, V), f32) for _ in range(heads)]
    for hop in range(hops, 0, -1):
        spot = jnp.maximum(mine - hop, 0)
        for h in range(heads):
            piece = pairs[spot, pl.ds(h * K, K), :]
            top, low = split_two(states[h])
            new = dot_nn(piece[:, :K], top) + dot_nn(piece[:, :K], low)
            states[h] = jnp.where(mine >= hop, new + piece[:, K:].astype(f32), states[h])

    def back(n, carry):
        at = pl.ds(pl.multiple_of(n * GROUP, GROUP), GROUP)
        for h in range(heads):
            pair = prefix[h, n]
            start = half(dot_three(pair[:, :K], states[h], dot_nn) + pair[:, K:])
            state_ref[h, n] = start
            sides = side_ref[h, n]
            update = half(sides[:, :V] - dot_nn(half(sides[:, V:]), start))
            update_ref[h, n] = update
            out = dot_nn(query_ref[h, n], start) + dot_nn(score_ref[h, n], update)
            out_ref[h, n] = out
            gate = gate_ref[at, h * V : (h + 1) * V]
            root = lax.rsqrt(jnp.mean(out * out, axis=-1, keepdims=True) + 1e-06)
            normed_ref[at, h * V : (h + 1) * V] = half(
                out * root * norm_ref[...] * (gate * jax.nn.sigmoid(gate))
            )
        for k in range(2, len(gathers)):

            @pl.when(n == min(2 * (k - 2), blocks - 1))
            def _(k=k):
                pump(k)

        return carry

    lax.fori_loop(0, blocks, back, 0)
    cot.arrive_all()
    for gather in gathers:
        gather.arrive_all()
    for copy in locals_ + [cot_local]:
        copy.wait()
    for gather in gathers + [ring, cot]:
        gather.finish()


def mixer_all(mixed, gate, taps, begins, rate, shift, norm, cotangent, shards, ident):
    tp_count, fsdp_count = lax.axis_size("tp"), lax.axis_size("fsdp")
    heads = rate.shape[0]
    splits = [parts_of(shard.shape[0], 2) for shard in shards]
    rows = mixed.shape[0]
    blocks = rows // GROUP
    wide = 2 if blocks % 2 == 0 else 1
    f32, bf16 = jnp.float32, jnp.bfloat16
    vmem = pl.BlockSpec(memory_space=pltpu.VMEM)
    smem = pl.BlockSpec(memory_space=pltpu.SMEM)
    anys = pl.BlockSpec(memory_space=pl.ANY)
    dma = pltpu.SemaphoreType.DMA
    shape = jax.ShapeDtypeStruct
    outs = [
        shape((rows, heads * V), bf16),
        shape((heads, blocks, GROUP, GROUP), bf16),
        shape((heads, blocks, GROUP, V + K), f32),
        shape((heads, blocks, GROUP, K), bf16),
        shape((heads, blocks, GROUP, GROUP), bf16),
        shape((heads, blocks, K, V), bf16),
        shape((heads, blocks, GROUP, V), bf16),
        shape((heads, blocks, GROUP, V), f32),
        shape((heads, blocks, K, K), f32),
        shape((heads, blocks, 8, 128), f32),
        shape((rows + RIM, mixed.shape[1]), bf16),
        shape((fsdp_count, heads * K, K + V), bf16),
        shape((tp_count,) + cotangent.shape, bf16),
    ] + [shape((fsdp_count,) + shard.shape, shard.dtype) for shard in shards]
    scratch = [
        pltpu.VMEM((heads, blocks, K, K + V), f32),
        pltpu.VMEM((heads, K, K + V), f32),
        dma((2,)),
        dma,
        dma((fsdp_count - 1,)),
        dma((fsdp_count,)),
        dma,
        dma((tp_count - 1,)),
        dma((tp_count,)),
    ]
    scratch += [dma] * len(shards)
    for _ in range(sum(len(split) for split in splits)):
        scratch += [dma((fsdp_count - 1,)), dma((fsdp_count,))]
    return pl.pallas_call(
        functools.partial(
            mixer_kernel, heads, blocks, tp_count, fsdp_count, wide, splits
        ),
        out_shape=outs,
        in_specs=[anys] + [vmem] * 3 + [smem] * 2 + [vmem] + [anys] * (1 + len(shards)),
        out_specs=[vmem] * 12 + [anys] * (1 + len(shards)),
        scratch_shapes=scratch,
        compiler_params=comm_params(ident, 56),
        name="mixer",
    )(mixed, gate, taps, begins, rate, shift, norm, cotangent, *shards)


def mixer_grad_kernel(heads, blocks, tp_count, fsdp_count, splits, *refs):
    bf16, f32 = jnp.bfloat16, jnp.float32
    refs = list(refs)

    def take(number):
        out = refs[:number]
        del refs[:number]
        return out

    extra_count = len(splits)
    padded, gate_ref, taps_ref, begin_ref, rate_ref, shift_ref, norm_ref = take(7)
    inv_ref, side_ref, query_ref, score_ref, state_ref, update_ref, out_ref = take(7)
    maps, scales, pairs, dm_ref = take(4)
    extras = take(extra_count)
    d_raw_ref, g_taps_ref, g_decay_ref, g_norm_ref = take(4)
    extra_outs = take(extra_count)
    d_out, base, local, d_state, halo, tail, d_all, rim_buf = take(8)
    rim_sems, ring_send, ring_recv = take(3)
    rows = blocks * GROUP
    mine = lax.axis_index("fsdp")
    first_place = mine * rows
    mixed_cols = 2 * heads * K + heads * V
    entry_barrier([("fsdp", fsdp_count)], everyone=True)
    sums, sum_outs = [], []
    for extra, out, split in zip(extras, extra_outs, splits):
        for part in split:
            s = take(7)
            sums.append(
                Scatter(
                    "fsdp", fsdp_count, None, s[0], s[1], s[2], s[3:], full=extra, part=part
                )
            )
            sum_outs.append(out)
    depth = 3
    for item in sums[:depth]:
        item.start()

    def pump(k):
        if k < len(sums):
            if k + depth < len(sums):
                sums[k + depth].start()
            sums[k].turn(sum_outs[k])

    g_norm_ref[...] = jnp.zeros_like(g_norm_ref)
    g_taps_ref[...] = jnp.zeros_like(g_taps_ref)
    g_decay_ref[...] = jnp.zeros_like(g_decay_ref)
    halo[...] = jnp.zeros_like(halo)
    source = (padded, taps_ref, gate_ref, begin_ref, rate_ref, shift_ref)
    row, col = triangles()

    def first(n, carry):
        at = pl.ds(pl.multiple_of(n * GROUP, GROUP), GROUP)
        for h in range(heads):
            cols = slice(h * V, (h + 1) * V)
            out = out_ref[h, n]
            root = lax.rsqrt(jnp.mean(out * out, axis=-1, keepdims=True) + 1e-06)
            normed = out * root
            gate = gate_ref[at, cols]
            sig = jax.nn.sigmoid(gate)
            silu = gate * sig
            given = dm_ref[at, cols]
            g_norm_ref[...] += jnp.sum(given * normed * silu, axis=0, keepdims=True)
            pulled = given * norm_ref[...]
            d_raw_ref[at, mixed_cols + h * V : mixed_cols + (h + 1) * V] = half(
                pulled * normed * (sig + silu * (1.0 - sig))
            )
            pulled = pulled * silu
            grad = root * (pulled - normed * jnp.mean(pulled * normed, axis=-1, keepdims=True))
            grad = half(grad)
            d_out[h, n] = grad
            through = dot_tn(score_ref[h, n], grad)
            base[h, n] = through
            key_part = half(side_ref[h, n][:, V:])
            local[h, n] = dot_tn(query_ref[h, n], grad) - dot_tn(key_part, half(through))
        return carry

    lax.fori_loop(0, blocks, first, 0)
    pump(0)

    def pull_state(n, h, grad):
        scale = scales[h, n][0:1, 0:1]
        return scale * grad + local[h, n] - dot_three(maps[h, n], grad, dot_tn)

    for h in range(heads):
        d_state[h] = jnp.zeros((K, V), f32)

    def chain(step, carry):
        n = blocks - 1 - step
        for h in range(heads):
            d_state[h] = pull_state(n, h, d_state[h])
        return carry

    lax.fori_loop(0, blocks, chain, 0)
    for h in range(heads):
        d_all[mine, pl.ds(h * K, K), :] = half(d_state[h])
    ring = Gather("fsdp", fsdp_count, d_all, ring_send, ring_recv)
    ring.start()
    pump(1)
    ring.forward_all()
    pump(2)
    ring.arrive_all()
    hops = min(fsdp_count - 1, -(-MAXLEN // rows))
    for h in range(heads):
        grad = jnp.zeros((K, V), f32)
        for hop in range(hops, 0, -1):
            spot = jnp.minimum(mine + hop, fsdp_count - 1)
            piece = pairs[spot, pl.ds(h * K, K), :][:, :K]
            top, low = split_two(grad)
            new = dot_tn(piece, top) + dot_tn(piece, low)
            new = new + d_all[spot, pl.ds(h * K, K), :].astype(f32)
            grad = jnp.where(mine + hop < fsdp_count, new, grad)
        d_state[h] = grad

    def second(step, carry):
        n = blocks - 1 - step
        at = pl.ds(pl.multiple_of(n * GROUP, GROUP), GROUP)
        lane = lax.broadcasted_iota(jnp.int32, (1, g_decay_ref.shape[1]), 1)
        smalls = []
        for h in range(heads):
            unit = Chunk(source, h, heads, n, first_place)
            query, key, key_last = half(unit.query), half(unit.key), half(unit.key_last)
            after = d_state[h]
            d_state[h] = pull_state(n, h, after)
            after_half = half(after)
            state, grad, update = state_ref[h, n], d_out[h, n], update_ref[h, n]
            sides = side_ref[h, n]
            d_update = half(base[h, n] + dot_nn(key_last, after_half))
            d_key_part = -dot_nt(d_update, state)
            read = dot_nt(grad, state)
            d_query = unit.carry * read
            d_carry = jnp.sum(read * unit.query, axis=1, keepdims=True)
            d_scores = dot_nt(grad, update)
            d_key_last = dot_nt(update, after_half)
            d_scale = jnp.sum(
                jnp.sum(after * state.astype(f32), axis=1, keepdims=True), axis=0, keepdims=True
            )
            d_sides = dot_tn(
                inv_ref[h, n], jnp.concatenate([d_update, half(d_key_part)], axis=1)
            )
            d_lower = -dot_nt(half(d_sides), half(sides))
            gram = dot_nt(key, key) * unit.weights
            pulled = d_lower * gram
            d_beta = jnp.sum(pulled, axis=1, keepdims=True)
            moved = unit.beta * pulled + d_scores * score_ref[h, n].astype(f32)
            d_gram = half(d_lower * (unit.beta * unit.weights))
            d_qk = half(d_scores * unit.factor)
            d_query = d_query + dot_nn(d_qk, key)
            d_key = dot_tn(d_qk, query) + dot_nn(d_gram, key) + dot_tn(d_gram, key)
            d_key = d_key + d_key_last * unit.last
            d_last = jnp.sum(d_key_last * unit.key_last, axis=1, keepdims=True)
            d_value_side, d_key_side = d_sides[:, :V], d_sides[:, V:]
            d_beta = d_beta + jnp.sum(d_value_side * unit.value, axis=1, keepdims=True)
            d_value = unit.beta * d_value_side
            mixed_side = jnp.sum(d_key_side * unit.key, axis=1, keepdims=True)
            d_key = d_key + (unit.beta * unit.carry) * d_key_side
            d_beta = d_beta + unit.carry * mixed_side
            d_carry = d_carry + unit.beta * mixed_side
            at_end = lax.broadcasted_iota(jnp.int32, (GROUP, 1), 0) == GROUP - 1
            d_carry = d_carry + jnp.where(at_end, d_scale, 0.0)
            d_cumul = d_carry * unit.carry - d_last
            d_cumul = d_cumul + jnp.where(
                at_end, jnp.sum(d_last, axis=0, keepdims=True), 0.0
            )
            d_cumul = d_cumul + jnp.sum(moved, axis=1, keepdims=True)
            d_row = jnp.sum(jnp.where(row == col, d_cumul, 0.0), axis=0, keepdims=True)
            d_row = d_row - jnp.sum(moved, axis=0, keepdims=True)
            d_decay = jnp.sum(jnp.where(col >= row, d_row, 0.0), axis=1, keepdims=True)
            d_decay_in = d_decay * unit.rate * jax.nn.sigmoid(unit.decay_in)
            log_sum = jnp.sum(d_decay * unit.decay, axis=0, keepdims=True)
            bias_sum = jnp.sum(d_decay_in, axis=0, keepdims=True)
            g_decay_ref[...] += jnp.where(lane == h, log_sum, 0.0) + jnp.where(
                lane == heads + h, bias_sum, 0.0
            )
            smalls.append((d_beta * unit.beta * (1.0 - unit.beta), d_decay_in))
            unscaled = unit.query * K**0.5
            d_query = d_query * K ** (-0.5)
            d_query = unit.query_root * (
                d_query - unscaled * jnp.sum(d_query * unscaled, axis=1, keepdims=True)
            )
            d_key = unit.key_root * (
                d_key - unit.key * jnp.sum(d_key * unit.key, axis=1, keepdims=True)
            )
            for part, given in enumerate((d_query, d_key, d_value)):
                start, size = unit.cols[part]
                sig, pre = unit.sigs[part], unit.pres[part]
                d_pre = given * sig * (1.0 + pre * (1.0 - sig))
                taps, spread = unit.taps[part], unit.padded[part]
                total = taps[0:1] * d_pre
                edge = jnp.zeros((RIM, size), f32)
                grads = [jnp.sum(d_pre * spread[RIM:], axis=0, keepdims=True)]
                whole = jnp.concatenate([edge, total], axis=0)
                for lag in range(1, CONV):
                    masked = d_pre * unit.ranges[lag - 1]
                    grads.append(
                        jnp.sum(
                            masked * pltpu.roll(spread, lag, 0)[RIM:], axis=0, keepdims=True
                        )
                    )
                    ext = jnp.concatenate([edge, taps[lag : lag + 1] * masked], axis=0)
                    whole = whole + pltpu.roll(ext, GROUP + RIM - lag, 0)
                for lag in range(CONV):
                    g_taps_ref[lag : lag + 1, start : start + size] += grads[lag]
                body = whole[RIM:]
                ended = body[GROUP - RIM :] + halo[:, start : start + size]
                halo[:, start : start + size] = whole[:RIM]
                body = jnp.concatenate([body[: GROUP - RIM], ended], axis=0)
                d_raw_ref[at, start : start + size] = half(body)

                @pl.when(step == 0)
                def _():
                    tail[:, start : start + size] = ended

        spot = lax.broadcasted_iota(jnp.int32, (GROUP, 2 * heads), 1)
        joined = jnp.zeros((GROUP, 2 * heads), f32)
        for h, (d_beta, d_decay_in) in enumerate(smalls):
            joined = joined + jnp.where(spot == h, d_beta, 0.0)
            joined = joined + jnp.where(spot == heads + h, d_decay_in, 0.0)
        d_raw_ref[at, mixed_cols + heads * V :] = half(joined)
        for k in range(3, len(sums)):

            @pl.when(step == min(k - 3, blocks - 1))
            def _(k=k):
                pump(k)

        return carry

    lax.fori_loop(0, blocks, second, 0)
    rim = pltpu.make_async_remote_copy(
        src_ref=halo,
        dst_ref=rim_buf,
        send_sem=rim_sems.at[0],
        recv_sem=rim_sems.at[1],
        device_id=on_axis("fsdp", lax.rem(mine + fsdp_count - 1, fsdp_count)),
        device_id_type=MESH,
    )
    rim.start()
    for item, out in zip(sums, sum_outs):
        item.close(out)
    rim.wait()
    d_raw_ref[rows - RIM : rows, 0:mixed_cols] = half(tail[...] + rim_buf[...])
    for item in sums + [ring]:
        item.finish()


def mixer_grad_all(
    padded, gate, taps, begins, rate, shift, norm, saved, pairs, d_mixer, extras, ident
):
    tp_count, fsdp_count = lax.axis_size("tp"), lax.axis_size("fsdp")
    heads = rate.shape[0]
    splits = [parts_of(extra.shape[1], 2) for extra in extras]
    rows = gate.shape[0]
    blocks = rows // GROUP
    mixed_cols = padded.shape[1]
    f32, bf16 = jnp.float32, jnp.bfloat16
    vmem = pl.BlockSpec(memory_space=pltpu.VMEM)
    smem = pl.BlockSpec(memory_space=pltpu.SMEM)
    dma = pltpu.SemaphoreType.DMA
    shape = jax.ShapeDtypeStruct
    outs = [
        shape((rows, mixed_cols + heads * V + 2 * heads), bf16),
        shape((CONV, mixed_cols), f32),
        shape((1, 128), f32),
        shape((1, V), f32),
    ] + [shape(extra.shape[1:], f32) for extra in extras]
    scratch = [
        pltpu.VMEM((heads, blocks, GROUP, V), bf16),
        pltpu.VMEM((heads, blocks, GROUP, V), f32),
        pltpu.VMEM((heads, blocks, K, V), f32),
        pltpu.VMEM((heads, K, V), f32),
        pltpu.VMEM((RIM, mixed_cols), f32),
        pltpu.VMEM((RIM, mixed_cols), f32),
        pltpu.VMEM((fsdp_count, heads * K, V), bf16),
        pltpu.VMEM((RIM, mixed_cols), f32),
        dma((2,)),
        dma((fsdp_count - 1,)),
        dma((fsdp_count,)),
    ]
    for extra, split in zip(extras, splits):
        for part in split:
            size = extra.shape[1] if part is None else part[1]
            scratch += scatter_scratch(fsdp_count, size, extra.shape[2], full=True)
    return pl.pallas_call(
        functools.partial(
            mixer_grad_kernel, heads, blocks, tp_count, fsdp_count, splits
        ),
        out_shape=outs,
        in_specs=[vmem] * 4 + [smem] * 2 + [vmem] * (12 + len(extras)),
        out_specs=[vmem] * len(outs),
        scratch_shapes=scratch,
        compiler_params=comm_params(ident, 60),
        name="mixer_grad",
    )(padded, gate, taps, begins, rate, shift, norm, *saved, pairs, d_mixer, *extras)


def shards(
    tokens,
    lengths,
    attn_gain,
    w_query,
    w_key,
    w_value,
    w_gate_out,
    w_beta,
    w_decay,
    conv_query,
    conv_key,
    conv_value,
    decay_log,
    decay_bias,
    out_gain,
    w_out,
    ffn_gain,
    w_ffn_gate,
    w_ffn_up,
    w_ffn_down,
    cotangent,
):
    count = lax.axis_size("fsdp")
    shard_rows = tokens.shape[0]
    query_cols, value_cols = w_query.shape[1], w_value.shape[1]
    hidden_cols = w_ffn_gate.shape[1]
    head_count = query_cols // K
    mixed_cols = 2 * query_cols + value_cols
    raw_cols = mixed_cols + value_cols

    tp_count = lax.axis_size("tp")
    width = tokens.shape[1]
    small_list = (attn_gain, ffn_gain, out_gain, conv_query, conv_key, conv_value)
    small = jnp.concatenate([part.astype(jnp.float32).reshape(-1) for part in small_list])
    small_width = -(-small.shape[0] // 1024) * 1024
    small = jnp.pad(small, (0, small_width - small.shape[0])).reshape(8, -1)
    gate_shard = jnp.concatenate([w_gate_out, w_beta, w_decay], axis=1)
    normed_blocks, small, *mixer_w, mixed_raw, gate_raw = front_all(
        tokens, small, [w_query, w_key, w_value, gate_shard], 0
    )
    small = small.reshape(count, -1)
    smalls, at = ([], 0)
    for part in small_list:
        piece = small[:, at : at + part.size]
        at = at + part.size
        if part.ndim == 3:
            piece = piece.reshape((count,) + part.shape).transpose(1, 2, 0, 3)
            smalls.append(piece.reshape(part.shape[0], part.shape[1], -1))
        else:
            smalls.append(piece.reshape(-1))
    gain_one, gain_two, norm_out, query_taps, key_taps, value_taps = smalls
    row_count = mixed_raw.shape[0]
    positions = lax.axis_index("fsdp") * row_count + jnp.arange(row_count, dtype=jnp.int32)
    begins = seq_begin(lengths, positions)
    taps = jnp.concatenate(
        [part.reshape(CONV, -1) for part in (query_taps, key_taps, value_taps)], axis=1
    )
    common = (
        gate_raw,
        taps,
        begins.reshape(-1, 1),
        -jnp.exp(decay_log),
        decay_bias,
        norm_out.reshape(1, -1),
    )
    normed_mixer, *saved, padded, pairs, cot_blocks, out_t, down_t, ffn_gate_w = (
        mixer_all(
            mixed_raw,
            *common,
            cotangent,
            [w_out.T, w_ffn_down.T, w_ffn_gate],
            1,
        )
    )
    out_t, ffn_gate_w, down_t = [
        part.reshape(width, -1) for part in (out_t, ffn_gate_w, down_t)
    ]
    (
        output,
        d_hidden,
        d_mixer,
        g_gate,
        g_up,
        grad_down_t,
        g_out,
        gain_two_part,
    ) = ffn_all(
        normed_mixer.reshape(tp_count, shard_rows, -1),
        tokens,
        cotangent,
        out_t,
        gain_two.reshape(1, -1),
        cot_blocks,
        ffn_gate_w,
        w_ffn_up,
        down_t,
        2,
    )
    d_mixer = d_mixer.reshape(row_count, -1)
    gain_two_part = gain_two_part.reshape(-1)

    d_raw, g_taps, g_decay, norm_out_part, *grads_ffn = mixer_grad_all(
        padded,
        *common,
        saved,
        pairs,
        d_mixer,
        [part.reshape(count, width // count, -1) for part in (g_out, g_gate, g_up)],
        3,
    )
    grad_out_t, grad_w_ffn_gate, grad_w_ffn_up = grads_ffn
    d_taps = [
        part.reshape(CONV, head_count, -1)
        for part in jnp.split(g_taps, (query_cols, 2 * query_cols), axis=1)
    ]
    decay_pair = g_decay[0, : 2 * head_count]

    def spread(taps):
        taps = taps.reshape(taps.shape[0], taps.shape[1], count, -1)
        return taps.transpose(2, 0, 1, 3).reshape(count, -1)

    small_parts = [
        gain_two_part.reshape(count, -1),
        norm_out_part.reshape(count, -1),
        spread(d_taps[0]),
        spread(d_taps[1]),
        spread(d_taps[2]),
        jnp.broadcast_to(decay_pair[None, :], (count, decay_pair.shape[0])),
    ]
    small_cat = jnp.concatenate(small_parts, axis=1)
    lanes = -(-max(small_cat.shape[1], 7 * (width // count)) // (7 * 128)) * 128
    small_cat = jnp.pad(small_cat, ((0, 0), (lanes, 7 * lanes - small_cat.shape[1])))
    d_tokens, small_own, small_all, *grads_mixer = last_all(
        d_raw.reshape(tp_count, shard_rows, -1),
        normed_blocks,
        tokens,
        gain_one.reshape(1, -1),
        d_hidden,
        small_cat.reshape(count, 8, lanes),
        mixer_w,
        4,
    )
    grad_w_ffn_down = grad_down_t.T
    grad_w_out = grad_out_t.T
    grads_w = grads_mixer[:3] + jnp.split(
        grads_mixer[3], (value_cols, value_cols + head_count), axis=1
    )
    small_cuts, at = ([], lanes)
    for part in small_parts:
        small_cuts.append(at)
        at = at + part.shape[1]
    small_cuts.append(at)
    own_parts = jnp.split(small_own.reshape(-1), small_cuts)
    all_parts = jnp.split(small_all.reshape(-1), small_cuts)
    small_out = [
        small_all[0, : width // count],
        all_parts[1],
        all_parts[2],
        own_parts[3],
        own_parts[4],
        own_parts[5],
        own_parts[6],
    ]
    return (
        output,
        d_tokens,
        small_out[0],
        *grads_w,
        small_out[3].reshape(conv_query.shape),
        small_out[4].reshape(conv_key.shape),
        small_out[5].reshape(conv_value.shape),
        small_out[6][:head_count],
        small_out[6][head_count:],
        small_out[2],
        grad_w_out,
        small_out[1],
        grad_w_ffn_gate,
        grad_w_ffn_up,
        grad_w_ffn_down,
    )


def solution(mesh):
    placed = (
        P(("fsdp", "tp"), None),
        P(),
        P("fsdp"),
        P("fsdp", "tp"),
        P("fsdp", "tp"),
        P("fsdp", "tp"),
        P("fsdp", "tp"),
        P("fsdp", "tp"),
        P("fsdp", "tp"),
        P(None, "tp", "fsdp"),
        P(None, "tp", "fsdp"),
        P(None, "tp", "fsdp"),
        P("tp"),
        P("tp"),
        P("fsdp"),
        P("tp", "fsdp"),
        P("fsdp"),
        P("fsdp", "tp"),
        P("fsdp", "tp"),
        P("tp", "fsdp"),
        P(("fsdp", "tp"), None),
    )
    return jax.shard_map(
        shards,
        mesh=mesh,
        in_specs=placed,
        out_specs=(
            P(("fsdp", "tp"), None),
            P(("fsdp", "tp"), None),
            P("fsdp"),
            P("fsdp", "tp"),
            P("fsdp", "tp"),
            P("fsdp", "tp"),
            P("fsdp", "tp"),
            P("fsdp", "tp"),
            P("fsdp", "tp"),
            P(None, "tp", "fsdp"),
            P(None, "tp", "fsdp"),
            P(None, "tp", "fsdp"),
            P("tp"),
            P("tp"),
            P("fsdp"),
            P("tp", "fsdp"),
            P("fsdp"),
            P("fsdp", "tp"),
            P("fsdp", "tp"),
            P("tp", "fsdp"),
        ),
        check_vma=False,
    )
```

```python
import functools

import jax
import jax.numpy as jnp
from jax import lax
from jax.experimental import pallas as pl
from jax.experimental.pallas import tpu as pltpu
from jax.sharding import PartitionSpec as P

K = 128
V = 256
CONV = 4
GROUP = 128
MAXLEN = 4096
RIM = 16


def mat_dot(left, right):
    return jnp.dot(left, right, preferred_element_type=jnp.float32)


def rms_scale(values, scale_gain):
    return (
        values * lax.rsqrt(jnp.mean(values * values, axis=-1, keepdims=True) + 1e-06) * scale_gain
    )


def seq_begin(lengths, positions):
    number = lengths.shape[0]
    earlier = jnp.arange(number)[None, :] < jnp.arange(number)[:, None]
    offsets = jnp.sum(jnp.where(earlier, lengths[None, :], 0), axis=1)
    chosen = jnp.where(offsets[None, :] <= positions[:, None], offsets[None, :], 0)
    return jnp.max(chosen, axis=1)


MESH = pl.DeviceIdType.MESH
INNER = 2


def on_axis(axis, index):
    return {axis: index}


def halves(axis):
    me = lax.axis_index(axis)
    return me, lax.div(me, INNER), lax.rem(me, INNER)


def entry_barrier(axes, everyone=False):
    barrier = pltpu.get_barrier_semaphore()
    total = 0
    for axis, count in axes:
        me, outer, inner = halves(axis)
        outers = count // INNER
        peers = [outer * INNER + (1 - inner)]
        for d in range(1, outers):
            peers.append(lax.rem(outer + d, outers) * INNER + inner)
        if everyone:
            peers = [lax.rem(me + d, count) for d in range(1, count)]
        for peer in peers:
            pl.semaphore_signal(
                barrier, inc=1, device_id=on_axis(axis, peer), device_id_type=MESH
            )
        total += len(peers)
    pl.semaphore_wait(barrier, total)


class Gather:
    def __init__(self, axis, count, buf, send, recv, own=None, part=None):
        self.axis, self.count, self.buf, self.send, self.recv = axis, count, buf, send, recv
        self.outers = count // INNER
        self.me, self.outer, self.inner = halves(axis)
        self.part = part
        if own is None:
            self.own = self.slot(self.me)
        else:
            self.own = own if part is None else own.at[pl.ds(*part)]

    def slot(self, index):
        if self.part is None:
            return self.buf.at[index]
        return self.buf.at[index, pl.ds(*self.part)]

    def block(self, d, across):
        outer = lax.rem(self.outer + self.outers - d, self.outers)
        return outer * INNER + ((1 - self.inner) if across else self.inner)

    def copy(self, d, forward):
        across = self.outer * INNER + 1 - self.inner
        if forward:
            index = self.block(d, False)
            src, target, sem = self.slot(index), across, self.outers - 1 + d
        else:
            index, src = self.me, self.own
            target = across
            if d:
                target = lax.rem(self.outer + d, self.outers) * INNER + self.inner
            sem = d
        return pltpu.make_async_remote_copy(
            src_ref=src,
            dst_ref=self.slot(index),
            send_sem=self.send.at[sem],
            recv_sem=self.recv.at[index],
            device_id=on_axis(self.axis, target),
            device_id_type=MESH,
        )

    def start(self):
        for d in list(range(1, self.outers)) + [0]:
            self.copy(d, False).start()

    def arrive(self, index):
        pltpu.make_async_remote_copy(
            src_ref=self.slot(index),
            dst_ref=self.slot(index),
            send_sem=self.send.at[0],
            recv_sem=self.recv.at[index],
            device_id=on_axis(self.axis, self.outer * INNER + 1 - self.inner),
            device_id_type=MESH,
        ).wait_recv()

    def forward(self, d):
        index = self.block(d, False)
        self.arrive(index)
        self.copy(d, True).start()
        return index

    def forward_all(self):
        for d in range(1, self.outers):
            self.forward(d)

    def arrive_all(self):
        for d in range(self.outers):
            self.arrive(self.block(d, True))

    def finish(self):
        for d in range(self.outers):
            self.copy(d, False).wait_send()
        for d in range(1, self.outers):
            self.copy(d, True).wait_send()


class Scatter:
    def __init__(self, axis, count, out, stage, send2, stage2, sems, full=None, part=None):
        self.axis, self.count, self.full, self.part = axis, count, full, part
        self.outers = count // INNER
        self.me, self.outer, self.inner = halves(axis)
        self.out, self.stage, self.send2, self.stage2 = out, stage, send2, stage2
        self.send_a, self.recv_a, self.send_b, self.recv_b = sems

    def target(self, d, across):
        outer = lax.rem(self.outer + d, self.outers)
        return outer * INNER + ((1 - self.inner) if across else self.inner)

    def own(self, d):
        if self.part is None:
            return self.full[self.target(d, False)].astype(jnp.float32)
        return self.full[self.target(d, False), pl.ds(*self.part)].astype(jnp.float32)

    def first(self, d):
        if self.full is None:
            src = self.out.at[d]
        elif self.part is None:
            src = self.full.at[self.target(d, True)]
        else:
            src = self.full.at[self.target(d, True), pl.ds(*self.part)]
        return pltpu.make_async_remote_copy(
            src_ref=src,
            dst_ref=self.stage.at[d],
            send_sem=self.send_a.at[d],
            recv_sem=self.recv_a.at[d],
            device_id=on_axis(self.axis, self.outer * INNER + 1 - self.inner),
            device_id_type=MESH,
        )

    def second(self, d):
        return pltpu.make_async_remote_copy(
            src_ref=self.send2.at[d - 1],
            dst_ref=self.stage2.at[d - 1],
            send_sem=self.send_b.at[d - 1],
            recv_sem=self.recv_b.at[d - 1],
            device_id=on_axis(self.axis, self.target(d, False)),
            device_id_type=MESH,
        )

    def send_across(self, d):
        self.first(d).start()

    def take_across(self, d):
        self.first(d).wait_recv()

    def send_outer(self, d):
        self.second(d).start()

    def take_outer(self, d):
        self.second(d).wait_recv()

    def order(self):
        return list(range(1, self.outers)) + [0]

    def start(self):
        for d in self.order():
            self.send_across(d)

    def turn(self, out):
        for d in self.order():
            self.take_across(d)
            total = self.own(d) + self.stage[d].astype(jnp.float32)
            if d:
                self.send2[d - 1] = total.astype(jnp.bfloat16)
                self.send_outer(d)
            else:
                self.write(out, total, False)

    def write(self, out, total, add):
        at = pl.ds(0, out.shape[0]) if self.part is None else pl.ds(*self.part)
        out[at, :] = (out[at, :] + total) if add else total

    def close(self, out):
        total = None
        for d in range(1, self.outers):
            self.take_outer(d)
            piece = self.stage2[d - 1].astype(jnp.float32)
            total = piece if total is None else total + piece
        if total is not None:
            self.write(out, total, True)

    def finish(self):
        for d in range(self.outers):
            self.first(d).wait_send()
        for d in range(1, self.outers):
            self.second(d).wait_send()


def parts_of(rows, pieces):
    size = rows // pieces
    if rows % pieces or size % 16:
        return [None]
    return [(at * size, size) for at in range(pieces)]


def scatter_scratch(count, rows, cols, dtype=jnp.bfloat16, full=False):
    outers = count // INNER
    own = [] if full else [pltpu.VMEM((outers, rows, cols), dtype)]
    return own + [
        pltpu.VMEM((outers, rows, cols), dtype),
        pltpu.VMEM((max(outers - 1, 1), rows, cols), dtype),
        pltpu.VMEM((max(outers - 1, 1), rows, cols), dtype),
        pltpu.SemaphoreType.DMA((outers,)),
        pltpu.SemaphoreType.DMA((outers,)),
        pltpu.SemaphoreType.DMA((max(outers - 1, 1),)),
        pltpu.SemaphoreType.DMA((max(outers - 1, 1),)),
    ]


def comm_params(ident, vmem_mb):
    return pltpu.CompilerParams(
        collective_id=ident, has_side_effects=True, vmem_limit_bytes=vmem_mb * 2**20
    )


def front_kernel(tp_count, fsdp_count, number, splits, *refs):
    bf16, f32 = jnp.bfloat16, jnp.float32
    refs = list(refs)

    def take(count):
        out = refs[:count]
        del refs[:count]
        return out

    tok_any, small_any = take(2)
    shards = take(number)
    n1_ref, small_ref = take(2)
    wholes = take(number)
    mixed_ref, gate_ref = take(2)
    tok_rows, gain_ref, local_sems = take(3)
    pieces = [take(2) for _ in range(2 + sum(len(split) for split in splits))]
    me_tp, me = lax.axis_index("tp"), lax.axis_index("fsdp")
    locals_ = [
        pltpu.make_async_copy(src, dst, local_sems.at[k])
        for k, (src, dst) in enumerate(
            [(tok_any, tok_rows.at[me_tp]), (small_any, small_ref.at[me])]
            + [(shard, whole.at[me]) for shard, whole in zip(shards, wholes)]
        )
    ]
    for copy in locals_:
        copy.start()
    entry_barrier([("fsdp", fsdp_count), ("tp", tp_count)])
    tok = Gather("tp", tp_count, tok_rows, pieces[0][0], pieces[0][1], own=tok_any)
    small = Gather("fsdp", fsdp_count, small_ref, pieces[1][0], pieces[1][1], own=small_any)
    groups, at = [], 2
    for shard, whole, split in zip(shards, wholes, splits):
        group = []
        for part in split:
            sems = pieces[at]
            at += 1
            group.append(
                Gather("fsdp", fsdp_count, whole, sems[0], sems[1], own=shard, part=part)
            )
        groups.append(group)
    items = [item for group in groups for item in group]
    depth = 3
    small.start()
    tok.start()
    for item in items[:depth]:
        item.start()
    small.forward_all()
    tok.forward_all()

    def pump(k):
        items[k].forward_all()
        if k + depth < len(items):
            items[k + depth].start()

    pumped = 0
    pump(0)
    pumped = 1
    small.arrive_all()
    tok.arrive_all()
    for copy in locals_:
        copy.wait()
    width = n1_ref.shape[2]
    share = width // fsdp_count
    for f in range(fsdp_count):
        gain_ref[0:1, f * share : (f + 1) * share] = small_ref[f, 0:1, 0:share]
    for b in range(tp_count):
        rows = tok_rows[b].astype(f32)
        root = lax.rsqrt(jnp.mean(rows * rows, axis=-1, keepdims=True) + 1e-06)
        n1_ref[b] = (rows * root * gain_ref[...]).astype(bf16)
        if b % 2 and pumped < len(items):
            pump(pumped)
            pumped += 1
    column = 0
    tall = tok_rows.shape[1]
    for k, (group, whole) in enumerate(zip(groups, wholes)):
        ahead = sum(len(part) for part in groups[: k + 2])
        while pumped < ahead:
            pump(pumped)
            pumped += 1
        for item in group:
            item.arrive_all()
        weight = whole[...].reshape(width, whole.shape[2])
        cols = whole.shape[2]
        for b in range(tp_count):
            product = dot_nn(n1_ref[b], weight)
            rows = pl.ds(b * tall, tall)
            if k + 1 < number:
                mixed_ref[rows, column : column + cols] = product.astype(bf16)
            else:
                gate_ref[rows, :] = product
        column += cols
    for item in [small, tok] + items:
        item.finish()


def front_all(tokens, small, shards, ident):
    tp_count, fsdp_count = lax.axis_size("tp"), lax.axis_size("fsdp")
    rows, width = tokens.shape
    f32, bf16 = jnp.float32, jnp.bfloat16
    shape = jax.ShapeDtypeStruct
    dma = pltpu.SemaphoreType.DMA
    vmem = pl.BlockSpec(memory_space=pltpu.VMEM)
    splits = [
        parts_of(shard.shape[0], 2 if shard.shape[1] > 2 * K else 1) for shard in shards
    ]
    mixed_cols = sum(shard.shape[1] for shard in shards[:-1])
    outs = (
        [
            shape((tp_count, rows, width), bf16),
            shape((fsdp_count,) + small.shape, f32),
        ]
        + [shape((fsdp_count,) + shard.shape, bf16) for shard in shards]
        + [
            shape((tp_count * rows, mixed_cols), bf16),
            shape((tp_count * rows, shards[-1].shape[1]), f32),
        ]
    )
    scratch = [
        pltpu.VMEM((tp_count, rows, width), bf16),
        pltpu.VMEM((1, width), f32),
        dma((2 + len(shards),)),
        dma((tp_count - 1,)),
        dma((tp_count,)),
    ]
    for _ in range(1 + sum(len(split) for split in splits)):
        scratch += [dma((fsdp_count - 1,)), dma((fsdp_count,))]
    return pl.pallas_call(
        functools.partial(front_kernel, tp_count, fsdp_count, len(shards), splits),
        out_shape=outs,
        in_specs=[pl.BlockSpec(memory_space=pl.ANY)] * (2 + len(shards)),
        out_specs=[vmem] * len(outs),
        scratch_shapes=scratch,
        compiler_params=comm_params(ident, 60),
        name="front",
    )(tokens, small, *shards)


def dot_nn(left, right):
    return lax.dot_general(
        left, right, (((1,), (0,)), ((), ())), preferred_element_type=jnp.float32
    )


def dot_nt(left, right):
    return lax.dot_general(
        left, right, (((1,), (1,)), ((), ())), preferred_element_type=jnp.float32
    )


def dot_tn(left, right):
    return lax.dot_general(
        left, right, (((0,), (0,)), ((), ())), preferred_element_type=jnp.float32
    )


def ffn_kernel(
    count,
    fsdp_count,
    splits,
    nm_ref,
    tok_ref,
    cot_ref,
    out_w_ref,
    gain_ref,
    cot_any,
    gate_any,
    up_any,
    down_any,
    output_ref,
    d_hidden_ref,
    d_mixer_ref,
    g_gate_ref,
    g_up_ref,
    g_down_out,
    g_out_ref,
    g_gain_ref,
    cot_rows,
    gate_w,
    up_w,
    down_w,
    n2,
    dh,
    act_s,
    dgate_s,
    dup_s,
    hidden_s,
    dact_s,
    g_down_full,
    load_sem,
    up_sem,
    n2_send,
    n2_recv,
    dh_send,
    dh_recv,
    *scatters,
):
    bf16, f32 = jnp.bfloat16, jnp.float32
    loads = [
        pltpu.make_async_copy(src, dst, load_sem.at[k])
        for k, (src, dst) in enumerate(
            ((cot_any, cot_rows), (down_any, down_w), (gate_any, gate_w))
        )
    ]
    for load in loads:
        load.start()
    up_local = pltpu.make_async_copy(up_any, up_w.at[lax.axis_index("fsdp")], up_sem)
    up_local.start()
    entry_barrier([("fsdp", fsdp_count), ("tp", count)])
    outers = count // INNER
    scatters = list(scatters)
    ups, downs = [], []
    for part in splits:
        sems = scatters[:2]
        del scatters[:2]
        ups.append(
            Gather("fsdp", fsdp_count, up_w, sems[0], sems[1], own=up_any, part=part)
        )
    for part in splits:
        s = scatters[:7]
        del scatters[:7]
        downs.append(
            Scatter(
                "fsdp", fsdp_count, None, s[0], s[1], s[2], s[3:], full=g_down_full, part=part
            )
        )
    for item in ups:
        item.start()
    sets = [scatters[8 * k : 8 * k + 8] for k in range(3)]
    mix_s, dn_s, ffn_s = [
        Scatter("tp", count, s[0], s[1], s[2], s[3], s[4:]) for s in sets
    ]
    order = list(range(1, outers)) + [0]

    for d in order:
        mix_s.out[d] = dot_nt(nm_ref[mix_s.target(d, True)], out_w_ref[...]).astype(bf16)
        mix_s.send_across(d)
    for d in order:
        part = dot_nt(nm_ref[mix_s.target(d, False)], out_w_ref[...])
        mix_s.take_across(d)
        if d:
            mix_s.send2[d - 1] = (part + mix_s.stage[d].astype(f32)).astype(bf16)
            mix_s.send_outer(d)
        else:
            hidden_s[...] = part + mix_s.stage[0].astype(f32) + tok_ref[...].astype(f32)
    loads[0].wait()
    loads[1].wait()
    for b in range(count):
        dact_s[b] = dot_nn(cot_rows[b], down_w[...])
        if b == count // 2:
            ups[0].forward_all()
    for item in ups[1:]:
        item.forward_all()
    total = hidden_s[...]
    for d in range(1, outers):
        mix_s.take_outer(d)
        total = total + mix_s.stage2[d - 1].astype(f32)
    hidden_s[...] = total
    root = lax.rsqrt(jnp.mean(total * total, axis=-1, keepdims=True) + 1e-06)
    me = mix_s.me
    n2[me] = (total * root * gain_ref[...]).astype(bf16)
    gather = Gather("tp", count, n2, n2_send, n2_recv)
    gather.start()
    loads[2].wait()
    for item in ups:
        item.arrive_all()
    up_local.wait()
    tall, hidden_cols = gate_w.shape

    def up_whole():
        return up_w[...].reshape(tall, hidden_cols)


    def block_ffn(b):
        rows = n2[b]
        gate_pre = dot_nn(rows, gate_w[...])
        up_pre = dot_nn(rows, up_whole())
        sig = jax.nn.sigmoid(gate_pre)
        silu = gate_pre * sig
        d_active = dact_s[b]
        d_gate = (d_active * up_pre * (sig + silu * (1.0 - sig))).astype(bf16)
        d_up = (d_active * silu).astype(bf16)
        dgate_s[b] = d_gate
        dup_s[b] = d_up
        act_s[b] = (silu * up_pre).astype(bf16)
        return dot_nt(d_gate, gate_w[...]) + dot_nt(d_up, up_whole())

    own_part = block_ffn(me)
    hold = {0: own_part}
    across = gather.block(0, True)
    gather.arrive(across)
    dn_s.out[0] = block_ffn(across).astype(bf16)
    dn_s.send_across(0)
    for d in range(1, outers):
        gather.forward(d)
    for d in range(1, outers):
        index = gather.block(d, True)
        gather.arrive(index)
        back = outers - d
        dn_s.out[back] = block_ffn(index).astype(bf16)
        dn_s.send_across(back)
    for d in range(1, outers):
        index = gather.block(d, False)
        back = outers - d
        part = block_ffn(index)
        dn_s.take_across(back)
        dn_s.send2[back - 1] = (part + dn_s.stage[back].astype(f32)).astype(bf16)
        dn_s.send_outer(back)
    for d in order:
        b = ffn_s.target(d, True)
        ffn_s.out[d] = dot_nt(act_s[b], down_w[...]).astype(bf16)
        ffn_s.send_across(d)
    width = n2.shape[2]
    depth = width // fsdp_count
    g_cols = max(256, depth)
    per = g_cols // depth

    def down_grad(k, carry):
        cols = pl.ds(pl.multiple_of(k * g_cols, g_cols), g_cols)
        total = dot_tn(cot_rows[0, :, cols], act_s[0])
        for b in range(1, count):
            total = total + dot_tn(cot_rows[b, :, cols], act_s[b])
        for j in range(per):
            g_down_full[k * per + j] = total[j * depth : (j + 1) * depth].astype(bf16)
        return carry

    lax.fori_loop(0, width // g_cols, down_grad, 0)
    for item in downs:
        item.start()
    dn_s.take_across(0)
    d_norm = own_part + dn_s.stage[0].astype(f32)
    for d in range(1, outers):
        dn_s.take_outer(d)
        d_norm = d_norm + dn_s.stage2[d - 1].astype(f32)
    hidden = hidden_s[...]
    root = lax.rsqrt(jnp.mean(hidden * hidden, axis=-1, keepdims=True) + 1e-06)
    scaled = hidden * root
    g_gain_ref[...] = jnp.sum(d_norm * scaled, axis=0, keepdims=True)
    pulled = d_norm * gain_ref[...]
    d_hidden = cot_ref[...].astype(f32) + root * (
        pulled - scaled * jnp.mean(pulled * scaled, axis=-1, keepdims=True)
    )
    d_hidden_ref[...] = d_hidden
    dh[me] = d_hidden.astype(bf16)
    gather2 = Gather("tp", count, dh, dh_send, dh_recv)
    gather2.start()
    for d in order:
        part = dot_nt(act_s[ffn_s.target(d, False)], down_w[...])
        ffn_s.take_across(d)
        if d:
            ffn_s.send2[d - 1] = (part + ffn_s.stage[d].astype(f32)).astype(bf16)
            ffn_s.send_outer(d)
        else:
            output_ref[...] = hidden_s[...] + part + ffn_s.stage[0].astype(f32)
    downs[0].turn(g_down_out)

    def gate_grad(k, carry):
        cols = pl.ds(pl.multiple_of(k * g_cols, g_cols), g_cols)
        gate_total = dot_tn(n2[0, :, cols], dgate_s[0])
        up_total = dot_tn(n2[0, :, cols], dup_s[0])
        for b in range(1, count):
            gate_total = gate_total + dot_tn(n2[b, :, cols], dgate_s[b])
            up_total = up_total + dot_tn(n2[b, :, cols], dup_s[b])
        g_gate_ref[cols, :] = gate_total.astype(bf16)
        g_up_ref[cols, :] = up_total.astype(bf16)
        return carry

    lax.fori_loop(0, width // g_cols, gate_grad, 0)
    for d in range(1, outers):
        gather2.forward(d)
    for item in downs[1:]:
        item.turn(g_down_out)
    for d in range(outers):
        gather2.arrive(gather2.block(d, True))
    for b in range(count):
        d_mixer_ref[b] = dot_nn(dh[b], out_w_ref[...])

    def out_grad(k, carry):
        cols = pl.ds(pl.multiple_of(k * g_cols, g_cols), g_cols)
        total = dot_tn(dh[0, :, cols], nm_ref[0])
        for b in range(1, count):
            total = total + dot_tn(dh[b, :, cols], nm_ref[b])
        g_out_ref[cols, :] = total.astype(bf16)
        return carry

    lax.fori_loop(0, width // g_cols, out_grad, 0)
    for d in range(1, outers):
        ffn_s.take_outer(d)
        output_ref[...] = output_ref[...] + ffn_s.stage2[d - 1].astype(f32)
    for item in downs:
        item.close(g_down_out)
    for part in [mix_s, gather, dn_s, ffn_s, gather2] + ups + downs:
        part.finish()


def ffn_all(nm, tokens, cotangent, out_w, gain, cot_rows, gate_w, up_w, down_w, ident):
    count, fsdp_count = lax.axis_size("tp"), lax.axis_size("fsdp")
    rows, width = tokens.shape
    depth = width // fsdp_count
    splits = parts_of(depth, 2)
    hidden = gate_w.shape[1]
    values = out_w.shape[1]
    f32, bf16 = jnp.float32, jnp.bfloat16
    vmem = pl.BlockSpec(memory_space=pltpu.VMEM)
    anys = pl.BlockSpec(memory_space=pl.ANY)
    dma = pltpu.SemaphoreType.DMA
    outs = [
        jax.ShapeDtypeStruct((rows, width), f32),
        jax.ShapeDtypeStruct((rows, width), f32),
        jax.ShapeDtypeStruct((count, rows, values), f32),
        jax.ShapeDtypeStruct((width, hidden), bf16),
        jax.ShapeDtypeStruct((width, hidden), bf16),
        jax.ShapeDtypeStruct((depth, hidden), f32),
        jax.ShapeDtypeStruct((width, values), bf16),
        jax.ShapeDtypeStruct((1, width), f32),
    ]
    scratch = [
        pltpu.VMEM((count, rows, width), bf16),
        pltpu.VMEM((width, hidden), bf16),
        pltpu.VMEM((fsdp_count, depth, hidden), bf16),
        pltpu.VMEM((width, hidden), bf16),
        pltpu.VMEM((count, rows, width), bf16),
        pltpu.VMEM((count, rows, width), bf16),
        pltpu.VMEM((count, rows, hidden), bf16),
        pltpu.VMEM((count, rows, hidden), bf16),
        pltpu.VMEM((count, rows, hidden), bf16),
        pltpu.VMEM((rows, width), f32),
        pltpu.VMEM((count, rows, hidden), f32),
        pltpu.VMEM((fsdp_count, depth, hidden), bf16),
        dma((3,)),
        dma,
        dma((count - 1,)),
        dma((count,)),
        dma((count - 1,)),
        dma((count,)),
    ]
    for _ in splits:
        scratch += [dma((fsdp_count - 1,)), dma((fsdp_count,))]
    for part in splits:
        size = depth if part is None else part[1]
        scratch += scatter_scratch(fsdp_count, size, hidden, full=True)
    for _ in range(3):
        scratch += scatter_scratch(count, rows, width)
    return pl.pallas_call(
        functools.partial(ffn_kernel, count, fsdp_count, splits),
        out_shape=outs,
        in_specs=[vmem] * 5 + [anys] * 4,
        out_specs=[vmem] * len(outs),
        scratch_shapes=scratch,
        compiler_params=comm_params(ident, 60),
        name="ffn",
    )(nm, tokens, cotangent, out_w, gain, cot_rows, gate_w, up_w, down_w)


def exchange_small(axis, count, src, buf, send, recv, spread):
    me = lax.axis_index(axis)
    copies = []
    for d in range(1, count):
        peer = lax.rem(me + d, count)
        copy = pltpu.make_async_remote_copy(
            src_ref=src.at[peer] if spread else src,
            dst_ref=buf.at[d - 1],
            send_sem=send.at[d - 1],
            recv_sem=recv.at[d - 1],
            device_id=on_axis(axis, peer),
            device_id_type=MESH,
        )
        copy.start()
        copies.append(copy)
    return copies


def last_kernel(tp_count, fsdp_count, widths, *refs):
    bf16, f32 = jnp.bfloat16, jnp.float32
    refs = list(refs)

    def take(number):
        out = refs[:number]
        del refs[:number]
        return out

    number = len(widths)
    d_raw_ref, n1_ref, tok_ref, gain_ref, d_hidden_ref, small_ref = take(6)
    weights = take(number)
    d_tok_ref, small_own_ref, small_all_ref = take(3)
    outs = take(number)
    small_send, small_buf, small_buf2 = take(3)
    small_sems = take(4)
    dn = take(8)
    fulls = take(number)
    sets = [take(7) for _ in range(number)]
    entry_barrier([("fsdp", fsdp_count), ("tp", tp_count)], everyone=True)
    dn_s = Scatter("tp", tp_count, dn[0], dn[1], dn[2], dn[3], dn[4:])
    sums = [
        Scatter("fsdp", fsdp_count, None, s[0], s[1], s[2], s[3:], full=full)
        for s, full in zip(sets, fulls)
    ]
    width = n1_ref.shape[2]
    depth = width // fsdp_count
    chunk = max(256, depth)
    per = chunk // depth
    starts = [sum(widths[:k]) for k in range(number)]

    def weight_grad(item):
        full, at, size = fulls[item], starts[item], widths[item]

        def step(k, carry):
            cols = pl.ds(pl.multiple_of(k * chunk, chunk), chunk)
            total = dot_tn(n1_ref[0, :, cols], d_raw_ref[0, :, at : at + size])
            for b in range(1, tp_count):
                total = total + dot_tn(n1_ref[b, :, cols], d_raw_ref[b, :, at : at + size])
            for j in range(per):
                full[k * per + j] = total[j * depth : (j + 1) * depth].astype(bf16)
            return carry

        lax.fori_loop(0, width // chunk, step, 0)

    def input_grad(b):
        total = None
        for item in range(number):
            at, size = starts[item], widths[item]
            weight = weights[item][...].reshape(width, size)
            piece = dot_nt(d_raw_ref[b, :, at : at + size], weight)
            total = piece if total is None else total + piece
        return total

    turns = list(reversed(range(number)))
    weight_grad(turns[0])
    sums[turns[0]].start()
    for d in dn_s.order():
        dn_s.out[d] = input_grad(dn_s.target(d, True)).astype(bf16)
        dn_s.send_across(d)
    weight_grad(turns[1])
    sums[turns[1]].start()
    held = None
    for d in dn_s.order():
        part = input_grad(dn_s.target(d, False))
        dn_s.take_across(d)
        if d:
            dn_s.send2[d - 1] = (part + dn_s.stage[d].astype(f32)).astype(bf16)
            dn_s.send_outer(d)
        else:
            held = part + dn_s.stage[0].astype(f32)
    d_tok_ref[...] = held
    sums[turns[0]].turn(outs[turns[0]])
    for k in range(2, number):
        weight_grad(turns[k])
        sums[turns[k]].start()
        sums[turns[k - 1]].turn(outs[turns[k - 1]])
    held = d_tok_ref[...]
    for d in range(1, dn_s.outers):
        dn_s.take_outer(d)
        held = held + dn_s.stage2[d - 1].astype(f32)
    tokens = tok_ref[...].astype(f32)
    root = lax.rsqrt(jnp.mean(tokens * tokens, axis=-1, keepdims=True) + 1e-06)
    scaled = tokens * root
    gain_part = jnp.sum(held * scaled, axis=0, keepdims=True)
    pulled = held * gain_ref[...]
    d_tok_ref[...] = d_hidden_ref[...] + root * (
        pulled - scaled * jnp.mean(pulled * scaled, axis=-1, keepdims=True)
    )
    small_send[...] = small_ref[...]
    for f in range(fsdp_count):
        small_send[f, 0:1, 0:depth] = gain_part[:, f * depth : (f + 1) * depth]
    copies = exchange_small(
        "fsdp", fsdp_count, small_send, small_buf, small_sems[0], small_sems[1], True
    )
    sums[turns[-1]].turn(outs[turns[-1]])
    small_sum = small_send[lax.axis_index("fsdp")]
    for d, copy in enumerate(copies):
        copy.wait_recv()
        small_sum = small_sum + small_buf[d]
    small_own_ref[...] = small_sum
    copies2 = exchange_small(
        "tp", tp_count, small_own_ref, small_buf2, small_sems[2], small_sems[3], False
    )
    for k in turns:
        sums[k].close(outs[k])
    for d, copy in enumerate(copies2):
        copy.wait_recv()
        small_sum = small_sum + small_buf2[d]
    small_all_ref[...] = small_sum
    for copy in copies + copies2:
        copy.wait_send()
    for item in [dn_s] + sums:
        item.finish()


def last_all(d_raw, n1, tokens, gain, d_hidden, small, weights, ident):
    tp_count, fsdp_count = lax.axis_size("tp"), lax.axis_size("fsdp")
    rows, width = tokens.shape
    widths = [weight.shape[2] for weight in weights]
    depth = width // fsdp_count
    f32, bf16 = jnp.float32, jnp.bfloat16
    vmem = pl.BlockSpec(memory_space=pltpu.VMEM)
    dma = pltpu.SemaphoreType.DMA
    outs = [
        jax.ShapeDtypeStruct((rows, width), f32),
        jax.ShapeDtypeStruct(small.shape[1:], f32),
        jax.ShapeDtypeStruct(small.shape[1:], f32),
    ] + [jax.ShapeDtypeStruct((depth, size), f32) for size in widths]
    scratch = [
        pltpu.VMEM(small.shape, f32),
        pltpu.VMEM((fsdp_count - 1,) + small.shape[1:], f32),
        pltpu.VMEM((tp_count - 1,) + small.shape[1:], f32),
        dma((fsdp_count - 1,)),
        dma((fsdp_count - 1,)),
        dma((tp_count - 1,)),
        dma((tp_count - 1,)),
    ]
    scratch += scatter_scratch(tp_count, rows, width)
    scratch += [pltpu.VMEM((fsdp_count, depth, size), bf16) for size in widths]
    for size in widths:
        scratch += scatter_scratch(fsdp_count, depth, size, full=True)
    return pl.pallas_call(
        functools.partial(last_kernel, tp_count, fsdp_count, widths),
        out_shape=outs,
        in_specs=[vmem] * (6 + len(weights)),
        out_specs=[vmem] * len(outs),
        scratch_shapes=scratch,
        compiler_params=comm_params(ident, 60),
        name="last",
    )(d_raw, n1, tokens, gain, d_hidden, small, *weights)


def split_two(value):
    top = value.astype(jnp.bfloat16)
    return top, (value - top.astype(jnp.float32)).astype(jnp.bfloat16)


def dot_three(left, right, dot):
    (a, b), (c, d) = split_two(left), split_two(right)
    return dot(a, c) + (dot(a, d) + dot(b, c))


def half(value):
    return value.astype(jnp.bfloat16)


def triangles():
    row = lax.broadcasted_iota(jnp.int32, (GROUP, GROUP), 0)
    col = lax.broadcasted_iota(jnp.int32, (GROUP, GROUP), 1)
    return row, col


def pair_mask(row, col, step):
    shift = step.bit_length() - 1
    high_row, high_col = row >> shift, col >> shift
    return ((high_row >> 1) == (high_col >> 1)) & (high_row > high_col)


def unit_inverses(lowers):
    row, col = triangles()
    eye = (row == col).astype(jnp.float32)
    mask = pair_mask(row, col, 1)
    inverses = [eye - jnp.where(mask, lower, 0.0) for lower in lowers]
    step = 2
    while step < GROUP:
        mask = pair_mask(row, col, step)
        corners = [half(jnp.where(mask, lower, 0.0)) for lower in lowers]
        tops = [half(inverse) for inverse in inverses]
        inner = [half(dot_nn(top, corner)) for top, corner in zip(tops, corners)]
        inverses = [
            inverse - dot_nn(left, top) for inverse, left, top in zip(inverses, inner, tops)
        ]
        step = step * 2
    rest = [
        eye - inverse - dot_three(lower, inverse, dot_nn)
        for inverse, lower in zip(inverses, lowers)
    ]
    return [
        inverse + dot_nn(half(inverse), half(gap)) for inverse, gap in zip(inverses, rest)
    ]


def conv_rows(padded, taps, ranges):
    rim = padded.shape[0] - GROUP
    total = taps[0:1] * padded[rim:]
    for lag in range(1, CONV):
        total = total + taps[lag : lag + 1] * (
            pltpu.roll(padded, lag, 0)[rim:] * ranges[lag - 1]
        )
    return total


def unit_norm(values):
    return lax.rsqrt(jnp.sum(values * values, axis=-1, keepdims=True) + 1e-06)


def soft_plus(value):
    return jnp.maximum(value, 0.0) + jnp.log1p(jnp.exp(-jnp.abs(value)))


class Chunk:
    def __init__(self, refs, head, heads, n, first_place):
        padded_ref, taps_ref, bd_ref, begin_ref, rate_ref, shift_ref = refs
        at_beta = heads * V + head
        self.head, self.n = head, n
        cols = (
            (head * K, K),
            (heads * K + head * K, K),
            (2 * heads * K + head * V, V),
        )
        self.cols = cols
        if isinstance(n, int):
            rows, padded_rows = pl.ds(n * GROUP, GROUP), pl.ds(n * GROUP, GROUP + RIM)
        else:
            start = pl.multiple_of(n * GROUP, GROUP)
            rows, padded_rows = pl.ds(start, GROUP), pl.ds(start, GROUP + RIM)
        self.rows = rows
        row, col = triangles()
        begin = begin_ref[rows, :]
        base = first_place + n * GROUP
        place = base + lax.broadcasted_iota(jnp.int32, (GROUP, 1), 0)
        self.ranges = [
            (place - lag >= begin).astype(jnp.float32) for lag in range(1, CONV)
        ]
        self.padded = [
            padded_ref[padded_rows, at : at + size].astype(jnp.float32) for at, size in cols
        ]
        self.taps = [taps_ref[:, at : at + size] for at, size in cols]
        self.pres = [
            conv_rows(padded, taps, self.ranges)
            for padded, taps in zip(self.padded, self.taps)
        ]
        self.sigs = [jax.nn.sigmoid(pre) for pre in self.pres]
        query, key, self.value = [pre * sig for pre, sig in zip(self.pres, self.sigs)]
        self.query_root, self.key_root = unit_norm(query), unit_norm(key)
        self.query = query * (self.query_root * K ** (-0.5))
        self.key = key * self.key_root
        self.beta = jax.nn.sigmoid(bd_ref[rows, at_beta : at_beta + 1])
        self.decay_in = bd_ref[rows, at_beta + heads : at_beta + heads + 1] + shift_ref[head]
        self.rate = rate_ref[head]
        decay = self.rate * soft_plus(self.decay_in)
        self.decay = decay
        lower = row >= col
        decay_row = jnp.sum(jnp.where(row == col, decay, 0.0), axis=0, keepdims=True)
        cumul = jnp.sum(jnp.where(lower, decay_row, 0.0), axis=1, keepdims=True)
        cumul_row = jnp.sum(jnp.where(row <= col, decay, 0.0), axis=0, keepdims=True)
        same = (begin <= base + col) & lower
        self.factor = jnp.where(same, jnp.exp(jnp.where(same, cumul - cumul_row, 0.0)), 0.0)
        self.carry = jnp.where(begin < base, jnp.exp(cumul), 0.0)
        self.scale = self.carry[GROUP - 1 :, :]
        last_alive = begin[GROUP - 1 :, :] <= place
        gap = cumul[GROUP - 1 :, :] - cumul
        self.last = jnp.where(last_alive, jnp.exp(jnp.where(last_alive, gap, 0.0)), 0.0)
        self.key_last = self.key * self.last
        self.weights = jnp.where(row > col, self.factor, 0.0)

    def sides(self):
        return jnp.concatenate(
            [self.beta * self.value, (self.beta * self.carry) * self.key], axis=1
        )


def mixer_kernel(heads, blocks, tp_count, fsdp_count, wide, splits, *refs):
    bf16, f32 = jnp.bfloat16, jnp.float32
    refs = list(refs)

    def take(number):
        out = refs[:number]
        del refs[:number]
        return out

    weight_count = len(splits)
    mixed_any, gate_ref, taps_ref, begin_ref, rate_ref, shift_ref, norm_ref = take(7)
    cot_any = take(1)[0]
    shards = take(weight_count)
    normed_ref, inv_ref, side_ref, query_ref, score_ref, state_ref, update_ref, out_ref = take(8)
    maps, scales, padded, pairs, cot_rows = take(5)
    wholes = take(weight_count)
    prefix, own_pair, rim_sems, load_sem, pair_send, pair_recv, cot_sems, cot_send, cot_recv = take(9)
    weight_sems = take(weight_count)
    piece_sems = [take(2) for _ in range(sum(len(split) for split in splits))]
    rows = blocks * GROUP
    mine = lax.axis_index("fsdp")
    load = pltpu.make_async_copy(mixed_any, padded.at[pl.ds(RIM, rows)], load_sem)
    load.start()
    entry_barrier([("fsdp", fsdp_count), ("tp", tp_count)], everyone=True)
    rim = pltpu.make_async_remote_copy(
        src_ref=mixed_any.at[pl.ds(rows - RIM, RIM)],
        dst_ref=padded.at[pl.ds(0, RIM)],
        send_sem=rim_sems.at[0],
        recv_sem=rim_sems.at[1],
        device_id=on_axis("fsdp", lax.rem(mine + 1, fsdp_count)),
        device_id_type=MESH,
    )
    rim.start()
    gathers, locals_ = [], []
    for k in range(weight_count):
        copy = pltpu.make_async_copy(shards[k], wholes[k].at[mine], weight_sems[k])
        copy.start()
        locals_.append(copy)
        for part in splits[k]:
            sems = piece_sems[len(gathers)]
            gathers.append(
                Gather(
                    "fsdp", fsdp_count, wholes[k], sems[0], sems[1], own=shards[k], part=part
                )
            )
    depth = 3
    for gather in gathers[:depth]:
        gather.start()
    cot = Gather("tp", tp_count, cot_rows, cot_send, cot_recv, own=cot_any)
    cot.start()
    cot_local = pltpu.make_async_copy(cot_any, cot_rows.at[cot.me], cot_sems)
    cot_local.start()
    load.wait()
    rim.wait()
    first_place = mine * rows
    source = (padded, taps_ref, gate_ref, begin_ref, rate_ref, shift_ref)
    row, col = triangles()
    turns = blocks // wide

    def pump(k):
        if k < len(gathers):
            gathers[k].forward_all()
            if k + depth < len(gathers):
                gathers[k + depth].start()

    for h in range(heads):
        own_pair[h] = jnp.concatenate(
            [(row == col).astype(f32), jnp.zeros((K, V), f32)], axis=1
        )

    def front(step, carry):
        units = [
            Chunk(source, h, heads, step * wide + j, first_place)
            for j in range(wide)
            for h in range(heads)
        ]
        lowers = [
            unit.beta * dot_three(unit.key, unit.key, dot_nt) * unit.weights for unit in units
        ]
        inverses = [half(inverse) for inverse in unit_inverses(lowers)]
        solved = [dot_nn(inv, half(unit.sides())) for inv, unit in zip(inverses, units)]
        for unit, inv, sides in zip(units, inverses, solved):
            h, n = unit.head, unit.n
            inv_ref[h, n] = inv
            side_ref[h, n] = sides
            query_ref[h, n] = half(unit.query * unit.carry)
            score_ref[h, n] = half(
                dot_nt(half(unit.query), half(unit.key)) * unit.factor
            )
            driven = dot_tn(half(unit.key_last), half(sides))
            maps[h, n] = driven[:, V:]
            scales[h, n] = jnp.broadcast_to(unit.scale, (8, 128))
            pair = own_pair[h]
            prefix[h, n] = pair
            moved = dot_three(driven[:, V:], pair, dot_nn)
            drive = jnp.concatenate([jnp.zeros((K, K), f32), driven[:, :V]], axis=1)
            own_pair[h] = unit.scale * pair + drive - moved

        return carry

    lax.fori_loop(0, turns, front, 0)
    for h in range(heads):
        pairs[mine, pl.ds(h * K, K), :] = half(own_pair[h])
    ring = Gather("fsdp", fsdp_count, pairs, pair_send, pair_recv)
    ring.start()
    cot.forward_all()
    pump(0)
    ring.forward_all()
    pump(1)
    ring.arrive_all()
    hops = min(fsdp_count - 1, -(-MAXLEN // rows))
    states = [jnp.zeros((K, V), f32) for _ in range(heads)]
    for hop in range(hops, 0, -1):
        spot = jnp.maximum(mine - hop, 0)
        for h in range(heads):
            piece = pairs[spot, pl.ds(h * K, K), :]
            top, low = split_two(states[h])
            new = dot_nn(piece[:, :K], top) + dot_nn(piece[:, :K], low)
            states[h] = jnp.where(mine >= hop, new + piece[:, K:].astype(f32), states[h])

    def back(n, carry):
        at = pl.ds(pl.multiple_of(n * GROUP, GROUP), GROUP)
        for h in range(heads):
            pair = prefix[h, n]
            start = half(dot_three(pair[:, :K], states[h], dot_nn) + pair[:, K:])
            state_ref[h, n] = start
            sides = side_ref[h, n]
            update = half(sides[:, :V] - dot_nn(half(sides[:, V:]), start))
            update_ref[h, n] = update
            out = dot_nn(query_ref[h, n], start) + dot_nn(score_ref[h, n], update)
            out_ref[h, n] = out
            gate = gate_ref[at, h * V : (h + 1) * V]
            root = lax.rsqrt(jnp.mean(out * out, axis=-1, keepdims=True) + 1e-06)
            normed_ref[at, h * V : (h + 1) * V] = half(
                out * root * norm_ref[...] * (gate * jax.nn.sigmoid(gate))
            )
        for k in range(2, len(gathers)):

            @pl.when(n == min(2 * (k - 2), blocks - 1))
            def _(k=k):
                pump(k)

        return carry

    lax.fori_loop(0, blocks, back, 0)
    cot.arrive_all()
    for gather in gathers:
        gather.arrive_all()
    for copy in locals_ + [cot_local]:
        copy.wait()
    for gather in gathers + [ring, cot]:
        gather.finish()


def mixer_all(mixed, gate, taps, begins, rate, shift, norm, cotangent, shards, ident):
    tp_count, fsdp_count = lax.axis_size("tp"), lax.axis_size("fsdp")
    heads = rate.shape[0]
    splits = [parts_of(shard.shape[0], 2) for shard in shards]
    rows = mixed.shape[0]
    blocks = rows // GROUP
    wide = 2 if blocks % 2 == 0 else 1
    f32, bf16 = jnp.float32, jnp.bfloat16
    vmem = pl.BlockSpec(memory_space=pltpu.VMEM)
    smem = pl.BlockSpec(memory_space=pltpu.SMEM)
    anys = pl.BlockSpec(memory_space=pl.ANY)
    dma = pltpu.SemaphoreType.DMA
    shape = jax.ShapeDtypeStruct
    outs = [
        shape((rows, heads * V), bf16),
        shape((heads, blocks, GROUP, GROUP), bf16),
        shape((heads, blocks, GROUP, V + K), f32),
        shape((heads, blocks, GROUP, K), bf16),
        shape((heads, blocks, GROUP, GROUP), bf16),
        shape((heads, blocks, K, V), bf16),
        shape((heads, blocks, GROUP, V), bf16),
        shape((heads, blocks, GROUP, V), f32),
        shape((heads, blocks, K, K), f32),
        shape((heads, blocks, 8, 128), f32),
        shape((rows + RIM, mixed.shape[1]), bf16),
        shape((fsdp_count, heads * K, K + V), bf16),
        shape((tp_count,) + cotangent.shape, bf16),
    ] + [shape((fsdp_count,) + shard.shape, shard.dtype) for shard in shards]
    scratch = [
        pltpu.VMEM((heads, blocks, K, K + V), f32),
        pltpu.VMEM((heads, K, K + V), f32),
        dma((2,)),
        dma,
        dma((fsdp_count - 1,)),
        dma((fsdp_count,)),
        dma,
        dma((tp_count - 1,)),
        dma((tp_count,)),
    ]
    scratch += [dma] * len(shards)
    for _ in range(sum(len(split) for split in splits)):
        scratch += [dma((fsdp_count - 1,)), dma((fsdp_count,))]
    return pl.pallas_call(
        functools.partial(
            mixer_kernel, heads, blocks, tp_count, fsdp_count, wide, splits
        ),
        out_shape=outs,
        in_specs=[anys] + [vmem] * 3 + [smem] * 2 + [vmem] + [anys] * (1 + len(shards)),
        out_specs=[vmem] * 12 + [anys] * (1 + len(shards)),
        scratch_shapes=scratch,
        compiler_params=comm_params(ident, 60),
        name="mixer",
    )(mixed, gate, taps, begins, rate, shift, norm, cotangent, *shards)


def mixer_grad_kernel(heads, blocks, tp_count, fsdp_count, splits, *refs):
    bf16, f32 = jnp.bfloat16, jnp.float32
    refs = list(refs)

    def take(number):
        out = refs[:number]
        del refs[:number]
        return out

    extra_count = len(splits)
    padded, gate_ref, taps_ref, begin_ref, rate_ref, shift_ref, norm_ref = take(7)
    inv_ref, side_ref, query_ref, score_ref, state_ref, update_ref, out_ref = take(7)
    maps, scales, pairs, dm_ref = take(4)
    extras = take(extra_count)
    d_raw_ref, g_taps_ref, g_decay_ref, g_norm_ref = take(4)
    extra_outs = take(extra_count)
    d_out, base, local, d_state, halo, tail, d_all, rim_buf = take(8)
    rim_sems, ring_send, ring_recv = take(3)
    rows = blocks * GROUP
    mine = lax.axis_index("fsdp")
    first_place = mine * rows
    mixed_cols = 2 * heads * K + heads * V
    entry_barrier([("fsdp", fsdp_count)], everyone=True)
    sums, sum_outs = [], []
    for extra, out, split in zip(extras, extra_outs, splits):
        for part in split:
            s = take(7)
            sums.append(
                Scatter(
                    "fsdp", fsdp_count, None, s[0], s[1], s[2], s[3:], full=extra, part=part
                )
            )
            sum_outs.append(out)
    depth = 4
    for item in sums[:depth]:
        item.start()

    def pump(k):
        if k < len(sums):
            if k + depth < len(sums):
                sums[k + depth].start()
            sums[k].turn(sum_outs[k])

    g_norm_ref[...] = jnp.zeros_like(g_norm_ref)
    g_taps_ref[...] = jnp.zeros_like(g_taps_ref)
    g_decay_ref[...] = jnp.zeros_like(g_decay_ref)
    halo[...] = jnp.zeros_like(halo)
    source = (padded, taps_ref, gate_ref, begin_ref, rate_ref, shift_ref)
    row, col = triangles()

    def first(n, carry):
        at = pl.ds(pl.multiple_of(n * GROUP, GROUP), GROUP)
        for h in range(heads):
            cols = slice(h * V, (h + 1) * V)
            out = out_ref[h, n]
            root = lax.rsqrt(jnp.mean(out * out, axis=-1, keepdims=True) + 1e-06)
            normed = out * root
            gate = gate_ref[at, cols]
            sig = jax.nn.sigmoid(gate)
            silu = gate * sig
            given = dm_ref[at, cols]
            g_norm_ref[...] += jnp.sum(given * normed * silu, axis=0, keepdims=True)
            pulled = given * norm_ref[...]
            d_raw_ref[at, mixed_cols + h * V : mixed_cols + (h + 1) * V] = half(
                pulled * normed * (sig + silu * (1.0 - sig))
            )
            pulled = pulled * silu
            grad = root * (pulled - normed * jnp.mean(pulled * normed, axis=-1, keepdims=True))
            grad = half(grad)
            d_out[h, n] = grad
            through = dot_tn(score_ref[h, n], grad)
            base[h, n] = through
            key_part = half(side_ref[h, n][:, V:])
            local[h, n] = dot_tn(query_ref[h, n], grad) - dot_tn(key_part, half(through))
        return carry

    lax.fori_loop(0, blocks, first, 0)
    pump(0)

    def pull_state(n, h, grad):
        scale = scales[h, n][0:1, 0:1]
        return scale * grad + local[h, n] - dot_three(maps[h, n], grad, dot_tn)

    for h in range(heads):
        d_state[h] = jnp.zeros((K, V), f32)

    def chain(step, carry):
        n = blocks - 1 - step
        for h in range(heads):
            d_state[h] = pull_state(n, h, d_state[h])
        return carry

    lax.fori_loop(0, blocks, chain, 0)
    for h in range(heads):
        d_all[mine, pl.ds(h * K, K), :] = half(d_state[h])
    ring = Gather("fsdp", fsdp_count, d_all, ring_send, ring_recv)
    ring.start()
    pump(1)
    ring.forward_all()
    pump(2)
    ring.arrive_all()
    hops = min(fsdp_count - 1, -(-MAXLEN // rows))
    for h in range(heads):
        grad = jnp.zeros((K, V), f32)
        for hop in range(hops, 0, -1):
            spot = jnp.minimum(mine + hop, fsdp_count - 1)
            piece = pairs[spot, pl.ds(h * K, K), :][:, :K]
            top, low = split_two(grad)
            new = dot_tn(piece, top) + dot_tn(piece, low)
            new = new + d_all[spot, pl.ds(h * K, K), :].astype(f32)
            grad = jnp.where(mine + hop < fsdp_count, new, grad)
        d_state[h] = grad

    def second(step, carry):
        n = blocks - 1 - step
        at = pl.ds(pl.multiple_of(n * GROUP, GROUP), GROUP)
        lane = lax.broadcasted_iota(jnp.int32, (1, g_decay_ref.shape[1]), 1)
        smalls = []
        for h in range(heads):
            unit = Chunk(source, h, heads, n, first_place)
            query, key, key_last = half(unit.query), half(unit.key), half(unit.key_last)
            after = d_state[h]
            d_state[h] = pull_state(n, h, after)
            after_half = half(after)
            state, grad, update = state_ref[h, n], d_out[h, n], update_ref[h, n]
            sides = side_ref[h, n]
            d_update = half(base[h, n] + dot_nn(key_last, after_half))
            d_key_part = -dot_nt(d_update, state)
            read = dot_nt(grad, state)
            d_query = unit.carry * read
            d_carry = jnp.sum(read * unit.query, axis=1, keepdims=True)
            d_scores = dot_nt(grad, update)
            d_key_last = dot_nt(update, after_half)
            d_scale = jnp.sum(
                jnp.sum(after * state.astype(f32), axis=1, keepdims=True), axis=0, keepdims=True
            )
            d_sides = dot_tn(
                inv_ref[h, n], jnp.concatenate([d_update, half(d_key_part)], axis=1)
            )
            d_lower = -dot_nt(half(d_sides), half(sides))
            gram = dot_nt(key, key) * unit.weights
            pulled = d_lower * gram
            d_beta = jnp.sum(pulled, axis=1, keepdims=True)
            moved = unit.beta * pulled + d_scores * score_ref[h, n].astype(f32)
            d_gram = half(d_lower * (unit.beta * unit.weights))
            d_qk = half(d_scores * unit.factor)
            d_query = d_query + dot_nn(d_qk, key)
            d_key = dot_tn(d_qk, query) + dot_nn(d_gram, key) + dot_tn(d_gram, key)
            d_key = d_key + d_key_last * unit.last
            d_last = jnp.sum(d_key_last * unit.key_last, axis=1, keepdims=True)
            d_value_side, d_key_side = d_sides[:, :V], d_sides[:, V:]
            d_beta = d_beta + jnp.sum(d_value_side * unit.value, axis=1, keepdims=True)
            d_value = unit.beta * d_value_side
            mixed_side = jnp.sum(d_key_side * unit.key, axis=1, keepdims=True)
            d_key = d_key + (unit.beta * unit.carry) * d_key_side
            d_beta = d_beta + unit.carry * mixed_side
            d_carry = d_carry + unit.beta * mixed_side
            at_end = lax.broadcasted_iota(jnp.int32, (GROUP, 1), 0) == GROUP - 1
            d_carry = d_carry + jnp.where(at_end, d_scale, 0.0)
            d_cumul = d_carry * unit.carry - d_last
            d_cumul = d_cumul + jnp.where(
                at_end, jnp.sum(d_last, axis=0, keepdims=True), 0.0
            )
            d_cumul = d_cumul + jnp.sum(moved, axis=1, keepdims=True)
            d_row = jnp.sum(jnp.where(row == col, d_cumul, 0.0), axis=0, keepdims=True)
            d_row = d_row - jnp.sum(moved, axis=0, keepdims=True)
            d_decay = jnp.sum(jnp.where(col >= row, d_row, 0.0), axis=1, keepdims=True)
            d_decay_in = d_decay * unit.rate * jax.nn.sigmoid(unit.decay_in)
            log_sum = jnp.sum(d_decay * unit.decay, axis=0, keepdims=True)
            bias_sum = jnp.sum(d_decay_in, axis=0, keepdims=True)
            g_decay_ref[...] += jnp.where(lane == h, log_sum, 0.0) + jnp.where(
                lane == heads + h, bias_sum, 0.0
            )
            smalls.append((d_beta * unit.beta * (1.0 - unit.beta), d_decay_in))
            unscaled = unit.query * K**0.5
            d_query = d_query * K ** (-0.5)
            d_query = unit.query_root * (
                d_query - unscaled * jnp.sum(d_query * unscaled, axis=1, keepdims=True)
            )
            d_key = unit.key_root * (
                d_key - unit.key * jnp.sum(d_key * unit.key, axis=1, keepdims=True)
            )
            for part, given in enumerate((d_query, d_key, d_value)):
                start, size = unit.cols[part]
                sig, pre = unit.sigs[part], unit.pres[part]
                d_pre = given * sig * (1.0 + pre * (1.0 - sig))
                taps, spread = unit.taps[part], unit.padded[part]
                total = taps[0:1] * d_pre
                edge = jnp.zeros((RIM, size), f32)
                grads = [jnp.sum(d_pre * spread[RIM:], axis=0, keepdims=True)]
                whole = jnp.concatenate([edge, total], axis=0)
                for lag in range(1, CONV):
                    masked = d_pre * unit.ranges[lag - 1]
                    grads.append(
                        jnp.sum(
                            masked * pltpu.roll(spread, lag, 0)[RIM:], axis=0, keepdims=True
                        )
                    )
                    ext = jnp.concatenate([edge, taps[lag : lag + 1] * masked], axis=0)
                    whole = whole + pltpu.roll(ext, GROUP + RIM - lag, 0)
                for lag in range(CONV):
                    g_taps_ref[lag : lag + 1, start : start + size] += grads[lag]
                body = whole[RIM:]
                ended = body[GROUP - RIM :] + halo[:, start : start + size]
                halo[:, start : start + size] = whole[:RIM]
                body = jnp.concatenate([body[: GROUP - RIM], ended], axis=0)
                d_raw_ref[at, start : start + size] = half(body)

                @pl.when(step == 0)
                def _():
                    tail[:, start : start + size] = ended

        spot = lax.broadcasted_iota(jnp.int32, (GROUP, 2 * heads), 1)
        joined = jnp.zeros((GROUP, 2 * heads), f32)
        for h, (d_beta, d_decay_in) in enumerate(smalls):
            joined = joined + jnp.where(spot == h, d_beta, 0.0)
            joined = joined + jnp.where(spot == heads + h, d_decay_in, 0.0)
        d_raw_ref[at, mixed_cols + heads * V :] = half(joined)
        for k in range(3, len(sums)):

            @pl.when(step == min((k - 3) * (blocks - 2) // max(len(sums) - 3, 1), blocks - 1))
            def _(k=k):
                pump(k)

        return carry

    lax.fori_loop(0, blocks, second, 0)
    rim = pltpu.make_async_remote_copy(
        src_ref=halo,
        dst_ref=rim_buf,
        send_sem=rim_sems.at[0],
        recv_sem=rim_sems.at[1],
        device_id=on_axis("fsdp", lax.rem(mine + fsdp_count - 1, fsdp_count)),
        device_id_type=MESH,
    )
    rim.start()
    for item, out in zip(sums, sum_outs):
        item.close(out)
    rim.wait()
    d_raw_ref[rows - RIM : rows, 0:mixed_cols] = half(tail[...] + rim_buf[...])
    for item in sums + [ring]:
        item.finish()


def mixer_grad_all(
    padded, gate, taps, begins, rate, shift, norm, saved, pairs, d_mixer, extras, ident
):
    tp_count, fsdp_count = lax.axis_size("tp"), lax.axis_size("fsdp")
    heads = rate.shape[0]
    splits = [parts_of(extra.shape[1], 4) for extra in extras]
    rows = gate.shape[0]
    blocks = rows // GROUP
    mixed_cols = padded.shape[1]
    f32, bf16 = jnp.float32, jnp.bfloat16
    vmem = pl.BlockSpec(memory_space=pltpu.VMEM)
    smem = pl.BlockSpec(memory_space=pltpu.SMEM)
    dma = pltpu.SemaphoreType.DMA
    shape = jax.ShapeDtypeStruct
    outs = [
        shape((rows, mixed_cols + heads * V + 2 * heads), bf16),
        shape((CONV, mixed_cols), f32),
        shape((1, 128), f32),
        shape((1, V), f32),
    ] + [shape(extra.shape[1:], f32) for extra in extras]
    scratch = [
        pltpu.VMEM((heads, blocks, GROUP, V), bf16),
        pltpu.VMEM((heads, blocks, GROUP, V), f32),
        pltpu.VMEM((heads, blocks, K, V), f32),
        pltpu.VMEM((heads, K, V), f32),
        pltpu.VMEM((RIM, mixed_cols), f32),
        pltpu.VMEM((RIM, mixed_cols), f32),
        pltpu.VMEM((fsdp_count, heads * K, V), bf16),
        pltpu.VMEM((RIM, mixed_cols), f32),
        dma((2,)),
        dma((fsdp_count - 1,)),
        dma((fsdp_count,)),
    ]
    for extra, split in zip(extras, splits):
        for part in split:
            size = extra.shape[1] if part is None else part[1]
            scratch += scatter_scratch(fsdp_count, size, extra.shape[2], full=True)
    return pl.pallas_call(
        functools.partial(
            mixer_grad_kernel, heads, blocks, tp_count, fsdp_count, splits
        ),
        out_shape=outs,
        in_specs=[vmem] * 4 + [smem] * 2 + [vmem] * (12 + len(extras)),
        out_specs=[vmem] * len(outs),
        scratch_shapes=scratch,
        compiler_params=comm_params(ident, 60),
        name="mixer_grad",
    )(padded, gate, taps, begins, rate, shift, norm, *saved, pairs, d_mixer, *extras)


def shards(
    tokens,
    lengths,
    attn_gain,
    w_query,
    w_key,
    w_value,
    w_gate_out,
    w_beta,
    w_decay,
    conv_query,
    conv_key,
    conv_value,
    decay_log,
    decay_bias,
    out_gain,
    w_out,
    ffn_gain,
    w_ffn_gate,
    w_ffn_up,
    w_ffn_down,
    cotangent,
):
    count = lax.axis_size("fsdp")
    shard_rows = tokens.shape[0]
    query_cols, value_cols = w_query.shape[1], w_value.shape[1]
    hidden_cols = w_ffn_gate.shape[1]
    head_count = query_cols // K
    mixed_cols = 2 * query_cols + value_cols
    raw_cols = mixed_cols + value_cols

    tp_count = lax.axis_size("tp")
    width = tokens.shape[1]
    small_list = (attn_gain, ffn_gain, out_gain, conv_query, conv_key, conv_value)
    small = jnp.concatenate([part.astype(jnp.float32).reshape(-1) for part in small_list])
    small_width = -(-small.shape[0] // 1024) * 1024
    small = jnp.pad(small, (0, small_width - small.shape[0])).reshape(8, -1)
    gate_shard = jnp.concatenate([w_gate_out, w_beta, w_decay], axis=1)
    normed_blocks, small, *mixer_w, mixed_raw, gate_raw = front_all(
        tokens, small, [w_query, w_key, w_value, gate_shard], 0
    )
    small = small.reshape(count, -1)
    smalls, at = ([], 0)
    for part in small_list:
        piece = small[:, at : at + part.size]
        at = at + part.size
        if part.ndim == 3:
            piece = piece.reshape((count,) + part.shape).transpose(1, 2, 0, 3)
            smalls.append(piece.reshape(part.shape[0], part.shape[1], -1))
        else:
            smalls.append(piece.reshape(-1))
    gain_one, gain_two, norm_out, query_taps, key_taps, value_taps = smalls
    row_count = mixed_raw.shape[0]
    positions = lax.axis_index("fsdp") * row_count + jnp.arange(row_count, dtype=jnp.int32)
    begins = seq_begin(lengths, positions)
    taps = jnp.concatenate(
        [part.reshape(CONV, -1) for part in (query_taps, key_taps, value_taps)], axis=1
    )
    common = (
        gate_raw,
        taps,
        begins.reshape(-1, 1),
        -jnp.exp(decay_log),
        decay_bias,
        norm_out.reshape(1, -1),
    )
    normed_mixer, *saved, padded, pairs, cot_blocks, out_t, down_t, ffn_gate_w = (
        mixer_all(
            mixed_raw,
            *common,
            cotangent,
            [w_out.T, w_ffn_down.T, w_ffn_gate],
            1,
        )
    )
    out_t, ffn_gate_w, down_t = [
        part.reshape(width, -1) for part in (out_t, ffn_gate_w, down_t)
    ]
    (
        output,
        d_hidden,
        d_mixer,
        g_gate,
        g_up,
        grad_down_t,
        g_out,
        gain_two_part,
    ) = ffn_all(
        normed_mixer.reshape(tp_count, shard_rows, -1),
        tokens,
        cotangent,
        out_t,
        gain_two.reshape(1, -1),
        cot_blocks,
        ffn_gate_w,
        w_ffn_up,
        down_t,
        2,
    )
    d_mixer = d_mixer.reshape(row_count, -1)
    gain_two_part = gain_two_part.reshape(-1)

    d_raw, g_taps, g_decay, norm_out_part, *grads_ffn = mixer_grad_all(
        padded,
        *common,
        saved,
        pairs,
        d_mixer,
        [part.reshape(count, width // count, -1) for part in (g_out, g_gate, g_up)],
        3,
    )
    grad_out_t, grad_w_ffn_gate, grad_w_ffn_up = grads_ffn
    d_taps = [
        part.reshape(CONV, head_count, -1)
        for part in jnp.split(g_taps, (query_cols, 2 * query_cols), axis=1)
    ]
    decay_pair = g_decay[0, : 2 * head_count]

    def spread(taps):
        taps = taps.reshape(taps.shape[0], taps.shape[1], count, -1)
        return taps.transpose(2, 0, 1, 3).reshape(count, -1)

    small_parts = [
        gain_two_part.reshape(count, -1),
        norm_out_part.reshape(count, -1),
        spread(d_taps[0]),
        spread(d_taps[1]),
        spread(d_taps[2]),
        jnp.broadcast_to(decay_pair[None, :], (count, decay_pair.shape[0])),
    ]
    small_cat = jnp.concatenate(small_parts, axis=1)
    lanes = -(-max(small_cat.shape[1], 7 * (width // count)) // (7 * 128)) * 128
    small_cat = jnp.pad(small_cat, ((0, 0), (lanes, 7 * lanes - small_cat.shape[1])))
    d_tokens, small_own, small_all, *grads_mixer = last_all(
        d_raw.reshape(tp_count, shard_rows, -1),
        normed_blocks,
        tokens,
        gain_one.reshape(1, -1),
        d_hidden,
        small_cat.reshape(count, 8, lanes),
        mixer_w,
        4,
    )
    grad_w_ffn_down = grad_down_t.T
    grad_w_out = grad_out_t.T
    grads_w = grads_mixer[:3] + jnp.split(
        grads_mixer[3], (value_cols, value_cols + head_count), axis=1
    )
    small_cuts, at = ([], lanes)
    for part in small_parts:
        small_cuts.append(at)
        at = at + part.shape[1]
    small_cuts.append(at)
    own_parts = jnp.split(small_own.reshape(-1), small_cuts)
    all_parts = jnp.split(small_all.reshape(-1), small_cuts)
    small_out = [
        small_all[0, : width // count],
        all_parts[1],
        all_parts[2],
        own_parts[3],
        own_parts[4],
        own_parts[5],
        own_parts[6],
    ]
    return (
        output,
        d_tokens,
        small_out[0],
        *grads_w,
        small_out[3].reshape(conv_query.shape),
        small_out[4].reshape(conv_key.shape),
        small_out[5].reshape(conv_value.shape),
        small_out[6][:head_count],
        small_out[6][head_count:],
        small_out[2],
        grad_w_out,
        small_out[1],
        grad_w_ffn_gate,
        grad_w_ffn_up,
        grad_w_ffn_down,
    )


def solution(mesh):
    placed = (
        P(("fsdp", "tp"), None),
        P(),
        P("fsdp"),
        P("fsdp", "tp"),
        P("fsdp", "tp"),
        P("fsdp", "tp"),
        P("fsdp", "tp"),
        P("fsdp", "tp"),
        P("fsdp", "tp"),
        P(None, "tp", "fsdp"),
        P(None, "tp", "fsdp"),
        P(None, "tp", "fsdp"),
        P("tp"),
        P("tp"),
        P("fsdp"),
        P("tp", "fsdp"),
        P("fsdp"),
        P("fsdp", "tp"),
        P("fsdp", "tp"),
        P("tp", "fsdp"),
        P(("fsdp", "tp"), None),
    )
    return jax.shard_map(
        shards,
        mesh=mesh,
        in_specs=placed,
        out_specs=(
            P(("fsdp", "tp"), None),
            P(("fsdp", "tp"), None),
            P("fsdp"),
            P("fsdp", "tp"),
            P("fsdp", "tp"),
            P("fsdp", "tp"),
            P("fsdp", "tp"),
            P("fsdp", "tp"),
            P("fsdp", "tp"),
            P(None, "tp", "fsdp"),
            P(None, "tp", "fsdp"),
            P(None, "tp", "fsdp"),
            P("tp"),
            P("tp"),
            P("fsdp"),
            P("tp", "fsdp"),
            P("fsdp"),
            P("fsdp", "tp"),
            P("fsdp", "tp"),
            P("tp", "fsdp"),
        ),
        check_vma=False,
    )
```

```python
import functools

import jax
import jax.numpy as jnp
from jax import lax
from jax.experimental import pallas as pl
from jax.experimental.pallas import tpu as pltpu
from jax.sharding import PartitionSpec as P

K = 128
V = 256
CONV = 4
GROUP = 128
MAXLEN = 4096
RIM = 16


def mat_dot(left, right):
    return jnp.dot(left, right, preferred_element_type=jnp.float32)


def rms_scale(values, scale_gain):
    return (
        values * lax.rsqrt(jnp.mean(values * values, axis=-1, keepdims=True) + 1e-06) * scale_gain
    )


def seq_begin(lengths, positions):
    number = lengths.shape[0]
    earlier = jnp.arange(number)[None, :] < jnp.arange(number)[:, None]
    offsets = jnp.sum(jnp.where(earlier, lengths[None, :], 0), axis=1)
    chosen = jnp.where(offsets[None, :] <= positions[:, None], offsets[None, :], 0)
    return jnp.max(chosen, axis=1)


MESH = pl.DeviceIdType.MESH
INNER = 2


def on_axis(axis, index):
    return {axis: index}


def halves(axis):
    me = lax.axis_index(axis)
    return me, lax.div(me, INNER), lax.rem(me, INNER)


def entry_barrier(axes, everyone=False):
    barrier = pltpu.get_barrier_semaphore()
    total = 0
    for axis, count in axes:
        me, outer, inner = halves(axis)
        outers = count // INNER
        peers = [outer * INNER + (1 - inner)]
        for d in range(1, outers):
            peers.append(lax.rem(outer + d, outers) * INNER + inner)
        if everyone:
            peers = [lax.rem(me + d, count) for d in range(1, count)]
        for peer in peers:
            pl.semaphore_signal(
                barrier, inc=1, device_id=on_axis(axis, peer), device_id_type=MESH
            )
        total += len(peers)
    pl.semaphore_wait(barrier, total)


class Gather:
    def __init__(self, axis, count, buf, send, recv, own=None, part=None):
        self.axis, self.count, self.buf, self.send, self.recv = axis, count, buf, send, recv
        self.outers = count // INNER
        self.me, self.outer, self.inner = halves(axis)
        self.part = part
        if own is None:
            self.own = self.slot(self.me)
        else:
            self.own = own if part is None else own.at[pl.ds(*part)]

    def slot(self, index):
        if self.part is None:
            return self.buf.at[index]
        return self.buf.at[index, pl.ds(*self.part)]

    def block(self, d, across):
        outer = lax.rem(self.outer + self.outers - d, self.outers)
        return outer * INNER + ((1 - self.inner) if across else self.inner)

    def copy(self, d, forward):
        across = self.outer * INNER + 1 - self.inner
        if forward:
            index = self.block(d, False)
            src, target, sem = self.slot(index), across, self.outers - 1 + d
        else:
            index, src = self.me, self.own
            target = across
            if d:
                target = lax.rem(self.outer + d, self.outers) * INNER + self.inner
            sem = d
        return pltpu.make_async_remote_copy(
            src_ref=src,
            dst_ref=self.slot(index),
            send_sem=self.send.at[sem],
            recv_sem=self.recv.at[index],
            device_id=on_axis(self.axis, target),
            device_id_type=MESH,
        )

    def start(self):
        for d in list(range(1, self.outers)) + [0]:
            self.copy(d, False).start()

    def arrive(self, index):
        pltpu.make_async_remote_copy(
            src_ref=self.slot(index),
            dst_ref=self.slot(index),
            send_sem=self.send.at[0],
            recv_sem=self.recv.at[index],
            device_id=on_axis(self.axis, self.outer * INNER + 1 - self.inner),
            device_id_type=MESH,
        ).wait_recv()

    def forward(self, d):
        index = self.block(d, False)
        self.arrive(index)
        self.copy(d, True).start()
        return index

    def forward_all(self):
        for d in range(1, self.outers):
            self.forward(d)

    def arrive_all(self):
        for d in range(self.outers):
            self.arrive(self.block(d, True))

    def finish(self):
        for d in range(self.outers):
            self.copy(d, False).wait_send()
        for d in range(1, self.outers):
            self.copy(d, True).wait_send()


class Scatter:
    def __init__(self, axis, count, out, stage, send2, stage2, sems, full=None, part=None):
        self.axis, self.count, self.full, self.part = axis, count, full, part
        self.outers = count // INNER
        self.me, self.outer, self.inner = halves(axis)
        self.out, self.stage, self.send2, self.stage2 = out, stage, send2, stage2
        self.send_a, self.recv_a, self.send_b, self.recv_b = sems

    def target(self, d, across):
        outer = lax.rem(self.outer + d, self.outers)
        return outer * INNER + ((1 - self.inner) if across else self.inner)

    def own(self, d):
        if self.part is None:
            return self.full[self.target(d, False)].astype(jnp.float32)
        return self.full[self.target(d, False), pl.ds(*self.part)].astype(jnp.float32)

    def first(self, d):
        if self.full is None:
            src = self.out.at[d]
        elif self.part is None:
            src = self.full.at[self.target(d, True)]
        else:
            src = self.full.at[self.target(d, True), pl.ds(*self.part)]
        return pltpu.make_async_remote_copy(
            src_ref=src,
            dst_ref=self.stage.at[d],
            send_sem=self.send_a.at[d],
            recv_sem=self.recv_a.at[d],
            device_id=on_axis(self.axis, self.outer * INNER + 1 - self.inner),
            device_id_type=MESH,
        )

    def second(self, d):
        return pltpu.make_async_remote_copy(
            src_ref=self.send2.at[d - 1],
            dst_ref=self.stage2.at[d - 1],
            send_sem=self.send_b.at[d - 1],
            recv_sem=self.recv_b.at[d - 1],
            device_id=on_axis(self.axis, self.target(d, False)),
            device_id_type=MESH,
        )

    def send_across(self, d):
        self.first(d).start()

    def take_across(self, d):
        self.first(d).wait_recv()

    def send_outer(self, d):
        self.second(d).start()

    def take_outer(self, d):
        self.second(d).wait_recv()

    def order(self):
        return list(range(1, self.outers)) + [0]

    def start(self):
        for d in self.order():
            self.send_across(d)

    def turn(self, out):
        for d in self.order():
            self.take_across(d)
            total = self.own(d) + self.stage[d].astype(jnp.float32)
            if d:
                self.send2[d - 1] = total.astype(jnp.bfloat16)
                self.send_outer(d)
            else:
                self.write(out, total, False)

    def write(self, out, total, add):
        at = pl.ds(0, out.shape[0]) if self.part is None else pl.ds(*self.part)
        out[at, :] = (out[at, :] + total) if add else total

    def close(self, out):
        total = None
        for d in range(1, self.outers):
            self.take_outer(d)
            piece = self.stage2[d - 1].astype(jnp.float32)
            total = piece if total is None else total + piece
        if total is not None:
            self.write(out, total, True)

    def finish(self):
        for d in range(self.outers):
            self.first(d).wait_send()
        for d in range(1, self.outers):
            self.second(d).wait_send()


def parts_of(rows, pieces):
    size = rows // pieces
    if rows % pieces or size % 16:
        return [None]
    return [(at * size, size) for at in range(pieces)]


def scatter_scratch(count, rows, cols, dtype=jnp.bfloat16, full=False):
    outers = count // INNER
    own = [] if full else [pltpu.VMEM((outers, rows, cols), dtype)]
    return own + [
        pltpu.VMEM((outers, rows, cols), dtype),
        pltpu.VMEM((max(outers - 1, 1), rows, cols), dtype),
        pltpu.VMEM((max(outers - 1, 1), rows, cols), dtype),
        pltpu.SemaphoreType.DMA((outers,)),
        pltpu.SemaphoreType.DMA((outers,)),
        pltpu.SemaphoreType.DMA((max(outers - 1, 1),)),
        pltpu.SemaphoreType.DMA((max(outers - 1, 1),)),
    ]


def comm_params(ident, vmem_mb):
    return pltpu.CompilerParams(
        collective_id=ident, has_side_effects=True, vmem_limit_bytes=vmem_mb * 2**20
    )


def front_kernel(tp_count, fsdp_count, number, splits, *refs):
    bf16, f32 = jnp.bfloat16, jnp.float32
    refs = list(refs)

    def take(count):
        out = refs[:count]
        del refs[:count]
        return out

    tok_any, small_any = take(2)
    shards = take(number)
    n1_ref, small_ref = take(2)
    wholes = take(number)
    mixed_ref, gate_ref = take(2)
    tok_rows, gain_ref, local_sems = take(3)
    pieces = [take(2) for _ in range(2 + sum(len(split) for split in splits))]
    me_tp, me = lax.axis_index("tp"), lax.axis_index("fsdp")
    locals_ = [
        pltpu.make_async_copy(src, dst, local_sems.at[k])
        for k, (src, dst) in enumerate(
            [(tok_any, tok_rows.at[me_tp]), (small_any, small_ref.at[me])]
            + [(shard, whole.at[me]) for shard, whole in zip(shards, wholes)]
        )
    ]
    for copy in locals_:
        copy.start()
    entry_barrier([("fsdp", fsdp_count), ("tp", tp_count)])
    tok = Gather("tp", tp_count, tok_rows, pieces[0][0], pieces[0][1], own=tok_any)
    small = Gather("fsdp", fsdp_count, small_ref, pieces[1][0], pieces[1][1], own=small_any)
    groups, at = [], 2
    for shard, whole, split in zip(shards, wholes, splits):
        group = []
        for part in split:
            sems = pieces[at]
            at += 1
            group.append(
                Gather("fsdp", fsdp_count, whole, sems[0], sems[1], own=shard, part=part)
            )
        groups.append(group)
    items = [item for group in groups for item in group]
    depth = 3
    small.start()
    tok.start()
    for item in items[:depth]:
        item.start()
    small.forward_all()
    tok.forward_all()

    def pump(k):
        items[k].forward_all()
        if k + depth < len(items):
            items[k + depth].start()

    pumped = 0
    pump(0)
    pumped = 1
    small.arrive_all()
    tok.arrive_all()
    for copy in locals_:
        copy.wait()
    width = n1_ref.shape[2]
    share = width // fsdp_count
    for f in range(fsdp_count):
        gain_ref[0:1, f * share : (f + 1) * share] = small_ref[f, 0:1, 0:share]
    for b in range(tp_count):
        rows = tok_rows[b].astype(f32)
        root = lax.rsqrt(jnp.mean(rows * rows, axis=-1, keepdims=True) + 1e-06)
        n1_ref[b] = (rows * root * gain_ref[...]).astype(bf16)
        if b % 2 and pumped < len(items):
            pump(pumped)
            pumped += 1
    column = 0
    tall = tok_rows.shape[1]
    for k, (group, whole) in enumerate(zip(groups, wholes)):
        ahead = sum(len(part) for part in groups[: k + 2])
        while pumped < ahead:
            pump(pumped)
            pumped += 1
        for item in group:
            item.arrive_all()
        weight = whole[...].reshape(width, whole.shape[2])
        cols = whole.shape[2]
        for b in range(tp_count):
            product = dot_nn(n1_ref[b], weight)
            rows = pl.ds(b * tall, tall)
            if k + 1 < number:
                mixed_ref[rows, column : column + cols] = product.astype(bf16)
            else:
                gate_ref[rows, :] = product
        column += cols
    for item in [small, tok] + items:
        item.finish()


def front_all(tokens, small, shards, ident):
    tp_count, fsdp_count = lax.axis_size("tp"), lax.axis_size("fsdp")
    rows, width = tokens.shape
    f32, bf16 = jnp.float32, jnp.bfloat16
    shape = jax.ShapeDtypeStruct
    dma = pltpu.SemaphoreType.DMA
    vmem = pl.BlockSpec(memory_space=pltpu.VMEM)
    splits = [
        parts_of(shard.shape[0], 2 if shard.shape[1] > 2 * K else 1) for shard in shards
    ]
    mixed_cols = sum(shard.shape[1] for shard in shards[:-1])
    outs = (
        [
            shape((tp_count, rows, width), bf16),
            shape((fsdp_count,) + small.shape, f32),
        ]
        + [shape((fsdp_count,) + shard.shape, bf16) for shard in shards]
        + [
            shape((tp_count * rows, mixed_cols), bf16),
            shape((tp_count * rows, shards[-1].shape[1]), f32),
        ]
    )
    scratch = [
        pltpu.VMEM((tp_count, rows, width), bf16),
        pltpu.VMEM((1, width), f32),
        dma((2 + len(shards),)),
        dma((tp_count - 1,)),
        dma((tp_count,)),
    ]
    for _ in range(1 + sum(len(split) for split in splits)):
        scratch += [dma((fsdp_count - 1,)), dma((fsdp_count,))]
    return pl.pallas_call(
        functools.partial(front_kernel, tp_count, fsdp_count, len(shards), splits),
        out_shape=outs,
        in_specs=[pl.BlockSpec(memory_space=pl.ANY)] * (2 + len(shards)),
        out_specs=[vmem] * len(outs),
        scratch_shapes=scratch,
        compiler_params=comm_params(ident, 60),
        name="front",
    )(tokens, small, *shards)


def dot_nn(left, right):
    return lax.dot_general(
        left, right, (((1,), (0,)), ((), ())), preferred_element_type=jnp.float32
    )


def dot_nt(left, right):
    return lax.dot_general(
        left, right, (((1,), (1,)), ((), ())), preferred_element_type=jnp.float32
    )


def dot_tn(left, right):
    return lax.dot_general(
        left, right, (((0,), (0,)), ((), ())), preferred_element_type=jnp.float32
    )


def ffn_kernel(
    count,
    fsdp_count,
    splits,
    nm_ref,
    tok_ref,
    cot_ref,
    out_w_ref,
    gain_ref,
    cot_any,
    gate_any,
    up_any,
    down_any,
    output_ref,
    d_hidden_ref,
    d_mixer_ref,
    g_gate_ref,
    g_up_ref,
    g_down_out,
    g_out_ref,
    g_gain_ref,
    cot_rows,
    gate_w,
    up_w,
    down_w,
    n2,
    dh,
    act_s,
    dgate_s,
    dup_s,
    hidden_s,
    dact_s,
    g_down_full,
    load_sem,
    up_sem,
    n2_send,
    n2_recv,
    dh_send,
    dh_recv,
    *scatters,
):
    bf16, f32 = jnp.bfloat16, jnp.float32
    loads = [
        pltpu.make_async_copy(src, dst, load_sem.at[k])
        for k, (src, dst) in enumerate(
            ((cot_any, cot_rows), (down_any, down_w), (gate_any, gate_w))
        )
    ]
    for load in loads:
        load.start()
    up_local = pltpu.make_async_copy(up_any, up_w.at[lax.axis_index("fsdp")], up_sem)
    up_local.start()
    entry_barrier([("fsdp", fsdp_count), ("tp", count)])
    outers = count // INNER
    scatters = list(scatters)
    ups, downs = [], []
    for part in splits:
        sems = scatters[:2]
        del scatters[:2]
        ups.append(
            Gather("fsdp", fsdp_count, up_w, sems[0], sems[1], own=up_any, part=part)
        )
    for part in splits:
        s = scatters[:7]
        del scatters[:7]
        downs.append(
            Scatter(
                "fsdp", fsdp_count, None, s[0], s[1], s[2], s[3:], full=g_down_full, part=part
            )
        )
    for item in ups:
        item.start()
    sets = [scatters[8 * k : 8 * k + 8] for k in range(3)]
    mix_s, dn_s, ffn_s = [
        Scatter("tp", count, s[0], s[1], s[2], s[3], s[4:]) for s in sets
    ]
    order = list(range(1, outers)) + [0]

    for d in order:
        mix_s.out[d] = dot_nt(nm_ref[mix_s.target(d, True)], out_w_ref[...]).astype(bf16)
        mix_s.send_across(d)
    for d in order:
        part = dot_nt(nm_ref[mix_s.target(d, False)], out_w_ref[...])
        mix_s.take_across(d)
        if d:
            mix_s.send2[d - 1] = (part + mix_s.stage[d].astype(f32)).astype(bf16)
            mix_s.send_outer(d)
        else:
            hidden_s[...] = part + mix_s.stage[0].astype(f32) + tok_ref[...].astype(f32)
    loads[0].wait()
    loads[1].wait()
    for b in range(count):
        dact_s[b] = dot_nn(cot_rows[b], down_w[...])
        if b == count // 2:
            ups[0].forward_all()
    for item in ups[1:]:
        item.forward_all()
    total = hidden_s[...]
    for d in range(1, outers):
        mix_s.take_outer(d)
        total = total + mix_s.stage2[d - 1].astype(f32)
    hidden_s[...] = total
    root = lax.rsqrt(jnp.mean(total * total, axis=-1, keepdims=True) + 1e-06)
    me = mix_s.me
    n2[me] = (total * root * gain_ref[...]).astype(bf16)
    gather = Gather("tp", count, n2, n2_send, n2_recv)
    gather.start()
    loads[2].wait()
    for item in ups:
        item.arrive_all()
    up_local.wait()
    tall, hidden_cols = gate_w.shape

    def up_whole():
        return up_w[...].reshape(tall, hidden_cols)


    def block_ffn(b):
        rows = n2[b]
        gate_pre = dot_nn(rows, gate_w[...])
        up_pre = dot_nn(rows, up_whole())
        sig = jax.nn.sigmoid(gate_pre)
        silu = gate_pre * sig
        d_active = dact_s[b]
        d_gate = (d_active * up_pre * (sig + silu * (1.0 - sig))).astype(bf16)
        d_up = (d_active * silu).astype(bf16)
        dgate_s[b] = d_gate
        dup_s[b] = d_up
        act_s[b] = (silu * up_pre).astype(bf16)
        return dot_nt(d_gate, gate_w[...]) + dot_nt(d_up, up_whole())

    own_part = block_ffn(me)
    hold = {0: own_part}
    across = gather.block(0, True)
    gather.arrive(across)
    dn_s.out[0] = block_ffn(across).astype(bf16)
    dn_s.send_across(0)
    for d in range(1, outers):
        gather.forward(d)
    for d in range(1, outers):
        index = gather.block(d, True)
        gather.arrive(index)
        back = outers - d
        dn_s.out[back] = block_ffn(index).astype(bf16)
        dn_s.send_across(back)
    for d in range(1, outers):
        index = gather.block(d, False)
        back = outers - d
        part = block_ffn(index)
        dn_s.take_across(back)
        dn_s.send2[back - 1] = (part + dn_s.stage[back].astype(f32)).astype(bf16)
        dn_s.send_outer(back)
    for d in order:
        b = ffn_s.target(d, True)
        ffn_s.out[d] = dot_nt(act_s[b], down_w[...]).astype(bf16)
        ffn_s.send_across(d)
    width = n2.shape[2]
    depth = width // fsdp_count
    g_cols = max(256, depth)
    per = g_cols // depth

    def down_grad(k, carry):
        cols = pl.ds(pl.multiple_of(k * g_cols, g_cols), g_cols)
        total = dot_tn(cot_rows[0, :, cols], act_s[0])
        for b in range(1, count):
            total = total + dot_tn(cot_rows[b, :, cols], act_s[b])
        for j in range(per):
            g_down_full[k * per + j] = total[j * depth : (j + 1) * depth].astype(bf16)
        return carry

    lax.fori_loop(0, width // g_cols, down_grad, 0)
    for item in downs:
        item.start()
    dn_s.take_across(0)
    d_norm = own_part + dn_s.stage[0].astype(f32)
    for d in range(1, outers):
        dn_s.take_outer(d)
        d_norm = d_norm + dn_s.stage2[d - 1].astype(f32)
    hidden = hidden_s[...]
    root = lax.rsqrt(jnp.mean(hidden * hidden, axis=-1, keepdims=True) + 1e-06)
    scaled = hidden * root
    g_gain_ref[...] = jnp.sum(d_norm * scaled, axis=0, keepdims=True)
    pulled = d_norm * gain_ref[...]
    d_hidden = cot_ref[...].astype(f32) + root * (
        pulled - scaled * jnp.mean(pulled * scaled, axis=-1, keepdims=True)
    )
    d_hidden_ref[...] = d_hidden
    dh[me] = d_hidden.astype(bf16)
    gather2 = Gather("tp", count, dh, dh_send, dh_recv)
    gather2.start()
    for d in order:
        part = dot_nt(act_s[ffn_s.target(d, False)], down_w[...])
        ffn_s.take_across(d)
        if d:
            ffn_s.send2[d - 1] = (part + ffn_s.stage[d].astype(f32)).astype(bf16)
            ffn_s.send_outer(d)
        else:
            output_ref[...] = hidden_s[...] + part + ffn_s.stage[0].astype(f32)
    downs[0].turn(g_down_out)

    def gate_grad(k, carry):
        cols = pl.ds(pl.multiple_of(k * g_cols, g_cols), g_cols)
        gate_total = dot_tn(n2[0, :, cols], dgate_s[0])
        up_total = dot_tn(n2[0, :, cols], dup_s[0])
        for b in range(1, count):
            gate_total = gate_total + dot_tn(n2[b, :, cols], dgate_s[b])
            up_total = up_total + dot_tn(n2[b, :, cols], dup_s[b])
        g_gate_ref[cols, :] = gate_total.astype(bf16)
        g_up_ref[cols, :] = up_total.astype(bf16)
        return carry

    lax.fori_loop(0, width // g_cols, gate_grad, 0)
    for d in range(1, outers):
        gather2.forward(d)
    for item in downs[1:]:
        item.turn(g_down_out)
    for d in range(outers):
        gather2.arrive(gather2.block(d, True))
    for b in range(count):
        d_mixer_ref[b] = dot_nn(dh[b], out_w_ref[...])

    def out_grad(k, carry):
        cols = pl.ds(pl.multiple_of(k * g_cols, g_cols), g_cols)
        total = dot_tn(dh[0, :, cols], nm_ref[0])
        for b in range(1, count):
            total = total + dot_tn(dh[b, :, cols], nm_ref[b])
        g_out_ref[cols, :] = total.astype(bf16)
        return carry

    lax.fori_loop(0, width // g_cols, out_grad, 0)
    for d in range(1, outers):
        ffn_s.take_outer(d)
        output_ref[...] = output_ref[...] + ffn_s.stage2[d - 1].astype(f32)
    for item in downs:
        item.close(g_down_out)
    for part in [mix_s, gather, dn_s, ffn_s, gather2] + ups + downs:
        part.finish()


def ffn_all(nm, tokens, cotangent, out_w, gain, cot_rows, gate_w, up_w, down_w, ident):
    count, fsdp_count = lax.axis_size("tp"), lax.axis_size("fsdp")
    rows, width = tokens.shape
    depth = width // fsdp_count
    splits = parts_of(depth, 2)
    hidden = gate_w.shape[1]
    values = out_w.shape[1]
    f32, bf16 = jnp.float32, jnp.bfloat16
    vmem = pl.BlockSpec(memory_space=pltpu.VMEM)
    anys = pl.BlockSpec(memory_space=pl.ANY)
    dma = pltpu.SemaphoreType.DMA
    outs = [
        jax.ShapeDtypeStruct((rows, width), f32),
        jax.ShapeDtypeStruct((rows, width), f32),
        jax.ShapeDtypeStruct((count, rows, values), f32),
        jax.ShapeDtypeStruct((width, hidden), bf16),
        jax.ShapeDtypeStruct((width, hidden), bf16),
        jax.ShapeDtypeStruct((depth, hidden), f32),
        jax.ShapeDtypeStruct((width, values), bf16),
        jax.ShapeDtypeStruct((1, width), f32),
    ]
    scratch = [
        pltpu.VMEM((count, rows, width), bf16),
        pltpu.VMEM((width, hidden), bf16),
        pltpu.VMEM((fsdp_count, depth, hidden), bf16),
        pltpu.VMEM((width, hidden), bf16),
        pltpu.VMEM((count, rows, width), bf16),
        pltpu.VMEM((count, rows, width), bf16),
        pltpu.VMEM((count, rows, hidden), bf16),
        pltpu.VMEM((count, rows, hidden), bf16),
        pltpu.VMEM((count, rows, hidden), bf16),
        pltpu.VMEM((rows, width), f32),
        pltpu.VMEM((count, rows, hidden), f32),
        pltpu.VMEM((fsdp_count, depth, hidden), bf16),
        dma((3,)),
        dma,
        dma((count - 1,)),
        dma((count,)),
        dma((count - 1,)),
        dma((count,)),
    ]
    for _ in splits:
        scratch += [dma((fsdp_count - 1,)), dma((fsdp_count,))]
    for part in splits:
        size = depth if part is None else part[1]
        scratch += scatter_scratch(fsdp_count, size, hidden, full=True)
    for _ in range(3):
        scratch += scatter_scratch(count, rows, width)
    return pl.pallas_call(
        functools.partial(ffn_kernel, count, fsdp_count, splits),
        out_shape=outs,
        in_specs=[vmem] * 5 + [anys] * 4,
        out_specs=[vmem] * len(outs),
        scratch_shapes=scratch,
        compiler_params=comm_params(ident, 60),
        name="ffn",
    )(nm, tokens, cotangent, out_w, gain, cot_rows, gate_w, up_w, down_w)


def exchange_small(axis, count, src, buf, send, recv, spread):
    me = lax.axis_index(axis)
    copies = []
    for d in range(1, count):
        peer = lax.rem(me + d, count)
        copy = pltpu.make_async_remote_copy(
            src_ref=src.at[peer] if spread else src,
            dst_ref=buf.at[d - 1],
            send_sem=send.at[d - 1],
            recv_sem=recv.at[d - 1],
            device_id=on_axis(axis, peer),
            device_id_type=MESH,
        )
        copy.start()
        copies.append(copy)
    return copies


def last_kernel(tp_count, fsdp_count, widths, *refs):
    bf16, f32 = jnp.bfloat16, jnp.float32
    refs = list(refs)

    def take(number):
        out = refs[:number]
        del refs[:number]
        return out

    number = len(widths)
    d_raw_ref, n1_ref, tok_ref, gain_ref, d_hidden_ref, small_ref = take(6)
    weights = take(number)
    d_tok_ref, small_own_ref, small_all_ref = take(3)
    outs = take(number - 1)
    gate_out, rest_out = take(2)
    outs.append(take(1)[0])
    small_send, small_buf, small_buf2 = take(3)
    small_sems = take(4)
    dn = take(8)
    fulls = take(number)
    sets = [take(7) for _ in range(number)]
    entry_barrier([("fsdp", fsdp_count), ("tp", tp_count)], everyone=True)
    dn_s = Scatter("tp", tp_count, dn[0], dn[1], dn[2], dn[3], dn[4:])
    sums = [
        Scatter("fsdp", fsdp_count, None, s[0], s[1], s[2], s[3:], full=full)
        for s, full in zip(sets, fulls)
    ]
    width = n1_ref.shape[2]
    depth = width // fsdp_count
    chunk = max(256, depth)
    per = chunk // depth
    starts = [sum(widths[:k]) for k in range(number)]

    def weight_grad(item):
        full, at, size = fulls[item], starts[item], widths[item]

        def step(k, carry):
            cols = pl.ds(pl.multiple_of(k * chunk, chunk), chunk)
            total = dot_tn(n1_ref[0, :, cols], d_raw_ref[0, :, at : at + size])
            for b in range(1, tp_count):
                total = total + dot_tn(n1_ref[b, :, cols], d_raw_ref[b, :, at : at + size])
            for j in range(per):
                full[k * per + j] = total[j * depth : (j + 1) * depth].astype(bf16)
            return carry

        lax.fori_loop(0, width // chunk, step, 0)

    def input_grad(b):
        total = None
        for item in range(number):
            at, size = starts[item], widths[item]
            weight = weights[item][...].reshape(width, size)
            piece = dot_nt(d_raw_ref[b, :, at : at + size], weight)
            total = piece if total is None else total + piece
        return total

    turns = list(reversed(range(number)))
    weight_grad(turns[0])
    sums[turns[0]].start()
    for d in dn_s.order():
        dn_s.out[d] = input_grad(dn_s.target(d, True)).astype(bf16)
        dn_s.send_across(d)
    weight_grad(turns[1])
    sums[turns[1]].start()
    held = None
    for d in dn_s.order():
        part = input_grad(dn_s.target(d, False))
        dn_s.take_across(d)
        if d:
            dn_s.send2[d - 1] = (part + dn_s.stage[d].astype(f32)).astype(bf16)
            dn_s.send_outer(d)
        else:
            held = part + dn_s.stage[0].astype(f32)
    d_tok_ref[...] = held
    sums[turns[0]].turn(outs[turns[0]])
    for k in range(2, number):
        weight_grad(turns[k])
        sums[turns[k]].start()
        sums[turns[k - 1]].turn(outs[turns[k - 1]])
    held = d_tok_ref[...]
    for d in range(1, dn_s.outers):
        dn_s.take_outer(d)
        held = held + dn_s.stage2[d - 1].astype(f32)
    tokens = tok_ref[...].astype(f32)
    root = lax.rsqrt(jnp.mean(tokens * tokens, axis=-1, keepdims=True) + 1e-06)
    scaled = tokens * root
    gain_part = jnp.sum(held * scaled, axis=0, keepdims=True)
    pulled = held * gain_ref[...]
    d_tok_ref[...] = d_hidden_ref[...] + root * (
        pulled - scaled * jnp.mean(pulled * scaled, axis=-1, keepdims=True)
    )
    small_send[...] = small_ref[...]
    for f in range(fsdp_count):
        small_send[f, 0:1, 0:depth] = gain_part[:, f * depth : (f + 1) * depth]
    copies = exchange_small(
        "fsdp", fsdp_count, small_send, small_buf, small_sems[0], small_sems[1], True
    )
    sums[turns[-1]].turn(outs[turns[-1]])
    small_sum = small_send[lax.axis_index("fsdp")]
    for d, copy in enumerate(copies):
        copy.wait_recv()
        small_sum = small_sum + small_buf[d]
    small_own_ref[...] = small_sum
    copies2 = exchange_small(
        "tp", tp_count, small_own_ref, small_buf2, small_sems[2], small_sems[3], False
    )
    for k in turns:
        sums[k].close(outs[k])
    gate_out[...] = outs[-1][:, : gate_out.shape[1]]
    rest_out[...] = outs[-1][:, gate_out.shape[1] :]
    for d, copy in enumerate(copies2):
        copy.wait_recv()
        small_sum = small_sum + small_buf2[d]
    small_all_ref[...] = small_sum
    for copy in copies + copies2:
        copy.wait_send()
    for item in [dn_s] + sums:
        item.finish()


def last_all(d_raw, n1, tokens, gain, d_hidden, small, weights, gate_cols, ident):
    tp_count, fsdp_count = lax.axis_size("tp"), lax.axis_size("fsdp")
    rows, width = tokens.shape
    widths = [weight.shape[2] for weight in weights]
    depth = width // fsdp_count
    f32, bf16 = jnp.float32, jnp.bfloat16
    vmem = pl.BlockSpec(memory_space=pltpu.VMEM)
    dma = pltpu.SemaphoreType.DMA
    outs = [
        jax.ShapeDtypeStruct((rows, width), f32),
        jax.ShapeDtypeStruct(small.shape[1:], f32),
        jax.ShapeDtypeStruct(small.shape[1:], f32),
    ] + [
        jax.ShapeDtypeStruct((depth, size), f32)
        for size in widths[:-1] + [gate_cols, widths[-1] - gate_cols]
    ]
    scratch = [
        pltpu.VMEM((depth, widths[-1]), f32),
        pltpu.VMEM(small.shape, f32),
        pltpu.VMEM((fsdp_count - 1,) + small.shape[1:], f32),
        pltpu.VMEM((tp_count - 1,) + small.shape[1:], f32),
        dma((fsdp_count - 1,)),
        dma((fsdp_count - 1,)),
        dma((tp_count - 1,)),
        dma((tp_count - 1,)),
    ]
    scratch += scatter_scratch(tp_count, rows, width)
    scratch += [pltpu.VMEM((fsdp_count, depth, size), bf16) for size in widths]
    for size in widths:
        scratch += scatter_scratch(fsdp_count, depth, size, full=True)
    return pl.pallas_call(
        functools.partial(last_kernel, tp_count, fsdp_count, widths),
        out_shape=outs,
        in_specs=[vmem] * (6 + len(weights)),
        out_specs=[vmem] * len(outs),
        scratch_shapes=scratch,
        compiler_params=comm_params(ident, 60),
        name="last",
    )(d_raw, n1, tokens, gain, d_hidden, small, *weights)


def split_two(value):
    top = value.astype(jnp.bfloat16)
    return top, (value - top.astype(jnp.float32)).astype(jnp.bfloat16)


def dot_three(left, right, dot):
    (a, b), (c, d) = split_two(left), split_two(right)
    return dot(a, c) + (dot(a, d) + dot(b, c))


def half(value):
    return value.astype(jnp.bfloat16)


def triangles():
    row = lax.broadcasted_iota(jnp.int32, (GROUP, GROUP), 0)
    col = lax.broadcasted_iota(jnp.int32, (GROUP, GROUP), 1)
    return row, col


def pair_mask(row, col, step):
    shift = step.bit_length() - 1
    high_row, high_col = row >> shift, col >> shift
    return ((high_row >> 1) == (high_col >> 1)) & (high_row > high_col)


def unit_inverses(lowers):
    row, col = triangles()
    eye = (row == col).astype(jnp.float32)
    mask = pair_mask(row, col, 1)
    inverses = [eye - jnp.where(mask, lower, 0.0) for lower in lowers]
    step = 2
    while step < GROUP:
        mask = pair_mask(row, col, step)
        corners = [half(jnp.where(mask, lower, 0.0)) for lower in lowers]
        tops = [half(inverse) for inverse in inverses]
        inner = [half(dot_nn(top, corner)) for top, corner in zip(tops, corners)]
        inverses = [
            inverse - dot_nn(left, top) for inverse, left, top in zip(inverses, inner, tops)
        ]
        step = step * 2
    rest = [
        eye - inverse - dot_three(lower, inverse, dot_nn)
        for inverse, lower in zip(inverses, lowers)
    ]
    return [
        inverse + dot_nn(half(inverse), half(gap)) for inverse, gap in zip(inverses, rest)
    ]


def conv_rows(padded, taps, ranges):
    rim = padded.shape[0] - GROUP
    total = taps[0:1] * padded[rim:]
    for lag in range(1, CONV):
        total = total + taps[lag : lag + 1] * (
            pltpu.roll(padded, lag, 0)[rim:] * ranges[lag - 1]
        )
    return total


def unit_norm(values):
    return lax.rsqrt(jnp.sum(values * values, axis=-1, keepdims=True) + 1e-06)


def soft_plus(value):
    return jnp.maximum(value, 0.0) + jnp.log1p(jnp.exp(-jnp.abs(value)))


class Chunk:
    def __init__(self, refs, head, heads, n, first_place):
        padded_ref, taps_ref, bd_ref, begin_ref, rate_ref, shift_ref = refs
        at_beta = heads * V + head
        self.head, self.n = head, n
        cols = (
            (head * K, K),
            (heads * K + head * K, K),
            (2 * heads * K + head * V, V),
        )
        self.cols = cols
        if isinstance(n, int):
            rows, padded_rows = pl.ds(n * GROUP, GROUP), pl.ds(n * GROUP, GROUP + RIM)
        else:
            start = pl.multiple_of(n * GROUP, GROUP)
            rows, padded_rows = pl.ds(start, GROUP), pl.ds(start, GROUP + RIM)
        self.rows = rows
        row, col = triangles()
        begin = begin_ref[rows, :]
        base = first_place + n * GROUP
        place = base + lax.broadcasted_iota(jnp.int32, (GROUP, 1), 0)
        self.ranges = [
            (place - lag >= begin).astype(jnp.float32) for lag in range(1, CONV)
        ]
        self.padded = [
            padded_ref[padded_rows, at : at + size].astype(jnp.float32) for at, size in cols
        ]
        self.taps = [taps_ref[:, at : at + size] for at, size in cols]
        self.pres = [
            conv_rows(padded, taps, self.ranges)
            for padded, taps in zip(self.padded, self.taps)
        ]
        self.sigs = [jax.nn.sigmoid(pre) for pre in self.pres]
        query, key, self.value = [pre * sig for pre, sig in zip(self.pres, self.sigs)]
        self.query_root, self.key_root = unit_norm(query), unit_norm(key)
        self.query = query * (self.query_root * K ** (-0.5))
        self.key = key * self.key_root
        self.beta = jax.nn.sigmoid(bd_ref[rows, at_beta : at_beta + 1])
        self.decay_in = bd_ref[rows, at_beta + heads : at_beta + heads + 1] + shift_ref[head]
        self.rate = rate_ref[head]
        decay = self.rate * soft_plus(self.decay_in)
        self.decay = decay
        lower = row >= col
        decay_row = jnp.sum(jnp.where(row == col, decay, 0.0), axis=0, keepdims=True)
        cumul = jnp.sum(jnp.where(lower, decay_row, 0.0), axis=1, keepdims=True)
        cumul_row = jnp.sum(jnp.where(row <= col, decay, 0.0), axis=0, keepdims=True)
        same = (begin <= base + col) & lower
        self.factor = jnp.where(same, jnp.exp(jnp.where(same, cumul - cumul_row, 0.0)), 0.0)
        self.carry = jnp.where(begin < base, jnp.exp(cumul), 0.0)
        self.scale = self.carry[GROUP - 1 :, :]
        last_alive = begin[GROUP - 1 :, :] <= place
        gap = cumul[GROUP - 1 :, :] - cumul
        self.last = jnp.where(last_alive, jnp.exp(jnp.where(last_alive, gap, 0.0)), 0.0)
        self.key_last = self.key * self.last
        self.weights = jnp.where(row > col, self.factor, 0.0)

    def sides(self):
        return jnp.concatenate(
            [self.beta * self.value, (self.beta * self.carry) * self.key], axis=1
        )


def mixer_kernel(heads, blocks, tp_count, fsdp_count, wide, splits, *refs):
    bf16, f32 = jnp.bfloat16, jnp.float32
    refs = list(refs)

    def take(number):
        out = refs[:number]
        del refs[:number]
        return out

    weight_count = len(splits)
    mixed_any, gate_ref, taps_ref, begin_ref, rate_ref, shift_ref, norm_ref = take(7)
    cot_any = take(1)[0]
    shards = take(weight_count)
    normed_ref, inv_ref, side_ref, query_ref, score_ref, state_ref, update_ref, out_ref = take(8)
    maps, scales, padded, pairs, cot_rows = take(5)
    wholes = take(weight_count)
    prefix, own_pair, rim_sems, load_sem, pair_send, pair_recv, cot_sems, cot_send, cot_recv = take(9)
    weight_sems = take(weight_count)
    piece_sems = [take(2) for _ in range(sum(len(split) for split in splits))]
    rows = blocks * GROUP
    mine = lax.axis_index("fsdp")
    load = pltpu.make_async_copy(mixed_any, padded.at[pl.ds(RIM, rows)], load_sem)
    load.start()
    entry_barrier([("fsdp", fsdp_count), ("tp", tp_count)], everyone=True)
    rim = pltpu.make_async_remote_copy(
        src_ref=mixed_any.at[pl.ds(rows - RIM, RIM)],
        dst_ref=padded.at[pl.ds(0, RIM)],
        send_sem=rim_sems.at[0],
        recv_sem=rim_sems.at[1],
        device_id=on_axis("fsdp", lax.rem(mine + 1, fsdp_count)),
        device_id_type=MESH,
    )
    rim.start()
    gathers, locals_ = [], []
    for k in range(weight_count):
        copy = pltpu.make_async_copy(shards[k], wholes[k].at[mine], weight_sems[k])
        copy.start()
        locals_.append(copy)
        for part in splits[k]:
            sems = piece_sems[len(gathers)]
            gathers.append(
                Gather(
                    "fsdp", fsdp_count, wholes[k], sems[0], sems[1], own=shards[k], part=part
                )
            )
    depth = 3
    for gather in gathers[:depth]:
        gather.start()
    cot = Gather("tp", tp_count, cot_rows, cot_send, cot_recv, own=cot_any)
    cot.start()
    cot_local = pltpu.make_async_copy(cot_any, cot_rows.at[cot.me], cot_sems)
    cot_local.start()
    load.wait()
    rim.wait()
    first_place = mine * rows
    source = (padded, taps_ref, gate_ref, begin_ref, rate_ref, shift_ref)
    row, col = triangles()
    turns = blocks // wide

    def pump(k):
        if k < len(gathers):
            gathers[k].forward_all()
            if k + depth < len(gathers):
                gathers[k + depth].start()

    for h in range(heads):
        own_pair[h] = jnp.concatenate(
            [(row == col).astype(f32), jnp.zeros((K, V), f32)], axis=1
        )

    def front(step, carry):
        units = [
            Chunk(source, h, heads, step * wide + j, first_place)
            for j in range(wide)
            for h in range(heads)
        ]
        lowers = [
            unit.beta * dot_three(unit.key, unit.key, dot_nt) * unit.weights for unit in units
        ]
        inverses = [half(inverse) for inverse in unit_inverses(lowers)]
        solved = [dot_nn(inv, half(unit.sides())) for inv, unit in zip(inverses, units)]
        for unit, inv, sides in zip(units, inverses, solved):
            h, n = unit.head, unit.n
            inv_ref[h, n] = inv
            side_ref[h, n] = half(sides)
            query_ref[h, n] = half(unit.query * unit.carry)
            score_ref[h, n] = half(
                dot_nt(half(unit.query), half(unit.key)) * unit.factor
            )
            driven = dot_tn(half(unit.key_last), half(sides))
            maps[h, n] = driven[:, V:]
            scales[h, n] = jnp.broadcast_to(unit.scale, (8, 128))
            pair = own_pair[h]
            prefix[h, n] = pair
            moved = dot_three(driven[:, V:], pair, dot_nn)
            drive = jnp.concatenate([jnp.zeros((K, K), f32), driven[:, :V]], axis=1)
            own_pair[h] = unit.scale * pair + drive - moved

        return carry

    lax.fori_loop(0, turns, front, 0)
    for h in range(heads):
        pairs[mine, pl.ds(h * K, K), :] = half(own_pair[h])
    ring = Gather("fsdp", fsdp_count, pairs, pair_send, pair_recv)
    ring.start()
    cot.forward_all()
    pump(0)
    ring.forward_all()
    pump(1)
    ring.arrive_all()
    hops = min(fsdp_count - 1, -(-MAXLEN // rows))
    states = [jnp.zeros((K, V), f32) for _ in range(heads)]
    for hop in range(hops, 0, -1):
        spot = jnp.maximum(mine - hop, 0)
        for h in range(heads):
            piece = pairs[spot, pl.ds(h * K, K), :]
            top, low = split_two(states[h])
            new = dot_nn(piece[:, :K], top) + dot_nn(piece[:, :K], low)
            states[h] = jnp.where(mine >= hop, new + piece[:, K:].astype(f32), states[h])

    def back(n, carry):
        at = pl.ds(pl.multiple_of(n * GROUP, GROUP), GROUP)
        for h in range(heads):
            pair = prefix[h, n]
            start = half(dot_three(pair[:, :K], states[h], dot_nn) + pair[:, K:])
            state_ref[h, n] = start
            sides = side_ref[h, n]
            update = half(sides[:, :V].astype(f32) - dot_nn(sides[:, V:], start))
            update_ref[h, n] = update
            out = dot_nn(query_ref[h, n], start) + dot_nn(score_ref[h, n], update)
            out_ref[h, n] = half(out)
            gate = gate_ref[at, h * V : (h + 1) * V]
            root = lax.rsqrt(jnp.mean(out * out, axis=-1, keepdims=True) + 1e-06)
            normed_ref[at, h * V : (h + 1) * V] = half(
                out * root * norm_ref[...] * (gate * jax.nn.sigmoid(gate))
            )
        for k in range(2, len(gathers)):

            @pl.when(n == min(2 * (k - 2), blocks - 1))
            def _(k=k):
                pump(k)

        return carry

    lax.fori_loop(0, blocks, back, 0)
    cot.arrive_all()
    for gather in gathers:
        gather.arrive_all()
    for copy in locals_ + [cot_local]:
        copy.wait()
    for gather in gathers + [ring, cot]:
        gather.finish()


def mixer_all(mixed, gate, taps, begins, rate, shift, norm, cotangent, shards, ident):
    tp_count, fsdp_count = lax.axis_size("tp"), lax.axis_size("fsdp")
    heads = rate.shape[0]
    splits = [parts_of(shard.shape[0], 2) for shard in shards]
    rows = mixed.shape[0]
    blocks = rows // GROUP
    wide = 2 if blocks % 2 == 0 else 1
    f32, bf16 = jnp.float32, jnp.bfloat16
    vmem = pl.BlockSpec(memory_space=pltpu.VMEM)
    smem = pl.BlockSpec(memory_space=pltpu.SMEM)
    anys = pl.BlockSpec(memory_space=pl.ANY)
    dma = pltpu.SemaphoreType.DMA
    shape = jax.ShapeDtypeStruct
    outs = [
        shape((rows, heads * V), bf16),
        shape((heads, blocks, GROUP, GROUP), bf16),
        shape((heads, blocks, GROUP, V + K), bf16),
        shape((heads, blocks, GROUP, K), bf16),
        shape((heads, blocks, GROUP, GROUP), bf16),
        shape((heads, blocks, K, V), bf16),
        shape((heads, blocks, GROUP, V), bf16),
        shape((heads, blocks, GROUP, V), bf16),
        shape((heads, blocks, K, K), f32),
        shape((heads, blocks, 8, 128), f32),
        shape((rows + RIM, mixed.shape[1]), bf16),
        shape((fsdp_count, heads * K, K + V), bf16),
        shape((tp_count,) + cotangent.shape, bf16),
    ] + [shape((fsdp_count,) + shard.shape, shard.dtype) for shard in shards]
    scratch = [
        pltpu.VMEM((heads, blocks, K, K + V), f32),
        pltpu.VMEM((heads, K, K + V), f32),
        dma((2,)),
        dma,
        dma((fsdp_count - 1,)),
        dma((fsdp_count,)),
        dma,
        dma((tp_count - 1,)),
        dma((tp_count,)),
    ]
    scratch += [dma] * len(shards)
    for _ in range(sum(len(split) for split in splits)):
        scratch += [dma((fsdp_count - 1,)), dma((fsdp_count,))]
    return pl.pallas_call(
        functools.partial(
            mixer_kernel, heads, blocks, tp_count, fsdp_count, wide, splits
        ),
        out_shape=outs,
        in_specs=[anys] + [vmem] * 3 + [smem] * 2 + [vmem] + [anys] * (1 + len(shards)),
        out_specs=[vmem] * 12 + [anys] * (1 + len(shards)),
        scratch_shapes=scratch,
        compiler_params=comm_params(ident, 60),
        name="mixer",
    )(mixed, gate, taps, begins, rate, shift, norm, cotangent, *shards)


def mixer_grad_kernel(heads, blocks, tp_count, fsdp_count, splits, *refs):
    bf16, f32 = jnp.bfloat16, jnp.float32
    refs = list(refs)

    def take(number):
        out = refs[:number]
        del refs[:number]
        return out

    extra_count = len(splits)
    padded, gate_ref, taps_ref, begin_ref, rate_ref, shift_ref, norm_ref = take(7)
    inv_ref, side_ref, query_ref, score_ref, state_ref, update_ref, out_ref = take(7)
    maps, scales, pairs, dm_ref = take(4)
    extras = take(extra_count)
    d_raw_ref, g_taps_ref, g_decay_ref, g_norm_ref = take(4)
    extra_outs = take(extra_count)
    d_out, base, local, d_state, halo, tail, d_all, rim_buf = take(8)
    rim_sems, ring_send, ring_recv = take(3)
    rows = blocks * GROUP
    mine = lax.axis_index("fsdp")
    first_place = mine * rows
    mixed_cols = 2 * heads * K + heads * V
    entry_barrier([("fsdp", fsdp_count)], everyone=True)
    sums, sum_outs = [], []
    for extra, out, split in zip(extras, extra_outs, splits):
        for part in split:
            s = take(7)
            sums.append(
                Scatter(
                    "fsdp", fsdp_count, None, s[0], s[1], s[2], s[3:], full=extra, part=part
                )
            )
            sum_outs.append(out)
    depth = 4
    for item in sums[:depth]:
        item.start()

    def pump(k):
        if k < len(sums):
            if k + depth < len(sums):
                sums[k + depth].start()
            sums[k].turn(sum_outs[k])

    g_norm_ref[...] = jnp.zeros_like(g_norm_ref)
    g_taps_ref[...] = jnp.zeros_like(g_taps_ref)
    g_decay_ref[...] = jnp.zeros_like(g_decay_ref)
    halo[...] = jnp.zeros_like(halo)
    source = (padded, taps_ref, gate_ref, begin_ref, rate_ref, shift_ref)
    row, col = triangles()

    def first(n, carry):
        at = pl.ds(pl.multiple_of(n * GROUP, GROUP), GROUP)
        for h in range(heads):
            cols = slice(h * V, (h + 1) * V)
            out = out_ref[h, n].astype(f32)
            root = lax.rsqrt(jnp.mean(out * out, axis=-1, keepdims=True) + 1e-06)
            normed = out * root
            gate = gate_ref[at, cols]
            sig = jax.nn.sigmoid(gate)
            silu = gate * sig
            given = dm_ref[at, cols]
            g_norm_ref[...] += jnp.sum(given * normed * silu, axis=0, keepdims=True)
            pulled = given * norm_ref[...]
            d_raw_ref[at, mixed_cols + h * V : mixed_cols + (h + 1) * V] = half(
                pulled * normed * (sig + silu * (1.0 - sig))
            )
            pulled = pulled * silu
            grad = root * (pulled - normed * jnp.mean(pulled * normed, axis=-1, keepdims=True))
            grad = half(grad)
            d_out[h, n] = grad
            through = dot_tn(score_ref[h, n], grad)
            base[h, n] = through
            key_part = half(side_ref[h, n][:, V:])
            local[h, n] = dot_tn(query_ref[h, n], grad) - dot_tn(key_part, half(through))
        return carry

    lax.fori_loop(0, blocks, first, 0)
    pump(0)

    def pull_state(n, h, grad):
        scale = scales[h, n][0:1, 0:1]
        return scale * grad + local[h, n] - dot_three(maps[h, n], grad, dot_tn)

    for h in range(heads):
        d_state[h] = jnp.zeros((K, V), f32)

    def chain(step, carry):
        n = blocks - 1 - step
        for h in range(heads):
            d_state[h] = pull_state(n, h, d_state[h])
        return carry

    lax.fori_loop(0, blocks, chain, 0)
    for h in range(heads):
        d_all[mine, pl.ds(h * K, K), :] = half(d_state[h])
    ring = Gather("fsdp", fsdp_count, d_all, ring_send, ring_recv)
    ring.start()
    pump(1)
    ring.forward_all()
    pump(2)
    ring.arrive_all()
    hops = min(fsdp_count - 1, -(-MAXLEN // rows))
    for h in range(heads):
        grad = jnp.zeros((K, V), f32)
        for hop in range(hops, 0, -1):
            spot = jnp.minimum(mine + hop, fsdp_count - 1)
            piece = pairs[spot, pl.ds(h * K, K), :][:, :K]
            top, low = split_two(grad)
            new = dot_tn(piece, top) + dot_tn(piece, low)
            new = new + d_all[spot, pl.ds(h * K, K), :].astype(f32)
            grad = jnp.where(mine + hop < fsdp_count, new, grad)
        d_state[h] = grad

    def second(step, carry):
        n = blocks - 1 - step
        at = pl.ds(pl.multiple_of(n * GROUP, GROUP), GROUP)
        lane = lax.broadcasted_iota(jnp.int32, (1, g_decay_ref.shape[1]), 1)
        smalls = []
        for h in range(heads):
            unit = Chunk(source, h, heads, n, first_place)
            query, key, key_last = half(unit.query), half(unit.key), half(unit.key_last)
            after = d_state[h]
            d_state[h] = pull_state(n, h, after)
            after_half = half(after)
            state, grad, update = state_ref[h, n], d_out[h, n], update_ref[h, n]
            sides = side_ref[h, n]
            d_update = half(base[h, n] + dot_nn(key_last, after_half))
            d_key_part = -dot_nt(d_update, state)
            read = dot_nt(grad, state)
            d_query = unit.carry * read
            d_carry = jnp.sum(read * unit.query, axis=1, keepdims=True)
            d_scores = dot_nt(grad, update)
            d_key_last = dot_nt(update, after_half)
            d_scale = jnp.sum(
                jnp.sum(after * state.astype(f32), axis=1, keepdims=True), axis=0, keepdims=True
            )
            d_sides = dot_tn(
                inv_ref[h, n], jnp.concatenate([d_update, half(d_key_part)], axis=1)
            )
            d_lower = -dot_nt(half(d_sides), half(sides))
            gram = dot_nt(key, key) * unit.weights
            pulled = d_lower * gram
            d_beta = jnp.sum(pulled, axis=1, keepdims=True)
            moved = unit.beta * pulled + d_scores * score_ref[h, n].astype(f32)
            d_gram = half(d_lower * (unit.beta * unit.weights))
            d_qk = half(d_scores * unit.factor)
            d_query = d_query + dot_nn(d_qk, key)
            d_key = dot_tn(d_qk, query) + dot_nn(d_gram, key) + dot_tn(d_gram, key)
            d_key = d_key + d_key_last * unit.last
            d_last = jnp.sum(d_key_last * unit.key_last, axis=1, keepdims=True)
            d_value_side, d_key_side = d_sides[:, :V], d_sides[:, V:]
            d_beta = d_beta + jnp.sum(d_value_side * unit.value, axis=1, keepdims=True)
            d_value = unit.beta * d_value_side
            mixed_side = jnp.sum(d_key_side * unit.key, axis=1, keepdims=True)
            d_key = d_key + (unit.beta * unit.carry) * d_key_side
            d_beta = d_beta + unit.carry * mixed_side
            d_carry = d_carry + unit.beta * mixed_side
            at_end = lax.broadcasted_iota(jnp.int32, (GROUP, 1), 0) == GROUP - 1
            d_carry = d_carry + jnp.where(at_end, d_scale, 0.0)
            d_cumul = d_carry * unit.carry - d_last
            d_cumul = d_cumul + jnp.where(
                at_end, jnp.sum(d_last, axis=0, keepdims=True), 0.0
            )
            d_cumul = d_cumul + jnp.sum(moved, axis=1, keepdims=True)
            d_row = jnp.sum(jnp.where(row == col, d_cumul, 0.0), axis=0, keepdims=True)
            d_row = d_row - jnp.sum(moved, axis=0, keepdims=True)
            d_decay = jnp.sum(jnp.where(col >= row, d_row, 0.0), axis=1, keepdims=True)
            d_decay_in = d_decay * unit.rate * jax.nn.sigmoid(unit.decay_in)
            log_sum = jnp.sum(d_decay * unit.decay, axis=0, keepdims=True)
            bias_sum = jnp.sum(d_decay_in, axis=0, keepdims=True)
            g_decay_ref[...] += jnp.where(lane == h, log_sum, 0.0) + jnp.where(
                lane == heads + h, bias_sum, 0.0
            )
            smalls.append((d_beta * unit.beta * (1.0 - unit.beta), d_decay_in))
            unscaled = unit.query * K**0.5
            d_query = d_query * K ** (-0.5)
            d_query = unit.query_root * (
                d_query - unscaled * jnp.sum(d_query * unscaled, axis=1, keepdims=True)
            )
            d_key = unit.key_root * (
                d_key - unit.key * jnp.sum(d_key * unit.key, axis=1, keepdims=True)
            )
            for part, given in enumerate((d_query, d_key, d_value)):
                start, size = unit.cols[part]
                sig, pre = unit.sigs[part], unit.pres[part]
                d_pre = given * sig * (1.0 + pre * (1.0 - sig))
                taps, spread = unit.taps[part], unit.padded[part]
                total = taps[0:1] * d_pre
                edge = jnp.zeros((RIM, size), f32)
                grads = [jnp.sum(d_pre * spread[RIM:], axis=0, keepdims=True)]
                whole = jnp.concatenate([edge, total], axis=0)
                for lag in range(1, CONV):
                    masked = d_pre * unit.ranges[lag - 1]
                    grads.append(
                        jnp.sum(
                            masked * pltpu.roll(spread, lag, 0)[RIM:], axis=0, keepdims=True
                        )
                    )
                    ext = jnp.concatenate([edge, taps[lag : lag + 1] * masked], axis=0)
                    whole = whole + pltpu.roll(ext, GROUP + RIM - lag, 0)
                for lag in range(CONV):
                    g_taps_ref[lag : lag + 1, start : start + size] += grads[lag]
                body = whole[RIM:]
                ended = body[GROUP - RIM :] + halo[:, start : start + size]
                halo[:, start : start + size] = whole[:RIM]
                body = jnp.concatenate([body[: GROUP - RIM], ended], axis=0)
                d_raw_ref[at, start : start + size] = half(body)

                @pl.when(step == 0)
                def _():
                    tail[:, start : start + size] = ended

        spot = lax.broadcasted_iota(jnp.int32, (GROUP, 2 * heads), 1)
        joined = jnp.zeros((GROUP, 2 * heads), f32)
        for h, (d_beta, d_decay_in) in enumerate(smalls):
            joined = joined + jnp.where(spot == h, d_beta, 0.0)
            joined = joined + jnp.where(spot == heads + h, d_decay_in, 0.0)
        d_raw_ref[at, mixed_cols + heads * V :] = half(joined)
        for k in range(3, len(sums)):

            @pl.when(step == min((k - 3) * (blocks - 2) // max(len(sums) - 3, 1), blocks - 1))
            def _(k=k):
                pump(k)

        return carry

    lax.fori_loop(0, blocks, second, 0)
    rim = pltpu.make_async_remote_copy(
        src_ref=halo,
        dst_ref=rim_buf,
        send_sem=rim_sems.at[0],
        recv_sem=rim_sems.at[1],
        device_id=on_axis("fsdp", lax.rem(mine + fsdp_count - 1, fsdp_count)),
        device_id_type=MESH,
    )
    rim.start()
    for item, out in zip(sums, sum_outs):
        item.close(out)
    rim.wait()
    d_raw_ref[rows - RIM : rows, 0:mixed_cols] = half(tail[...] + rim_buf[...])
    for item in sums + [ring]:
        item.finish()


def mixer_grad_all(
    padded, gate, taps, begins, rate, shift, norm, saved, pairs, d_mixer, extras, ident
):
    tp_count, fsdp_count = lax.axis_size("tp"), lax.axis_size("fsdp")
    heads = rate.shape[0]
    splits = [parts_of(extra.shape[1], 4) for extra in extras]
    rows = gate.shape[0]
    blocks = rows // GROUP
    mixed_cols = padded.shape[1]
    f32, bf16 = jnp.float32, jnp.bfloat16
    vmem = pl.BlockSpec(memory_space=pltpu.VMEM)
    smem = pl.BlockSpec(memory_space=pltpu.SMEM)
    dma = pltpu.SemaphoreType.DMA
    shape = jax.ShapeDtypeStruct
    outs = [
        shape((rows, mixed_cols + heads * V + 2 * heads), bf16),
        shape((CONV, mixed_cols), f32),
        shape((1, 128), f32),
        shape((1, V), f32),
    ] + [shape(extra.shape[1:], f32) for extra in extras]
    scratch = [
        pltpu.VMEM((heads, blocks, GROUP, V), bf16),
        pltpu.VMEM((heads, blocks, GROUP, V), f32),
        pltpu.VMEM((heads, blocks, K, V), f32),
        pltpu.VMEM((heads, K, V), f32),
        pltpu.VMEM((RIM, mixed_cols), f32),
        pltpu.VMEM((RIM, mixed_cols), f32),
        pltpu.VMEM((fsdp_count, heads * K, V), bf16),
        pltpu.VMEM((RIM, mixed_cols), f32),
        dma((2,)),
        dma((fsdp_count - 1,)),
        dma((fsdp_count,)),
    ]
    for extra, split in zip(extras, splits):
        for part in split:
            size = extra.shape[1] if part is None else part[1]
            scratch += scatter_scratch(fsdp_count, size, extra.shape[2], full=True)
    return pl.pallas_call(
        functools.partial(
            mixer_grad_kernel, heads, blocks, tp_count, fsdp_count, splits
        ),
        out_shape=outs,
        in_specs=[vmem] * 4 + [smem] * 2 + [vmem] * (12 + len(extras)),
        out_specs=[vmem] * len(outs),
        scratch_shapes=scratch,
        compiler_params=comm_params(ident, 60),
        name="mixer_grad",
    )(padded, gate, taps, begins, rate, shift, norm, *saved, pairs, d_mixer, *extras)


def shards(
    tokens,
    lengths,
    attn_gain,
    w_query,
    w_key,
    w_value,
    w_gate_out,
    w_beta,
    w_decay,
    conv_query,
    conv_key,
    conv_value,
    decay_log,
    decay_bias,
    out_gain,
    w_out,
    ffn_gain,
    w_ffn_gate,
    w_ffn_up,
    w_ffn_down,
    cotangent,
):
    count = lax.axis_size("fsdp")
    shard_rows = tokens.shape[0]
    query_cols, value_cols = w_query.shape[1], w_value.shape[1]
    hidden_cols = w_ffn_gate.shape[1]
    head_count = query_cols // K
    mixed_cols = 2 * query_cols + value_cols
    raw_cols = mixed_cols + value_cols

    tp_count = lax.axis_size("tp")
    width = tokens.shape[1]
    small_list = (attn_gain, ffn_gain, out_gain, conv_query, conv_key, conv_value)
    small = jnp.concatenate([part.astype(jnp.float32).reshape(-1) for part in small_list])
    small_width = -(-small.shape[0] // 1024) * 1024
    small = jnp.pad(small, (0, small_width - small.shape[0])).reshape(8, -1)
    gate_shard = jnp.concatenate([w_gate_out, w_beta, w_decay], axis=1)
    normed_blocks, small, *mixer_w, mixed_raw, gate_raw = front_all(
        tokens, small, [w_query, w_key, w_value, gate_shard], 0
    )
    small = small.reshape(count, -1)
    smalls, at = ([], 0)
    for part in small_list:
        piece = small[:, at : at + part.size]
        at = at + part.size
        if part.ndim == 3:
            piece = piece.reshape((count,) + part.shape).transpose(1, 2, 0, 3)
            smalls.append(piece.reshape(part.shape[0], part.shape[1], -1))
        else:
            smalls.append(piece.reshape(-1))
    gain_one, gain_two, norm_out, query_taps, key_taps, value_taps = smalls
    row_count = mixed_raw.shape[0]
    positions = lax.axis_index("fsdp") * row_count + jnp.arange(row_count, dtype=jnp.int32)
    begins = seq_begin(lengths, positions)
    taps = jnp.concatenate(
        [part.reshape(CONV, -1) for part in (query_taps, key_taps, value_taps)], axis=1
    )
    common = (
        gate_raw,
        taps,
        begins.reshape(-1, 1),
        -jnp.exp(decay_log),
        decay_bias,
        norm_out.reshape(1, -1),
    )
    normed_mixer, *saved, padded, pairs, cot_blocks, out_t, down_t, ffn_gate_w = (
        mixer_all(
            mixed_raw,
            *common,
            cotangent,
            [w_out.T, w_ffn_down.T, w_ffn_gate],
            1,
        )
    )
    out_t, ffn_gate_w, down_t = [
        part.reshape(width, -1) for part in (out_t, ffn_gate_w, down_t)
    ]
    (
        output,
        d_hidden,
        d_mixer,
        g_gate,
        g_up,
        grad_down_t,
        g_out,
        gain_two_part,
    ) = ffn_all(
        normed_mixer.reshape(tp_count, shard_rows, -1),
        tokens,
        cotangent,
        out_t,
        gain_two.reshape(1, -1),
        cot_blocks,
        ffn_gate_w,
        w_ffn_up,
        down_t,
        2,
    )
    d_mixer = d_mixer.reshape(row_count, -1)
    gain_two_part = gain_two_part.reshape(-1)

    d_raw, g_taps, g_decay, norm_out_part, *grads_ffn = mixer_grad_all(
        padded,
        *common,
        saved,
        pairs,
        d_mixer,
        [part.reshape(count, width // count, -1) for part in (g_out, g_gate, g_up)],
        3,
    )
    grad_out_t, grad_w_ffn_gate, grad_w_ffn_up = grads_ffn
    d_taps = [
        part.reshape(CONV, head_count, -1)
        for part in jnp.split(g_taps, (query_cols, 2 * query_cols), axis=1)
    ]
    decay_pair = g_decay[0, : 2 * head_count]

    def spread(taps):
        taps = taps.reshape(taps.shape[0], taps.shape[1], count, -1)
        return taps.transpose(2, 0, 1, 3).reshape(count, -1)

    small_parts = [
        gain_two_part.reshape(count, -1),
        norm_out_part.reshape(count, -1),
        spread(d_taps[0]),
        spread(d_taps[1]),
        spread(d_taps[2]),
        jnp.broadcast_to(decay_pair[None, :], (count, decay_pair.shape[0])),
    ]
    small_cat = jnp.concatenate(small_parts, axis=1)
    lanes = -(-max(small_cat.shape[1], 7 * (width // count)) // (7 * 128)) * 128
    small_cat = jnp.pad(small_cat, ((0, 0), (lanes, 7 * lanes - small_cat.shape[1])))
    d_tokens, small_own, small_all, *grads_mixer = last_all(
        d_raw.reshape(tp_count, shard_rows, -1),
        normed_blocks,
        tokens,
        gain_one.reshape(1, -1),
        d_hidden,
        small_cat.reshape(count, 8, lanes),
        mixer_w,
        value_cols,
        4,
    )
    grad_w_ffn_down = grad_down_t.T
    grad_w_out = grad_out_t.T
    grads_w = grads_mixer[:4] + jnp.split(grads_mixer[4], 2, axis=1)
    small_cuts, at = ([], lanes)
    for part in small_parts:
        small_cuts.append(at)
        at = at + part.shape[1]
    small_cuts.append(at)
    own_parts = jnp.split(small_own.reshape(-1), small_cuts)
    all_parts = jnp.split(small_all.reshape(-1), small_cuts)
    small_out = [
        small_all[0, : width // count],
        all_parts[1],
        all_parts[2],
        own_parts[3],
        own_parts[4],
        own_parts[5],
        own_parts[6],
    ]
    return (
        output,
        d_tokens,
        small_out[0],
        *grads_w,
        small_out[3].reshape(conv_query.shape),
        small_out[4].reshape(conv_key.shape),
        small_out[5].reshape(conv_value.shape),
        small_out[6][:head_count],
        small_out[6][head_count:],
        small_out[2],
        grad_w_out,
        small_out[1],
        grad_w_ffn_gate,
        grad_w_ffn_up,
        grad_w_ffn_down,
    )


def solution(mesh):
    placed = (
        P(("fsdp", "tp"), None),
        P(),
        P("fsdp"),
        P("fsdp", "tp"),
        P("fsdp", "tp"),
        P("fsdp", "tp"),
        P("fsdp", "tp"),
        P("fsdp", "tp"),
        P("fsdp", "tp"),
        P(None, "tp", "fsdp"),
        P(None, "tp", "fsdp"),
        P(None, "tp", "fsdp"),
        P("tp"),
        P("tp"),
        P("fsdp"),
        P("tp", "fsdp"),
        P("fsdp"),
        P("fsdp", "tp"),
        P("fsdp", "tp"),
        P("tp", "fsdp"),
        P(("fsdp", "tp"), None),
    )
    return jax.shard_map(
        shards,
        mesh=mesh,
        in_specs=placed,
        out_specs=(
            P(("fsdp", "tp"), None),
            P(("fsdp", "tp"), None),
            P("fsdp"),
            P("fsdp", "tp"),
            P("fsdp", "tp"),
            P("fsdp", "tp"),
            P("fsdp", "tp"),
            P("fsdp", "tp"),
            P("fsdp", "tp"),
            P(None, "tp", "fsdp"),
            P(None, "tp", "fsdp"),
            P(None, "tp", "fsdp"),
            P("tp"),
            P("tp"),
            P("fsdp"),
            P("tp", "fsdp"),
            P("fsdp"),
            P("fsdp", "tp"),
            P("fsdp", "tp"),
            P("tp", "fsdp"),
        ),
        check_vma=False,
    )
```
